32 devices in a mesh: groups: 2 (over y), seq: 4 (over z), tensor: 4 (over x, core).
Axes of the slice: x: 2, y: 2, z: 4, core: 2. Of those that a mesh axis runs over, the one named last changes fastest.
Arguments:
- activations: bfloat16 [2048, 4096], P(('groups', 'seq')), parts along dimension 0, may hold values from -6 to 6
- token_adapter_index: int32 [2048], P(('groups', 'seq')), parts along dimension 0, may hold values from 0 to 15
- gate_scanned_weight: bfloat16 [4096, 2, 8192], P('seq', None, 'tensor'), may hold values from -0.09375 to 0.09375
- state_vector_weight: bfloat16 [4096, 2, 1024], P('seq'), may hold values from -0.09375 to 0.09375
- time_step_weight: bfloat16 [4096, 128], P('seq', 'tensor'), may hold values from -0.09375 to 0.09375
- adapter_down_maps: bfloat16 [4096, 256], P('seq'), may hold values from -0.09375 to 0.09375
- adapter_up_maps: bfloat16 [256, 2, 8192], P(None, None, 'tensor'), may hold values from -1.5 to 1.5
- scanned_channel_taps: float32 [4, 8192], P(None, 'tensor'), may hold values from -3 to 3
- state_vector_taps: float32 [4, 2, 1024], replicated, may hold values from -3 to 3
- earlier_scanned_channels: bfloat16 [6, 8192], P('groups', 'tensor'), parts along dimension 0, may hold values from -6 to 6
- earlier_state_vectors: bfloat16 [6, 2, 1024], P('groups'), parts along dimension 0, may hold values from -6 to 6
- head_step_bias: float32 [128], P('tensor'), may hold values from -4 to -1
- adapter_step_shift: float32 [16, 128], P(None, 'tensor'), may hold values from -3 to 3
- head_decay_rate: float32 [128], P('tensor'), may hold values from 0.0001953125 to 0.3
- starting_head_state: float32 [256, 64, 128], P(('groups', 'tensor')), parts along dimension 0, may hold values from -6 to 6
- gated_norm_gain: float32 [8192], P('tensor'), may hold values from 0.1 to 1.9
- output_projection_weight: bfloat16 [8192, 4096], P('tensor', 'seq'), may hold values from -0.0625 to 0.0625
Outputs:
- mixed: bfloat16 [2048, 4096], P(('groups', 'tensor'), 'seq'), parts along dimension 0
- checkpoints: float32 [8, 128, 64, 128], P(('groups', 'seq'), 'tensor'), parts along dimension 0
The draws below stay inside these ranges and needn't reach their ends.
There are 2 independent parts, one for each index of `groups`. The reference program is written for one: setup_inputs(seed, part) draws one part's arguments, and reference() takes and returns one part's arrays. A program takes and returns all parts, laid end to end along the dimension named above; an argument that names none is the same for every part. Nothing has to cross between parts.
All inputs are finite; a program needn't handle non-finite values.
Results may differ from the reference program's by a relative error of at most 0.02.
Values may be sent and summed in bfloat16 or wider, within the bound.
No kernel may reach another device: no remote copies, remote signals or barrier semaphores. Data moves between devices by JAX's collectives and lax.ppermute only.
A program may use at most 192 MiB of HBM per device.

```python
import math
import jax
import jax.numpy as jnp
import numpy as np
from jax import lax

MODEL_WIDTH = 4096
HEADS = 128
HEAD_DIM = 64
STATE = 128
HEAD_SETS = 8
ADAPTER_COUNT = 16
ADAPTER_RANK = 16
CONV = 4
BLOCK = 128
TOK_DEV = 256
TOKENS = 1024
INNER_CHANNELS = 8192


def place_ends(values, own_key, smallest, largest):
    longest = values.shape.index(max(values.shape))
    spots = []
    for shift in (0, 1):
        where = [jax.random.randint(jax.random.fold_in(own_key, axis), (), 0, length) for axis, length in enumerate(values.shape)]
        where[longest] = (where[longest] + shift) % values.shape[longest]
        spots.append(tuple(where))
    return values.at[spots[0]].set(smallest).at[spots[1]].set(largest)


def shard_levels(stream_key, extent, split, low, high):
    gain, own = 1.0, jax.random.fold_in(stream_key, 6)
    for dim, shards_of in split:
        heights = jnp.exp(jax.random.uniform(jax.random.fold_in(own, dim), (shards_of,), jnp.float32, low / len(split), high / len(split)))
        gain = gain * jnp.repeat(heights, extent[dim] // shards_of).reshape([-1 if axis == dim else 1 for axis in range(len(extent))])
    return gain


def rank_bounds(count, lean):
    weights = [(1 << 20) // math.isqrt(standing ** lean) + 1 for standing in range(1, count + 1)]
    deviation = 1 + sum(weights) // (1 << 30)
    return np.cumsum(np.array([max(1, weight // deviation) for weight in weights]))


def ranked(rng, dims, count, lean):
    listing = rank_bounds(count, lean)
    ticket = jax.random.randint(jax.random.fold_in(rng, 1), dims, 0, int(listing[count - 1]))
    grade = jnp.searchsorted(jnp.asarray(listing, jnp.int32), ticket, side="right")
    return jax.random.permutation(jax.random.fold_in(rng, 2), count)[grade].astype(jnp.int32)


def gaussian(key, shape, scale, bound, shards=(), held_as=jnp.bfloat16):
    values = jax.random.normal(key, shape, jnp.float32) * scale
    if len(shards) > 0:
        values = shard_levels(key, shape, shards, -0.22, 0.18) * values
    return jnp.clip(values, min=-bound, max=bound).astype(held_as)


def setup_inputs(seed: int = 0, part: int = 0) -> dict:
    key_list = jax.random.split(jax.random.key(seed), 18)
    own_keys = jax.random.split(jax.random.fold_in(key_list[17], part), 18)
    activations = gaussian(own_keys[0], (TOKENS, MODEL_WIDTH), 1.0, 6.0, ((0, 4),))
    token_adapter_index = place_ends(ranked(own_keys[1], (TOKENS,), ADAPTER_COUNT, 2), jax.random.fold_in(own_keys[1], 3), 0, ADAPTER_COUNT - 1).astype(jnp.int32)
    gate_scanned_weight = gaussian(key_list[2], (MODEL_WIDTH, 2, INNER_CHANNELS), MODEL_WIDTH ** -0.5, 0.09375, ((0, 4), (2, 4)))
    state_vector_weight = gaussian(key_list[3], (MODEL_WIDTH, 2, HEAD_SETS * STATE), MODEL_WIDTH ** -0.5, 0.09375, ((0, 4),))
    time_step_weight = gaussian(key_list[4], (MODEL_WIDTH, HEADS), MODEL_WIDTH ** -0.5, 0.09375, ((0, 4), (1, 4)))
    adapter_down_maps = gaussian(key_list[5], (MODEL_WIDTH, ADAPTER_COUNT * ADAPTER_RANK), MODEL_WIDTH ** -0.5, 0.09375, ((0, 4),))
    adapter_up_maps = gaussian(key_list[6], (ADAPTER_COUNT * ADAPTER_RANK, 2, INNER_CHANNELS), ADAPTER_RANK ** -0.5, 1.5, ((2, 4),))
    scanned_channel_taps = gaussian(key_list[7], (CONV, INNER_CHANNELS), 0.5, 3.0, ((1, 4),), jnp.float32)
    state_vector_taps = gaussian(key_list[8], (CONV, 2, HEAD_SETS * STATE), 0.5, 3.0, (), jnp.float32)
    earlier_scanned_channels = gaussian(own_keys[9], (CONV - 1, INNER_CHANNELS), 1.0, 6.0, ((1, 4),))
    earlier_state_vectors = gaussian(own_keys[10], (CONV - 1, 2, HEAD_SETS * STATE), 1.0, 6.0)
    head_step_bias = jnp.clip(-4.0 + 3.0 * jax.random.uniform(key_list[11], (HEADS,), jnp.float32) ** shard_levels(key_list[11], (HEADS,), ((0, 4),), -0.2, 0.2), -4.0, -1.0)
    adapter_step_shift = gaussian(key_list[12], (ADAPTER_COUNT, HEADS), 0.5, 3.0, ((1, 4),), jnp.float32)
    head_decay_rate = jnp.clip(jnp.exp(math.log(0.3) - 7.336937 * jax.random.uniform(key_list[13], (HEADS,), jnp.float32) ** shard_levels(key_list[13], (HEADS,), ((0, 4),), -0.2, 0.2)), 0.0001953125, 0.3)
    starting_head_state = gaussian(own_keys[14], (HEADS, HEAD_DIM, STATE), 1.0, 6.0, ((0, 4),), jnp.float32)
    gated_norm_gain = jnp.clip(1.0 + 0.18 * jax.random.normal(key_list[15], (INNER_CHANNELS,), jnp.float32), 0.1, 1.9)
    output_projection_weight = gaussian(key_list[16], (INNER_CHANNELS, MODEL_WIDTH), INNER_CHANNELS ** -0.5, 0.0625, ((0, 4), (1, 4)))
    return {"activations": activations, "token_adapter_index": token_adapter_index, "gate_scanned_weight": gate_scanned_weight, "state_vector_weight": state_vector_weight, "time_step_weight": time_step_weight, "adapter_down_maps": adapter_down_maps, "adapter_up_maps": adapter_up_maps, "scanned_channel_taps": scanned_channel_taps, "state_vector_taps": state_vector_taps, "earlier_scanned_channels": earlier_scanned_channels, "earlier_state_vectors": earlier_state_vectors, "head_step_bias": head_step_bias, "adapter_step_shift": adapter_step_shift, "head_decay_rate": head_decay_rate, "starting_head_state": starting_head_state, "gated_norm_gain": gated_norm_gain, "output_projection_weight": output_projection_weight}


def settle(value):
    return lax.optimization_barrier(value.astype(jnp.bfloat16))

def causal_conv(series, prior, kernel):
    count = series.shape[0]
    padded = jnp.concatenate([prior, series], axis=0).astype(jnp.float32)
    total = jnp.zeros(series.shape, jnp.float32)
    for offset in range(CONV):
        total = total + kernel[offset] * padded[offset:offset + count]
    return settle(jax.nn.silu(total))

def reference(activations, token_adapter_index, gate_scanned_weight, state_vector_weight, time_step_weight, adapter_down_maps, adapter_up_maps, scanned_channel_taps, state_vector_taps, earlier_scanned_channels, earlier_state_vectors, head_step_bias, adapter_step_shift, head_decay_rate, starting_head_state, gated_norm_gain, output_projection_weight):
    count = activations.shape[0]
    inner_channel_width = HEADS * HEAD_DIM
    state_width = 2 * HEAD_SETS * STATE
    per_set = HEADS // HEAD_SETS
    owner_adapter = jnp.arange(ADAPTER_COUNT * ADAPTER_RANK, dtype=jnp.int32) // ADAPTER_RANK
    adapter_hidden = jnp.dot(activations, adapter_down_maps, preferred_element_type=jnp.float32)
    adapter_hidden = settle(jnp.where(token_adapter_index[:, None] == owner_adapter[None, :], adapter_hidden, 0.0))
    gate_and_scanned = jnp.dot(activations, gate_scanned_weight.reshape(MODEL_WIDTH, 2 * inner_channel_width), preferred_element_type=jnp.float32)
    gate_and_scanned = gate_and_scanned + jnp.dot(adapter_hidden, adapter_up_maps.reshape(ADAPTER_COUNT * ADAPTER_RANK, 2 * inner_channel_width), preferred_element_type=jnp.float32)
    gate_and_scanned = settle(gate_and_scanned).reshape(count, 2, inner_channel_width)
    gate_values = gate_and_scanned[:, 0]
    mix_values = gate_and_scanned[:, 1]
    state_io = settle(jnp.dot(activations, state_vector_weight.reshape(MODEL_WIDTH, state_width), preferred_element_type=jnp.float32))
    step_raw = jnp.dot(activations, time_step_weight, preferred_element_type=jnp.float32)
    mix_conv = causal_conv(mix_values, earlier_scanned_channels, scanned_channel_taps)
    state_conv = causal_conv(state_io, earlier_state_vectors.reshape(CONV - 1, state_width), state_vector_taps.reshape(CONV, state_width))
    state_conv = state_conv.reshape(count, 2, HEAD_SETS, STATE)
    timestep = jax.nn.softplus(step_raw + head_step_bias + adapter_step_shift[token_adapter_index])
    log_decay = -head_decay_rate * timestep
    blocks = count // BLOCK
    mix_blocks = mix_conv.reshape(blocks, BLOCK, HEADS, HEAD_DIM)
    input_blocks = state_conv[:, 0].reshape(blocks, BLOCK, HEAD_SETS, STATE)
    output_blocks = state_conv[:, 1].reshape(blocks, BLOCK, HEAD_SETS, STATE)
    step_blocks = timestep.reshape(blocks, BLOCK, HEADS)
    decay_blocks = log_decay.reshape(blocks, BLOCK, HEADS)
    causal = jnp.tril(jnp.ones((BLOCK, BLOCK), dtype=bool))

    def one_block(state, inputs):
        mix_here, input_here, output_here, step_here, decay_here = inputs
        cumulative = jnp.cumsum(decay_here, axis=0)
        scores = jnp.einsum('ign,jgn->gij', output_here.astype(jnp.float32), input_here.astype(jnp.float32))
        scores = jnp.repeat(scores, per_set, axis=0)
        cum_heads = cumulative.T
        gaps = cum_heads[:, :, None] - cum_heads[:, None, :]
        weight = jnp.where(causal[None], jnp.exp(jnp.minimum(gaps, 0.0)), 0.0)
        mixing = settle(scores * weight * step_here.T[:, None, :])
        intra_out = jnp.einsum('hij,jhp->ihp', mixing.astype(jnp.float32), mix_here.astype(jnp.float32))
        input_heads = jnp.repeat(input_here, per_set, axis=1)
        output_heads = jnp.repeat(output_here, per_set, axis=1)
        inter_out = jnp.exp(cumulative)[:, :, None] * jnp.einsum('ihn,hpn->ihp', output_heads.astype(jnp.float32), state, precision=lax.Precision.HIGHEST)
        block_total = cumulative[-1]
        scaled = settle(mix_here.astype(jnp.float32) * (step_here * jnp.exp(block_total[None, :] - cumulative))[:, :, None])
        update = jnp.einsum('jhp,jhn->hpn', scaled.astype(jnp.float32), input_heads.astype(jnp.float32))
        new_state = jnp.exp(block_total)[:, None, None] * state + update
        return (new_state, (intra_out + inter_out, new_state))
    unused, outputs = lax.scan(one_block, starting_head_state, (mix_blocks, input_blocks, output_blocks, step_blocks, decay_blocks))
    scan_out = outputs[0].reshape(count, inner_channel_width)
    block_ends = outputs[1]
    gated = settle(scan_out * jax.nn.silu(gate_values.astype(jnp.float32)))
    squares = lax.optimization_barrier(jnp.sum(jnp.square(gated.astype(jnp.float32)), axis=1))
    hidden = settle(gated.astype(jnp.float32) * gated_norm_gain)
    partial_sum = jnp.dot(hidden, output_projection_weight, preferred_element_type=jnp.float32)
    mixed = (partial_sum * lax.rsqrt(squares / inner_channel_width + 1e-05)[:, None]).astype(jnp.bfloat16)
    per_device = TOK_DEV // BLOCK
    checkpoints = block_ends[per_device - 1::per_device]
    return (mixed, checkpoints)
```

```python
import functools
import jax
import jax.numpy as jnp
from jax import lax
from jax.experimental import pallas as pl
from jax.experimental.pallas import tpu as pltpu
from jax.sharding import PartitionSpec as P

HEADS = 128
HEAD_DIM = 64
STATE = 128
HEAD_SETS = 8
ADAPTER_COUNT = 16
ADAPTER_RANK = 16
CONV = 4
BLOCK = 128
LANES = 128


bf16 = jnp.bfloat16
f32 = jnp.float32


def silu(v):
    return v / (1.0 + jnp.exp(-v))


def scan_kernel(acc, tail, state, shift, rate, taps, gated, state_out, tail_out, rows):
    ch = gated.shape[1]
    wide = ch + 2 * STATE
    rows[0:8, :] = tail[...]
    rows[8 : 8 + BLOCK, :] = acc[:, ch : ch + wide].astype(f32)
    tail_out[...] = rows[BLOCK : BLOCK + 8, :]

    def conv(start, width):
        total = jnp.zeros((BLOCK, width), f32)
        for k in range(CONV):
            first = 8 - (CONV - 1) + k
            total = total + (
                taps[k : k + 1, start : start + width]
                * rows[first : first + BLOCK, start : start + width]
            )
        return silu(total).astype(bf16)

    input_vec = conv(ch, STATE)
    output_vec = conv(ch + STATE, STATE)
    raw = acc[:, ch + wide :].astype(f32) + shift[...]
    step = jnp.maximum(raw, 0.0) + jnp.log1p(jnp.exp(-jnp.abs(raw)))
    row = lax.broadcasted_iota(jnp.int32, (BLOCK, BLOCK), 0)
    col = lax.broadcasted_iota(jnp.int32, (BLOCK, BLOCK), 1)
    causal = row >= col
    cum = jnp.dot(
        causal.astype(f32),
        -rate[...] * step,
        precision=lax.Precision.HIGHEST,
        preferred_element_type=f32,
    )
    cum_t = cum.T
    step_t = step.T
    scores = lax.dot_general(
        output_vec, input_vec, (((1,), (1,)), ((), ())), preferred_element_type=f32
    )
    scores = jnp.where(causal, scores, 0.0)
    first_half = col < HEAD_DIM
    input_t = input_vec.T
    for pair in range(ch // LANES):
        lanes = slice(pair * LANES, (pair + 1) * LANES)
        x = conv(pair * LANES, LANES)
        held = state[:, lanes]
        high = held.astype(bf16)
        low = (held - high.astype(f32)).astype(bf16)
        inter = jnp.dot(output_vec, high, preferred_element_type=f32) + jnp.dot(
            output_vec, low, preferred_element_type=f32
        )
        cums, steps, outs = [], [], []
        for h in (2 * pair, 2 * pair + 1):
            cum_i = jnp.broadcast_to(cum[:, h : h + 1], (BLOCK, BLOCK))
            weight = jnp.exp(jnp.minimum(cum_i - cum_t[h : h + 1, :], 0.0))
            mixing = (scores * weight * step_t[h : h + 1, :]).astype(bf16)
            outs.append(jnp.dot(mixing, x, preferred_element_type=f32))
            cums.append(cum_i)
            steps.append(jnp.broadcast_to(step[:, h : h + 1], (BLOCK, BLOCK)))
        cum_i = jnp.where(first_half, cums[0], cums[1])
        total = cum_i[BLOCK - 1 :, :]
        out = jnp.where(first_half, outs[0], outs[1]) + jnp.exp(cum_i) * inter
        gated[:, lanes] = (out * silu(acc[:, lanes].astype(f32))).astype(bf16)
        factor = jnp.where(first_half, steps[0], steps[1]) * jnp.exp(total - cum_i)
        scaled = (x.astype(f32) * factor).astype(bf16)
        state_out[:, lanes] = jnp.exp(total) * held + jnp.dot(
            input_t, scaled, preferred_element_type=f32
        )


def scan_block(acc, tail, state, shift, rate, taps, ch):
    wide = ch + 2 * STATE
    return pl.pallas_call(
        scan_kernel,
        out_shape=(
            jax.ShapeDtypeStruct((BLOCK, ch), bf16),
            jax.ShapeDtypeStruct((STATE, ch), f32),
            jax.ShapeDtypeStruct((8, wide), f32),
        ),
        scratch_shapes=[pltpu.VMEM((BLOCK + 8, wide), f32)],
        cost_estimate=pl.CostEstimate(
            flops=8 * BLOCK * BLOCK * ch,
            bytes_accessed=8 * BLOCK * ch * 4,
            transcendentals=2 * BLOCK * BLOCK * ch // HEAD_DIM,
        ),
        name="scan_block",
    )(acc, tail, state, shift, rate, taps)


def per_device(
    activations,
    token_adapter_index,
    gate_scanned_weight,
    state_vector_weight,
    time_step_weight,
    adapter_down_maps,
    adapter_up_maps,
    scanned_channel_taps,
    state_vector_taps,
    earlier_scanned_channels,
    earlier_state_vectors,
    head_step_bias,
    adapter_step_shift,
    head_decay_rate,
    starting_head_state,
    gated_norm_gain,
    output_projection_weight,
):
    n = lax.axis_size("seq")
    here = lax.axis_index("seq")
    shards = lax.axis_size("tensor")
    shard = lax.axis_index("tensor")
    core = shard % 2
    rows = activations.shape[0]
    tokens = rows * n
    depth = gate_scanned_weight.shape[0]
    heads_here = time_step_weight.shape[1]
    heads = heads_here // 2
    ch = heads * HEAD_DIM
    per_set = HEADS // HEAD_SETS
    assert per_set % heads == 0 and n % 2 == 0 and shards % 2 == 0
    blocks = tokens // BLOCK
    rank = ADAPTER_COUNT * ADAPTER_RANK
    right = [(j, j + 1) for j in range(n - 1)]
    left = [(j + 1, j) for j in range(n - 1)]
    swap = [(j, j ^ 1) for j in range(shards)]
    at_first = here == 0
    at_last = here == n - 1

    half = depth // 2
    index_rows = 16 * -(-rows // (16 * half))
    index_pad = jnp.pad(
        token_adapter_index.astype(bf16), (0, index_rows * half - rows)
    ).reshape(index_rows, half)

    def piece(dest):
        part = lax.dynamic_slice(activations, (0, dest * depth + core * half), (rows, half))
        return jnp.concatenate([part, index_pad], axis=0)

    pieces = [piece(here)]
    for k in range(1, n):
        pairs = [(j, (j + k) % n) for j in range(n)]
        pieces.append(lax.ppermute(piece((here + k) % n), "seq", pairs))
    pieces = jnp.stack(pieces)
    ordered = [
        lax.dynamic_index_in_dim(pieces, (here - b) % n, 0, False) for b in range(n)
    ]
    index = jnp.concatenate([p[rows:].reshape(-1)[:rows] for p in ordered]).astype(jnp.int32)
    mine = jnp.concatenate([p[:rows] for p in ordered], axis=0)
    other = lax.ppermute(mine, "tensor", swap)
    low_half = jnp.where(core == 0, mine, other)
    high_half = jnp.where(core == 0, other, mine)
    inputs = jnp.concatenate([low_half, high_half], axis=1)

    owner = jnp.arange(rank, dtype=jnp.int32) // ADAPTER_RANK
    lowrank = jnp.dot(inputs, adapter_down_maps, preferred_element_type=f32)
    lowrank = jnp.where(index[:, None] == owner[None, :], lowrank, 0.0).astype(bf16)
    inputs = jnp.concatenate([inputs, lowrank], axis=1)

    def weights_of(end):
        cols = slice(end * ch, (end + 1) * ch)
        first = (shard * heads_here + end * heads) // per_set * STATE
        io = lax.dynamic_slice_in_dim(state_vector_weight, first, STATE, 2)
        steps = time_step_weight[:, end * heads : (end + 1) * heads]
        top = jnp.concatenate(
            [
                gate_scanned_weight[:, 0, cols],
                gate_scanned_weight[:, 1, cols],
                io[:, 0],
                io[:, 1],
                jnp.pad(steps, ((0, 0), (0, LANES - heads))),
            ],
            axis=1,
        )
        bottom = jnp.concatenate(
            [
                adapter_up_maps[:, 0, cols],
                adapter_up_maps[:, 1, cols],
                jnp.zeros((rank, 2 * STATE + LANES), bf16),
            ],
            axis=1,
        )
        return jnp.concatenate([top, bottom], axis=0)

    to_first, to_last = (
        jnp.dot(inputs, weights_of(end), preferred_element_type=f32).astype(bf16)
        for end in range(2)
    )

    end = jnp.where(at_first, 0, 1)
    first_head = end * heads
    first_ch = end * ch
    first_io = (shard * heads_here + first_head) // per_set * STATE

    def own(array, start, size, axis):
        return lax.dynamic_slice_in_dim(array, start, size, axis)

    taps = jnp.concatenate(
        [
            own(scanned_channel_taps, first_ch, ch, 1),
            own(state_vector_taps, first_io, STATE, 2).reshape(CONV, 2 * STATE),
        ],
        axis=1,
    )
    tail = jnp.concatenate(
        [
            own(earlier_scanned_channels, first_ch, ch, 1),
            own(earlier_state_vectors, first_io, STATE, 2).reshape(CONV - 1, 2 * STATE),
        ],
        axis=1,
    ).astype(f32)
    tail = jnp.pad(tail, ((8 - (CONV - 1), 0), (0, 0)))
    onehot = (index[:, None] == jnp.arange(ADAPTER_COUNT, dtype=jnp.int32)[None, :]).astype(f32)
    shift = head_step_bias + jnp.dot(
        onehot, adapter_step_shift, precision=lax.Precision.HIGHEST, preferred_element_type=f32
    )
    shift = jnp.pad(own(shift, first_head, heads, 1), ((0, 0), (0, LANES - heads)))
    rate = jnp.pad(own(head_decay_rate, first_head, heads, 0), (0, LANES - heads))[None]
    state = own(starting_head_state, first_head, heads, 0).reshape(ch, STATE).T

    def block_of(array, index):
        start = jnp.clip(index, 0, blocks - 1) * BLOCK
        return lax.dynamic_slice_in_dim(array, start, BLOCK, 0)

    sends = blocks + n - 2
    sum_right = sum_left = pass_right = pass_left = None
    gated_blocks, from_left, from_right, states = [], [], [], []
    for step in range(blocks + 2 * n - 3):
        if step <= sends:
            go_right = block_of(to_last, step - here)
            go_left = block_of(to_first, step - (n - 1 - here))
            if step > 0:
                go_right = (go_right.astype(f32) + sum_right.astype(f32)).astype(bf16)
                go_left = (go_left.astype(f32) + sum_left.astype(f32)).astype(bf16)
            if step < sends:
                sum_right = lax.ppermute(go_right, "seq", right)
                sum_left = lax.ppermute(go_left, "seq", left)
        if step < n - 1:
            continue
        block = step - (n - 1)
        if block < blocks:
            acc = jnp.where(at_first, go_left, go_right)
            gated, state, tail = scan_block(
                acc, tail, state, shift[block * BLOCK : (block + 1) * BLOCK], rate, taps, ch
            )
            gated_blocks.append(gated)
            if (block + 1) * BLOCK % rows == 0:
                states.append(state.astype(bf16))
            out_right = gated if block == 0 else jnp.where(at_first, gated, pass_right)
            out_left = gated if block == 0 else jnp.where(at_last, gated, pass_left)
        else:
            out_right, out_left = pass_right, pass_left
        pass_right = lax.ppermute(out_right, "seq", right)
        pass_left = lax.ppermute(out_left, "seq", left)
        from_left.append(pass_right)
        from_right.append(pass_left)

    gated = jnp.concatenate(gated_blocks, axis=0)
    stream = jnp.concatenate(from_left, axis=0)
    first_part = jnp.where(
        at_first,
        gated,
        own(stream, jnp.maximum(here - 1, 0) * BLOCK, tokens, 0),
    )
    stream = jnp.concatenate(from_right, axis=0)
    last_part = jnp.where(
        at_last,
        gated,
        own(stream, jnp.maximum(n - 2 - here, 0) * BLOCK, tokens, 0),
    )

    arrived = [jnp.where(at_first, states[0], states[n - 1])]
    for k in range(1, n):
        leaving = jnp.where(at_first, states[k], states[n - 1 - k])
        arrived.append(lax.ppermute(leaving, "seq", [(0, k), (n - 1, n - 1 - k)]))
    arrived = jnp.stack(arrived)
    finish = jnp.concatenate(
        [
            lax.dynamic_index_in_dim(arrived, which, 0, False).T.reshape(heads, HEAD_DIM, STATE)
            for which in (here, n - 1 - here)
        ],
        axis=0,
    ).astype(f32)

    channels = jnp.concatenate([first_part, last_part], axis=1).astype(f32)
    squares = jnp.sum(jnp.square(channels), axis=1)
    hidden = (channels * gated_norm_gain).astype(bf16)
    partial = jnp.dot(hidden, output_projection_weight, preferred_element_type=f32).astype(bf16)
    width = partial.shape[1]
    chips = shards // 2
    chip = shard // 2
    size = tokens // shards
    partial = partial.reshape(chips, 2, size, width)
    squares = squares.reshape(chips, 2, size)

    def over_tensor(array, kind):
        keep = lax.dynamic_index_in_dim(array, core, 1, False).astype(f32)
        give = lax.dynamic_index_in_dim(array, 1 - core, 1, False)
        both = (keep + lax.ppermute(give, "tensor", swap).astype(f32)).astype(kind)
        total = lax.dynamic_index_in_dim(both, chip, 0, False).astype(f32)
        for k in range(1, chips):
            pairs = [(j, (j + 2 * k) % shards) for j in range(shards)]
            give = lax.dynamic_index_in_dim(both, (chip + k) % chips, 0, False)
            total = total + lax.ppermute(give, "tensor", pairs).astype(f32)
        return total

    summed = over_tensor(partial, bf16)
    total_squares = over_tensor(squares, f32)
    mixed = (summed * lax.rsqrt(total_squares / (HEADS * HEAD_DIM) + 1e-05)[:, None]).astype(bf16)
    return (mixed, finish[None])


def solution(mesh):
    return jax.shard_map(
        per_device,
        mesh=mesh,
        in_specs=(
            P(("groups", "seq"), None),
            P(("groups", "seq")),
            P("seq", None, "tensor"),
            P("seq", None, None),
            P("seq", "tensor"),
            P("seq", None),
            P(None, None, "tensor"),
            P(None, "tensor"),
            P(),
            P("groups", "tensor"),
            P("groups", None, None),
            P("tensor"),
            P(None, "tensor"),
            P("tensor"),
            P(("groups", "tensor"), None, None),
            P("tensor"),
            P("tensor", "seq"),
        ),
        out_specs=(P(("groups", "tensor"), "seq"), P(("groups", "seq"), "tensor", None, None)),
        check_vma=False,
    )
```

```python
import functools
import jax
import jax.numpy as jnp
from jax import lax
from jax.experimental import pallas as pl
from jax.experimental.pallas import tpu as pltpu
from jax.sharding import PartitionSpec as P

HEADS = 128
HEAD_DIM = 64
STATE = 128
HEAD_SETS = 8
ADAPTER_COUNT = 16
ADAPTER_RANK = 16
CONV = 4
BLOCK = 128
LANES = 128


bf16 = jnp.bfloat16
f32 = jnp.float32


def silu(v):
    return v / (1.0 + jnp.exp(-v))


def project_kernel(
    where, mine, other, down, weight, up, small, mixed_out, gate_out, *, rows, tile
):
    half = mine.shape[2]
    core = where[0]
    low = pl.multiple_of(core * half, half)
    high = pl.multiple_of((1 - core) * half, half)
    near = mine[0, :rows, :]
    far = other[0, :rows, :]

    def both(of_low, of_high):
        return jnp.dot(near, of_low, preferred_element_type=f32) + jnp.dot(
            far, of_high, preferred_element_type=f32
        )

    rank = down.shape[1]
    lowrank = both(down[pl.ds(low, half), :], down[pl.ds(high, half), :])
    span = min(half, rows)
    owner = lax.broadcasted_iota(jnp.int32, (rank, span), 0) // ADAPTER_RANK
    masks = []
    for part in range(rows // span):
        index = mine[0, rows + part : rows + part + 1, :span].astype(f32).astype(jnp.int32)
        masks.append((owner == index).astype(f32).T)
    mask = masks[0] if len(masks) == 1 else jnp.concatenate(masks, axis=0)
    lowrank = jnp.where(mask > 0.5, lowrank, 0.0).astype(bf16)

    ch = gate_out.shape[2]
    per_end = ch // tile

    def columns(step, carry):
        end = step // per_end
        src = pl.ds(pl.multiple_of(step * tile, tile), tile)
        dst = pl.ds(pl.multiple_of((step - end * per_end) * tile, tile), tile)
        for pair, out in ((0, gate_out), (1, mixed_out)):
            total = both(
                weight[pair, pl.ds(low, half), src], weight[pair, pl.ds(high, half), src]
            )
            total = total + jnp.dot(lowrank, up[pair, :, src], preferred_element_type=f32)
            out[end, :, dst] = total.astype(bf16)
        return carry

    lax.fori_loop(0, 2 * per_end, columns, 0)
    for end in range(2):
        mixed_out[end, :, ch:] = both(
            small[end, pl.ds(low, half), :], small[end, pl.ds(high, half), :]
        ).astype(bf16)


def project(where, mine, other, down, weight, up, small, count, rows, ch):
    n, height, half = mine.shape
    whole = lambda a: pl.BlockSpec(a.shape, lambda b, w: (0,) * a.ndim, pipeline_mode=pl.Buffered(1))
    picked = pl.BlockSpec((1, height, half), lambda b, w: (w[1 + b], 0, 0))
    wide = ch + small.shape[2]
    flops = 2 * count * rows * (2 * half) * 2 * (ch + wide)
    return pl.pallas_call(
        functools.partial(project_kernel, rows=rows, tile=min(256, ch)),
        out_shape=(
            jax.ShapeDtypeStruct((2, count * rows, wide), bf16),
            jax.ShapeDtypeStruct((2, count * rows, ch), bf16),
        ),
        grid_spec=pltpu.PrefetchScalarGridSpec(
            num_scalar_prefetch=1,
            grid=(count,),
            in_specs=[picked, picked, whole(down), whole(weight), whole(up), whole(small)],
            out_specs=[
                pl.BlockSpec((2, rows, wide), lambda b, w: (0, b, 0)),
                pl.BlockSpec((2, rows, ch), lambda b, w: (0, b, 0)),
            ],
        ),
        cost_estimate=pl.CostEstimate(
            flops=flops, bytes_accessed=2 * weight.size + 2 * count * rows * 2 * (ch + wide), transcendentals=0
        ),
        name="project",
    )(where, mine, other, down, weight, up, small)


def scan_kernel(*refs, passing, more):
    (
        where, gate_right, gate_left, sum_right, sum_left, came_right, came_left,
        tail, state, index, table, rate, taps,
        go_right, go_left, state_out, tail_out, rows, gates,
    ) = refs
    ch = state.shape[1]
    wide = ch + 2 * STATE
    first = where[0] == 1
    last = where[1] == 1

    right = (gate_right[0].astype(f32) + came_right[:, :ch].astype(f32)).astype(bf16)
    left = (gate_left[0].astype(f32) + came_left[:, :ch].astype(f32)).astype(bf16)
    if more:
        go_right[:, :ch] = right
        go_left[:, :ch] = left
    gates[...] = jnp.where(first, left.astype(f32), right.astype(f32))
    here = ch if more else 0

    rows[0:8, :] = tail[...]
    rows[8 : 8 + BLOCK, :] = jnp.where(
        first, sum_left[:, :wide].astype(f32), sum_right[:, :wide].astype(f32)
    )
    tail_out[...] = rows[BLOCK : BLOCK + 8, :]

    def conv(start, width):
        total = jnp.zeros((BLOCK, width), f32)
        for k in range(CONV):
            begin = 8 - (CONV - 1) + k
            total = total + (
                taps[k : k + 1, start : start + width]
                * rows[begin : begin + BLOCK, start : start + width]
            )
        return silu(total).astype(bf16)

    input_vec = conv(ch, STATE)
    output_vec = conv(ch + STATE, STATE)
    row = lax.broadcasted_iota(jnp.int32, (BLOCK, BLOCK), 0)
    col = lax.broadcasted_iota(jnp.int32, (BLOCK, BLOCK), 1)
    causal = row >= col
    chosen = (row == index[...].astype(jnp.int32)).astype(f32).T
    shift = jnp.dot(
        chosen, table[...], precision=lax.Precision.HIGHEST, preferred_element_type=f32
    )
    raw = jnp.where(first, sum_left[:, wide:].astype(f32), sum_right[:, wide:].astype(f32)) + shift
    step = jnp.maximum(raw, 0.0) + jnp.log1p(jnp.exp(-jnp.abs(raw)))
    cum = jnp.dot(
        causal.astype(f32),
        -rate[...] * step,
        precision=lax.Precision.HIGHEST,
        preferred_element_type=f32,
    )
    cum_t = cum.T
    step_t = step.T
    scores = lax.dot_general(
        output_vec, input_vec, (((1,), (1,)), ((), ())), preferred_element_type=f32
    )
    scores = jnp.where(causal, scores, 0.0)
    first_half = col < HEAD_DIM
    input_t = input_vec.T
    for pair in range(ch // LANES):
        lanes = slice(pair * LANES, (pair + 1) * LANES)
        x = conv(pair * LANES, LANES)
        held = state[:, lanes]
        high = held.astype(bf16)
        low = (held - high.astype(f32)).astype(bf16)
        inter = jnp.dot(output_vec, high, preferred_element_type=f32) + jnp.dot(
            output_vec, low, preferred_element_type=f32
        )
        cums, steps, outs = [], [], []
        for h in (2 * pair, 2 * pair + 1):
            cum_i = jnp.broadcast_to(cum[:, h : h + 1], (BLOCK, BLOCK))
            weight = jnp.exp(jnp.minimum(cum_i - cum_t[h : h + 1, :], 0.0))
            mixing = (scores * weight * step_t[h : h + 1, :]).astype(bf16)
            outs.append(jnp.dot(mixing, x, preferred_element_type=f32))
            cums.append(cum_i)
            steps.append(jnp.broadcast_to(step[:, h : h + 1], (BLOCK, BLOCK)))
        cum_i = jnp.where(first_half, cums[0], cums[1])
        total = cum_i[BLOCK - 1 :, :]
        out = jnp.where(first_half, outs[0], outs[1]) + jnp.exp(cum_i) * inter
        gated = out * silu(gates[:, lanes])
        spot = slice(here + pair * LANES, here + (pair + 1) * LANES)
        from_left, from_right = gated, gated
        if passing:
            came = slice(ch + pair * LANES, ch + (pair + 1) * LANES)
            from_left = jnp.where(first, gated, came_right[:, came].astype(f32))
            from_right = jnp.where(last, gated, came_left[:, came].astype(f32))
        go_right[:, spot] = from_left.astype(bf16)
        go_left[:, spot] = from_right.astype(bf16)
        factor = jnp.where(first_half, steps[0], steps[1]) * jnp.exp(total - cum_i)
        scaled = (x.astype(f32) * factor).astype(bf16)
        state_out[:, lanes] = jnp.exp(total) * held + jnp.dot(
            input_t, scaled, preferred_element_type=f32
        )


def scan_block(where, gates, sums, came, tail, state, index, table, rate, taps, passing, more):
    ch = state.shape[1]
    wide = ch + 2 * STATE
    out = 2 * ch if more else ch
    whole = lambda a: pl.BlockSpec(a.shape, lambda b, w: (0,) * a.ndim)
    others = (*sums, *came, tail, state, index, table, rate, taps)
    return pl.pallas_call(
        functools.partial(scan_kernel, passing=passing, more=more),
        out_shape=(
            jax.ShapeDtypeStruct((BLOCK, out), bf16),
            jax.ShapeDtypeStruct((BLOCK, out), bf16),
            jax.ShapeDtypeStruct((STATE, ch), f32),
            jax.ShapeDtypeStruct((8, wide), f32),
        ),
        grid_spec=pltpu.PrefetchScalarGridSpec(
            num_scalar_prefetch=1,
            grid=(1,),
            in_specs=[
                pl.BlockSpec((1, BLOCK, ch), lambda b, w: (1, w[2], 0)),
                pl.BlockSpec((1, BLOCK, ch), lambda b, w: (0, w[3], 0)),
                *(whole(a) for a in others),
            ],
            out_specs=[
                pl.BlockSpec((BLOCK, out), lambda b, w: (0, 0)),
                pl.BlockSpec((BLOCK, out), lambda b, w: (0, 0)),
                pl.BlockSpec((STATE, ch), lambda b, w: (0, 0)),
                pl.BlockSpec((8, wide), lambda b, w: (0, 0)),
            ],
            scratch_shapes=[pltpu.VMEM((BLOCK + 8, wide), f32), pltpu.VMEM((BLOCK, ch), f32)],
        ),
        cost_estimate=pl.CostEstimate(
            flops=8 * BLOCK * BLOCK * ch,
            bytes_accessed=16 * BLOCK * ch,
            transcendentals=2 * BLOCK * BLOCK * ch // HEAD_DIM,
        ),
        name="scan_block",
    )(where, gates, gates, *others)


def output_kernel(where, *refs, n, count):
    blocks = refs[: 2 * n * count]
    gain, weight, out, held = refs[2 * n * count :]
    ch = held.shape[1] // 2
    width = weight.shape[1]
    here = where[0]
    for block in range(count):
        for side in range(2):
            place = here if side == 0 else n - 1 - here
            for k in range(n):
                source = blocks[(block * 2 + side) * n + k]

                @pl.when(place == k)
                def _():
                    held[block * BLOCK : (block + 1) * BLOCK, side * ch : (side + 1) * ch] = source[...]

    values = held[...].astype(f32)
    squares = jnp.sum(values * values, axis=1, keepdims=True)
    hidden = (values * gain[...]).astype(bf16)
    out[:, :width] = jnp.dot(hidden, weight[...], preferred_element_type=f32).astype(bf16)
    out[:, width:] = jnp.broadcast_to(squares, (count * BLOCK, LANES)).astype(bf16)


def output_block(where, blocks, n, gain, weight, ch):
    count = len(blocks) // (2 * n)
    width = weight.shape[1]
    spot = lambda a: pl.BlockSpec((BLOCK, ch), lambda b, w: (0, a.shape[1] // ch - 1))
    whole = lambda a: pl.BlockSpec(a.shape, lambda b, w: (0, 0))
    return pl.pallas_call(
        functools.partial(output_kernel, n=n, count=count),
        out_shape=jax.ShapeDtypeStruct((count * BLOCK, width + LANES), bf16),
        grid_spec=pltpu.PrefetchScalarGridSpec(
            num_scalar_prefetch=1,
            grid=(1,),
            in_specs=[*(spot(a) for a in blocks), whole(gain), whole(weight)],
            out_specs=pl.BlockSpec((count * BLOCK, width + LANES), lambda b, w: (0, 0)),
            scratch_shapes=[pltpu.VMEM((count * BLOCK, 2 * ch), bf16)],
        ),
        cost_estimate=pl.CostEstimate(
            flops=4 * count * BLOCK * ch * width, bytes_accessed=4 * ch * width + 2 * len(blocks) * BLOCK * ch, transcendentals=0
        ),
        name="output_block",
    )(where, *blocks, gain, weight)


def per_device(
    activations,
    token_adapter_index,
    gate_scanned_weight,
    state_vector_weight,
    time_step_weight,
    adapter_down_maps,
    adapter_up_maps,
    scanned_channel_taps,
    state_vector_taps,
    earlier_scanned_channels,
    earlier_state_vectors,
    head_step_bias,
    adapter_step_shift,
    head_decay_rate,
    starting_head_state,
    gated_norm_gain,
    output_projection_weight,
):
    n = lax.axis_size("seq")
    here = lax.axis_index("seq")
    shards = lax.axis_size("tensor")
    shard = lax.axis_index("tensor")
    core = shard % 2
    rows = activations.shape[0]
    tokens = rows * n
    depth = gate_scanned_weight.shape[0]
    heads_here = time_step_weight.shape[1]
    heads = heads_here // 2
    ch = heads * HEAD_DIM
    per_set = HEADS // HEAD_SETS
    size = tokens // shards
    assert per_set % heads == 0 and n % 2 == 0 and shards % 2 == 0 and size % BLOCK == 0
    blocks = tokens // BLOCK
    right = [(j, j + 1) for j in range(n - 1)]
    left = [(j + 1, j) for j in range(n - 1)]
    swap = [(j, j ^ 1) for j in range(shards)]
    at_first = here == 0
    at_last = here == n - 1
    as_int = lambda v: v.astype(jnp.int32)

    def own(array, start, count, axis):
        return lax.dynamic_slice_in_dim(array, start, count, axis)

    half = depth // 2
    index_rows = 16 * -(-rows // (16 * half))
    index_pad = jnp.pad(
        token_adapter_index.astype(bf16), (0, index_rows * half - rows)
    ).reshape(index_rows, half)

    def piece(dest):
        part = lax.dynamic_slice(activations, (0, dest * depth + core * half), (rows, half))
        return jnp.concatenate([part, index_pad], axis=0)

    pieces = [piece(here)]
    for k in range(1, n):
        pairs = [(j, (j + k) % n) for j in range(n)]
        pieces.append(lax.ppermute(piece((here + k) % n), "seq", pairs))
    mine = jnp.stack(pieces)
    other = lax.ppermute(mine, "tensor", swap)
    index = mine[:, rows:].reshape(n, -1)[:, :rows]
    index = jnp.concatenate(
        [lax.dynamic_index_in_dim(index, (here - b) % n, 0, False) for b in range(n)]
    ).astype(f32).reshape(blocks, 1, BLOCK)

    weight = jnp.swapaxes(gate_scanned_weight, 0, 1)
    up = jnp.swapaxes(adapter_up_maps, 0, 1)

    def small_of(end):
        first = (shard * heads_here + end * heads) // per_set * STATE
        io = own(state_vector_weight, first, STATE, 2).reshape(depth, 2 * STATE)
        steps = time_step_weight[:, end * heads : (end + 1) * heads]
        return jnp.concatenate([io, jnp.pad(steps, ((0, 0), (0, LANES - heads)))], axis=1)

    small = jnp.stack([small_of(0), small_of(1)])
    order = [as_int(core)] + [as_int((here - b) % n) for b in range(n)]
    order = jnp.stack(order)
    early = project(order, mine, other, adapter_down_maps, weight, up, small, 1, rows, ch)
    every = project(order, mine, other, adapter_down_maps, weight, up, small, n, rows, ch)

    end = jnp.where(at_first, 0, 1)
    first_head = end * heads
    first_ch = end * ch
    first_io = (shard * heads_here + first_head) // per_set * STATE
    taps = jnp.concatenate(
        [
            own(scanned_channel_taps, first_ch, ch, 1),
            own(state_vector_taps, first_io, STATE, 2).reshape(CONV, 2 * STATE),
        ],
        axis=1,
    )
    tail = jnp.concatenate(
        [
            own(earlier_scanned_channels, first_ch, ch, 1),
            own(earlier_state_vectors, first_io, STATE, 2).reshape(CONV - 1, 2 * STATE),
        ],
        axis=1,
    ).astype(f32)
    tail = jnp.pad(tail, ((8 - (CONV - 1), 0), (0, 0)))
    table = own(adapter_step_shift + head_step_bias, first_head, heads, 1)
    table = jnp.pad(table, ((0, LANES - ADAPTER_COUNT), (0, LANES - heads)))
    rate = jnp.pad(own(head_decay_rate, first_head, heads, 0), (0, LANES - heads))[None]
    state = own(starting_head_state, first_head, heads, 0).reshape(ch, STATE).T
    gain = gated_norm_gain[None]

    def turn(step, limit):
        return jnp.clip(step - here, 0, limit - 1), jnp.clip(step - (n - 1 - here), 0, limit - 1)

    def taken(array, step, limit):
        to_right, to_left = turn(step, limit)
        shape = (1, BLOCK, array.shape[2])
        return (
            lax.dynamic_slice(array, (1, to_right * BLOCK, 0), shape)[0],
            lax.dynamic_slice(array, (0, to_left * BLOCK, 0), shape)[0],
        )

    def added(a, b):
        return (a.astype(f32) + b.astype(f32)).astype(bf16)

    def onward(pair):
        return lax.ppermute(pair[0], "seq", right), lax.ppermute(pair[1], "seq", left)

    sends = blocks + n - 2
    early_blocks = rows // BLOCK
    sums = came = None
    went, arrived, states = {}, {}, []
    outs = []
    for step in range(blocks + 2 * n - 3):
        block = step - (n - 1)
        source, limit = (early, early_blocks) if step < early_blocks else (every, blocks)
        if step <= sends:
            go = taken(source[0], step, limit)
            if step > 0:
                go = tuple(map(added, go, sums))
            if step < sends:
                sums = onward(go)
        if step < n - 1:
            gates = taken(source[1], step, limit)
            if step > 0:
                gates = tuple(map(added, gates, came))
            came = onward(gates)
            continue
        if block < blocks:
            to_right, to_left = turn(step, blocks)
            where = jnp.stack(list(map(as_int, (at_first, at_last, to_right, to_left))))
            *onto, state, tail = scan_block(
                where, every[1], go, came, tail, state, index[block], table, rate, taps,
                block > 0, step < sends,
            )
            if (block + 1) * BLOCK % rows == 0:
                states.append(state.astype(bf16))
            went[block] = tuple(onto)
            came = onward(onto)
        else:
            came = onward(tuple(a[:, -ch:] for a in came))
        arrived[step] = came
        done = step - (2 * n - 3)
        per = size // BLOCK
        if done >= 0 and (done + 1) % per == 0:
            needed = []
            for b in range(done + 1 - per, done + 1):
                for side in range(2):
                    needed.append(went[b][side])
                    needed.extend(arrived[b + n - 2 + k][side] for k in range(1, n))
            outs.append(
                output_block(as_int(here)[None], needed, n, gain, output_projection_weight, ch)
            )

    landed = [jnp.where(at_first, states[0], states[n - 1])]
    for k in range(1, n):
        leaving = jnp.where(at_first, states[k], states[n - 1 - k])
        landed.append(lax.ppermute(leaving, "seq", [(0, k), (n - 1, n - 1 - k)]))
    landed = jnp.stack(landed)
    finish = jnp.concatenate(
        [
            lax.dynamic_index_in_dim(landed, which, 0, False).T.reshape(heads, HEAD_DIM, STATE)
            for which in (here, n - 1 - here)
        ],
        axis=0,
    ).astype(f32)

    chips = shards // 2
    chip = shard // 2
    halves = []
    for k in range(chips):
        keep = jnp.where(core == 0, outs[2 * k], outs[2 * k + 1])
        give = jnp.where(core == 0, outs[2 * k + 1], outs[2 * k])
        halves.append(added(keep, lax.ppermute(give, "tensor", swap)))
    halves = jnp.stack(halves)
    total = lax.dynamic_index_in_dim(halves, chip, 0, False).astype(f32)
    for k in range(1, chips):
        pairs = [(j, (j + 2 * k) % shards) for j in range(shards)]
        give = lax.dynamic_index_in_dim(halves, (chip + k) % chips, 0, False)
        total = total + lax.ppermute(give, "tensor", pairs).astype(f32)
    width = output_projection_weight.shape[1]
    scale = lax.rsqrt(total[:, width : width + 1] / (HEADS * HEAD_DIM) + 1e-05)
    mixed = (total[:, :width] * scale).astype(bf16)
    return (mixed, finish[None])


def solution(mesh):
    return jax.shard_map(
        per_device,
        mesh=mesh,
        in_specs=(
            P(("groups", "seq"), None),
            P(("groups", "seq")),
            P("seq", None, "tensor"),
            P("seq", None, None),
            P("seq", "tensor"),
            P("seq", None),
            P(None, None, "tensor"),
            P(None, "tensor"),
            P(),
            P("groups", "tensor"),
            P("groups", None, None),
            P("tensor"),
            P(None, "tensor"),
            P("tensor"),
            P(("groups", "tensor"), None, None),
            P("tensor"),
            P("tensor", "seq"),
        ),
        out_specs=(P(("groups", "tensor"), "seq"), P(("groups", "seq"), "tensor", None, None)),
        check_vma=False,
    )
```

```python
import functools
import jax
import jax.numpy as jnp
from jax import lax
from jax.experimental import pallas as pl
from jax.experimental.pallas import tpu as pltpu
from jax.sharding import PartitionSpec as P


HEADS = 128
HEAD_DIM = 64
STATE = 128
HEAD_SETS = 8
ADAPTER_COUNT = 16
ADAPTER_RANK = 16
CONV = 4
BLOCK = 128
LANES = 128


bf16 = jnp.bfloat16
f32 = jnp.float32


def silu(v):
    return v / (1.0 + jnp.exp(-v))


def project_kernel(
    where, mine, other, down, weight, up, small, mixed_out, gate_out, near, far, lowrank, *, rows
):
    half = near.shape[1]
    count = near.shape[0] // rows
    core = where[0]
    low = pl.multiple_of(core * half, half)
    high = pl.multiple_of((1 - core) * half, half)
    step = pl.program_id(0)
    ch = gate_out.shape[2]
    tile = weight.shape[2]
    per_end = ch // tile

    def both(of_low, of_high):
        return jnp.dot(near[...], of_low, preferred_element_type=f32) + jnp.dot(
            far[...], of_high, preferred_element_type=f32
        )

    @pl.when(step == 0)
    def _():
        rank = down.shape[1]
        span = min(half, rows)
        owner = lax.broadcasted_iota(jnp.int32, (rank, span), 0) // ADAPTER_RANK
        masks = []
        for b in range(count):
            near[b * rows : (b + 1) * rows, :] = mine[where[1 + b], :rows, :]
            far[b * rows : (b + 1) * rows, :] = other[where[1 + b], :rows, :]
            for part in range(rows // span):
                index = mine[where[1 + b], rows : rows + 16, :span].astype(f32)
                index = index[part : part + 1].astype(jnp.int32)
                masks.append((owner == index).astype(f32).T)
        mask = masks[0] if len(masks) == 1 else jnp.concatenate(masks, axis=0)
        full = both(down[pl.ds(low, half), :], down[pl.ds(high, half), :])
        lowrank[...] = jnp.where(mask > 0.5, full, 0.0).astype(bf16)
        for end in range(2):
            mixed_out[end, :, ch:] = both(
                small[end, pl.ds(low, half), :], small[end, pl.ds(high, half), :]
            ).astype(bf16)

    end = step // per_end
    dst = pl.ds(pl.multiple_of((step - end * per_end) * tile, tile), tile)
    for pair, out in ((0, gate_out), (1, mixed_out)):
        total = both(weight[pair, pl.ds(low, half), :], weight[pair, pl.ds(high, half), :])
        total = total + jnp.dot(lowrank[...], up[pair], preferred_element_type=f32)
        out[end, :, dst] = total.astype(bf16)


def project(where, mine, other, down, weight, up, small, count, rows, ch):
    half = mine.shape[2]
    tile = min(256, ch)
    whole = lambda a: pl.BlockSpec(a.shape, lambda b, w: (0,) * a.ndim)
    striped = lambda a: pl.BlockSpec((2, a.shape[1], tile), lambda b, w: (0, 0, b))
    wide = ch + small.shape[2]
    held = lambda c: pl.BlockSpec((2, count * rows, c), lambda b, w: (0, 0, 0))
    flops = 2 * count * rows * (2 * half) * 2 * (ch + wide)
    return pl.pallas_call(
        functools.partial(project_kernel, rows=rows),
        out_shape=(
            jax.ShapeDtypeStruct((2, count * rows, wide), bf16),
            jax.ShapeDtypeStruct((2, count * rows, ch), bf16),
        ),
        grid_spec=pltpu.PrefetchScalarGridSpec(
            num_scalar_prefetch=1,
            grid=(2 * ch // tile,),
            in_specs=[
                whole(mine), whole(other), whole(down), striped(weight), striped(up), whole(small)
            ],
            out_specs=[held(wide), held(ch)],
            scratch_shapes=[
                pltpu.VMEM((count * rows, half), bf16),
                pltpu.VMEM((count * rows, half), bf16),
                pltpu.VMEM((count * rows, down.shape[1]), bf16),
            ],
        ),
        cost_estimate=pl.CostEstimate(
            flops=flops,
            bytes_accessed=2 * weight.size + 4 * count * rows * (ch + wide),
            transcendentals=0,
        ),
        name="project",
    )(where, mine, other, down, weight, up, small)


def scan_kernel(*refs, passing, more):
    (
        where, gate_right, gate_left, sum_right, sum_left, came_right, came_left,
        tail, state, index, table, rate, taps,
        go_right, go_left, state_out, tail_out, rows, gates, cum_rows, step_rows,
    ) = refs
    ch = state.shape[1]
    wide = ch + 2 * STATE
    first = where[0] == 1
    last = where[1] == 1

    right = (gate_right[0].astype(f32) + came_right[:, :ch].astype(f32)).astype(bf16)
    left = (gate_left[0].astype(f32) + came_left[:, :ch].astype(f32)).astype(bf16)
    if more:
        go_right[:, :ch] = right
        go_left[:, :ch] = left
    gates[...] = jnp.where(first, left.astype(f32), right.astype(f32))
    here = ch if more else 0

    rows[0:8, :] = tail[...]
    rows[8 : 8 + BLOCK, :] = jnp.where(
        first, sum_left[:, :wide].astype(f32), sum_right[:, :wide].astype(f32)
    )
    tail_out[...] = rows[BLOCK : BLOCK + 8, :]

    def conv(at):
        total = jnp.zeros((BLOCK, LANES), f32)
        for k in range(CONV):
            begin = 8 - (CONV - 1) + k
            total = total + taps[k : k + 1, at] * rows[begin : begin + BLOCK, at]
        return silu(total).astype(bf16)

    input_vec = conv(pl.ds(ch, STATE))
    output_vec = conv(pl.ds(ch + STATE, STATE))
    row = lax.broadcasted_iota(jnp.int32, (BLOCK, BLOCK), 0)
    col = lax.broadcasted_iota(jnp.int32, (BLOCK, BLOCK), 1)
    causal = row >= col
    chosen = (row == index[...].astype(jnp.int32)).astype(f32).T
    shift = jnp.dot(
        chosen, table[...], precision=lax.Precision.HIGHEST, preferred_element_type=f32
    )
    raw = jnp.where(first, sum_left[:, wide:].astype(f32), sum_right[:, wide:].astype(f32)) + shift
    step = jnp.maximum(raw, 0.0) + jnp.log1p(jnp.exp(-jnp.abs(raw)))
    cum = jnp.dot(
        causal.astype(f32),
        -rate[...] * step,
        precision=lax.Precision.HIGHEST,
        preferred_element_type=f32,
    )
    cum_rows[...] = cum.T
    step_rows[...] = step.T
    scores = lax.dot_general(
        output_vec, input_vec, (((1,), (1,)), ((), ())), preferred_element_type=f32
    )
    scores = jnp.where(causal, scores, 0.0)
    first_half = col < HEAD_DIM
    input_t = input_vec.T

    def two_heads(pair, carry):
        lanes = pl.ds(pl.multiple_of(pair * LANES, LANES), LANES)
        x = conv(lanes)
        held = state[:, lanes]
        high = held.astype(bf16)
        low = (held - high.astype(f32)).astype(bf16)
        inter = jnp.dot(output_vec, high, preferred_element_type=f32) + jnp.dot(
            output_vec, low, preferred_element_type=f32
        )
        turned = LANES - 2 * pair
        cum_here = pltpu.roll(cum, turned, 1)
        step_here = pltpu.roll(step, turned, 1)
        cums, steps, outs = [], [], []
        for h in range(2):
            row_of = pl.ds(2 * pair + h, 1)
            cum_i = jnp.broadcast_to(cum_here[:, h : h + 1], (BLOCK, BLOCK))
            weight = jnp.exp(jnp.minimum(cum_i - cum_rows[row_of, :], 0.0))
            mixing = (scores * weight * step_rows[row_of, :]).astype(bf16)
            outs.append(jnp.dot(mixing, x, preferred_element_type=f32))
            cums.append(cum_i)
            steps.append(jnp.broadcast_to(step_here[:, h : h + 1], (BLOCK, BLOCK)))
        cum_i = jnp.where(first_half, cums[0], cums[1])
        total = cum_i[BLOCK - 1 :, :]
        out = jnp.where(first_half, outs[0], outs[1]) + jnp.exp(cum_i) * inter
        gated = out * silu(gates[:, lanes])
        spot = pl.ds(pl.multiple_of(here + pair * LANES, LANES), LANES)
        from_left, from_right = gated, gated
        if passing:
            beside = pl.ds(pl.multiple_of(ch + pair * LANES, LANES), LANES)
            from_left = jnp.where(first, gated, came_right[:, beside].astype(f32))
            from_right = jnp.where(last, gated, came_left[:, beside].astype(f32))
        go_right[:, spot] = from_left.astype(bf16)
        go_left[:, spot] = from_right.astype(bf16)
        factor = jnp.where(first_half, steps[0], steps[1]) * jnp.exp(total - cum_i)
        scaled = (x.astype(f32) * factor).astype(bf16)
        state_out[:, lanes] = jnp.exp(total) * held + jnp.dot(
            input_t, scaled, preferred_element_type=f32
        )
        return carry

    lax.fori_loop(0, ch // LANES, two_heads, 0, unroll=2)


def scan_block(where, gates, sums, came, tail, state, index, table, rate, taps, passing, more):
    ch = state.shape[1]
    wide = ch + 2 * STATE
    out = 2 * ch if more else ch
    whole = lambda a: pl.BlockSpec(a.shape, lambda b, w: (0,) * a.ndim)
    others = (*sums, *came, tail, state, index, table, rate, taps)
    return pl.pallas_call(
        functools.partial(scan_kernel, passing=passing, more=more),
        out_shape=(
            jax.ShapeDtypeStruct((BLOCK, out), bf16),
            jax.ShapeDtypeStruct((BLOCK, out), bf16),
            jax.ShapeDtypeStruct((STATE, ch), f32),
            jax.ShapeDtypeStruct((8, wide), f32),
        ),
        grid_spec=pltpu.PrefetchScalarGridSpec(
            num_scalar_prefetch=1,
            grid=(1,),
            in_specs=[
                pl.BlockSpec((1, BLOCK, ch), lambda b, w: (1, w[2], 0)),
                pl.BlockSpec((1, BLOCK, ch), lambda b, w: (0, w[3], 0)),
                *(whole(a) for a in others),
            ],
            out_specs=[
                pl.BlockSpec((BLOCK, out), lambda b, w: (0, 0)),
                pl.BlockSpec((BLOCK, out), lambda b, w: (0, 0)),
                pl.BlockSpec((STATE, ch), lambda b, w: (0, 0)),
                pl.BlockSpec((8, wide), lambda b, w: (0, 0)),
            ],
            scratch_shapes=[
                pltpu.VMEM((BLOCK + 8, wide), f32),
                pltpu.VMEM((BLOCK, ch), f32),
                pltpu.VMEM((LANES, BLOCK), f32),
                pltpu.VMEM((LANES, BLOCK), f32),
            ],
        ),
        cost_estimate=pl.CostEstimate(
            flops=8 * BLOCK * BLOCK * ch,
            bytes_accessed=16 * BLOCK * ch,
            transcendentals=2 * BLOCK * BLOCK * ch // HEAD_DIM,
        ),
        name="scan_block",
    )(where, gates, gates, *others)


def output_kernel(where, *refs, n, count):
    blocks = refs[: 2 * n * count]
    gain, weight, out, held, sems = refs[2 * n * count :]
    ch = held.shape[1] // 2
    width = weight.shape[1]
    here = where[0]

    def fetch(act):
        for block in range(count):
            for side in range(2):
                place = here if side == 0 else n - 1 - here
                for k in range(n):
                    source = blocks[(block * 2 + side) * n + k]
                    start = source.shape[1] - ch

                    @pl.when(place == k)
                    def _():
                        act(
                            pltpu.make_async_copy(
                                source.at[:, start:],
                                held.at[pl.ds(block * BLOCK, BLOCK), pl.ds(side * ch, ch)],
                                sems.at[block, side],
                            )
                        )

    fetch(lambda copy: copy.start())
    fetch(lambda copy: copy.wait())
    values = held[...].astype(f32)
    squares = jnp.sum(values * values, axis=1, keepdims=True)
    hidden = (values * gain[...]).astype(bf16)
    out[:, :width] = jnp.dot(hidden, weight[...], preferred_element_type=f32).astype(bf16)
    out[:, width:] = jnp.broadcast_to(squares, (count * BLOCK, LANES)).astype(bf16)


def output_block(where, blocks, n, gain, weight, ch):
    count = len(blocks) // (2 * n)
    width = weight.shape[1]
    whole = lambda a: pl.BlockSpec(a.shape, lambda b, w: (0, 0))
    return pl.pallas_call(
        functools.partial(output_kernel, n=n, count=count),
        out_shape=jax.ShapeDtypeStruct((count * BLOCK, width + LANES), bf16),
        grid_spec=pltpu.PrefetchScalarGridSpec(
            num_scalar_prefetch=1,
            grid=(1,),
            in_specs=[*(pl.BlockSpec(memory_space=pl.ANY) for _ in blocks), whole(gain), whole(weight)],
            out_specs=pl.BlockSpec((count * BLOCK, width + LANES), lambda b, w: (0, 0)),
            scratch_shapes=[
                pltpu.VMEM((count * BLOCK, 2 * ch), bf16),
                pltpu.SemaphoreType.DMA((count, 2)),
            ],
        ),
        cost_estimate=pl.CostEstimate(
            flops=4 * count * BLOCK * ch * width, bytes_accessed=4 * ch * width + 8 * count * BLOCK * ch, transcendentals=0
        ),
        name="output_block",
    )(where, *blocks, gain, weight)


def per_device(
    activations,
    token_adapter_index,
    gate_scanned_weight,
    state_vector_weight,
    time_step_weight,
    adapter_down_maps,
    adapter_up_maps,
    scanned_channel_taps,
    state_vector_taps,
    earlier_scanned_channels,
    earlier_state_vectors,
    head_step_bias,
    adapter_step_shift,
    head_decay_rate,
    starting_head_state,
    gated_norm_gain,
    output_projection_weight,
):
    n = lax.axis_size("seq")
    here = lax.axis_index("seq")
    shards = lax.axis_size("tensor")
    shard = lax.axis_index("tensor")
    core = shard % 2
    rows = activations.shape[0]
    tokens = rows * n
    depth = gate_scanned_weight.shape[0]
    heads_here = time_step_weight.shape[1]
    heads = heads_here // 2
    ch = heads * HEAD_DIM
    per_set = HEADS // HEAD_SETS
    size = tokens // shards
    assert per_set % heads == 0 and n % 2 == 0 and shards % 2 == 0 and size % BLOCK == 0
    blocks = tokens // BLOCK
    right = [(j, j + 1) for j in range(n - 1)]
    left = [(j + 1, j) for j in range(n - 1)]
    swap = [(j, j ^ 1) for j in range(shards)]
    at_first = here == 0
    at_last = here == n - 1
    as_int = lambda v: v.astype(jnp.int32)

    def own(array, start, count, axis):
        return lax.dynamic_slice_in_dim(array, start, count, axis)

    half = depth // 2
    index_rows = 16 * -(-rows // (16 * half))
    index_pad = jnp.pad(
        token_adapter_index.astype(bf16), (0, index_rows * half - rows)
    ).reshape(index_rows, half)

    def piece(dest):
        part = lax.dynamic_slice(activations, (0, dest * depth + core * half), (rows, half))
        return jnp.concatenate([part, index_pad], axis=0)

    pieces = [piece(here)]
    for k in range(1, n):
        pairs = [(j, (j + k) % n) for j in range(n)]
        pieces.append(lax.ppermute(piece((here + k) % n), "seq", pairs))
    weight = jnp.swapaxes(gate_scanned_weight, 0, 1)
    up = jnp.swapaxes(adapter_up_maps, 0, 1)

    def small_of(end):
        first = (shard * heads_here + end * heads) // per_set * STATE
        io = own(state_vector_weight, first, STATE, 2).reshape(depth, 2 * STATE)
        steps = time_step_weight[:, end * heads : (end + 1) * heads]
        return jnp.concatenate([io, jnp.pad(steps, ((0, 0), (0, LANES - heads)))], axis=1)

    small = jnp.stack([small_of(0), small_of(1)])
    mine, weight, up, small = lax.optimization_barrier((jnp.stack(pieces), weight, up, small))
    other = lax.ppermute(mine, "tensor", swap)
    index = mine[:, rows:].reshape(n, -1)[:, :rows]
    index = jnp.concatenate(
        [lax.dynamic_index_in_dim(index, (here - b) % n, 0, False) for b in range(n)]
    ).astype(f32).reshape(blocks, 1, BLOCK)

    order = [as_int(core)] + [as_int((here - b) % n) for b in range(n)]
    order = jnp.stack(order)
    early = project(order, mine, other, adapter_down_maps, weight, up, small, 1, rows, ch)
    every = project(order, mine, other, adapter_down_maps, weight, up, small, n, rows, ch)

    end = jnp.where(at_first, 0, 1)
    first_head = end * heads
    first_ch = end * ch
    first_io = (shard * heads_here + first_head) // per_set * STATE
    taps = jnp.concatenate(
        [
            own(scanned_channel_taps, first_ch, ch, 1),
            own(state_vector_taps, first_io, STATE, 2).reshape(CONV, 2 * STATE),
        ],
        axis=1,
    )
    tail = jnp.concatenate(
        [
            own(earlier_scanned_channels, first_ch, ch, 1),
            own(earlier_state_vectors, first_io, STATE, 2).reshape(CONV - 1, 2 * STATE),
        ],
        axis=1,
    ).astype(f32)
    tail = jnp.pad(tail, ((8 - (CONV - 1), 0), (0, 0)))
    table = own(adapter_step_shift + head_step_bias, first_head, heads, 1)
    table = jnp.pad(table, ((0, LANES - ADAPTER_COUNT), (0, LANES - heads)))
    rate = jnp.pad(own(head_decay_rate, first_head, heads, 0), (0, LANES - heads))[None]
    state = own(starting_head_state, first_head, heads, 0).reshape(ch, STATE).T
    gain = gated_norm_gain[None]

    def turn(step, limit):
        return jnp.clip(step - here, 0, limit - 1), jnp.clip(step - (n - 1 - here), 0, limit - 1)

    def taken(array, step, limit):
        to_right, to_left = turn(step, limit)
        shape = (1, BLOCK, array.shape[2])
        return (
            lax.dynamic_slice(array, (1, to_right * BLOCK, 0), shape)[0],
            lax.dynamic_slice(array, (0, to_left * BLOCK, 0), shape)[0],
        )

    def added(a, b):
        return (a.astype(f32) + b.astype(f32)).astype(bf16)

    def onward(pair):
        ahead = lax.ppermute(pair[0], "seq", right)
        back = lax.ppermute(pair[1], "seq", left)
        return ahead, back

    sends = blocks + n - 2
    early_blocks = rows // BLOCK

    def tied(*pairs):
        flat = lax.optimization_barrier(tuple(a for pair in pairs for a in pair))
        return [tuple(flat[k : k + 2]) for k in range(0, len(flat), 2)]

    sums = came = before = None
    went, arrived, states = {}, {}, []
    outs = []
    pending = None
    for step in range(blocks + 2 * n - 3):
        block = step - (n - 1)
        source, limit = (early, early_blocks) if step < early_blocks else (every, blocks)
        if step <= sends:
            go = taken(source[0], step, limit)
            if step > 1:
                sums, before = tied(sums, before)
            if step > 0:
                go = tuple(map(added, go, sums))
                came, sums = tied(came, sums)
            before = came
            if step < sends:
                sums = onward(go)
        if step < n - 1:
            gates = taken(source[1], step, limit)
            if step > 0:
                gates = tuple(map(added, gates, came))
            came = onward(gates)
            continue
        if block < blocks:
            to_right, to_left = turn(step, blocks)
            where = jnp.stack(list(map(as_int, (at_first, at_last, to_right, to_left))))
            *onto, state, tail = scan_block(
                where, every[1], go, came, tail, state, index[block], table, rate, taps,
                block > 0, step < sends,
            )
            if (block + 1) * BLOCK % rows == 0:
                states.append(state.astype(bf16))
            went[block] = tuple(onto)
            came = onward(onto)
        else:
            (came,) = tied(came)
            came = onward(tuple(a[:, -ch:] for a in came))
        arrived[step] = came
        done = step - (2 * n - 3)
        per = size // BLOCK
        if done >= 0 and (done + 1) % per == 0:
            needed = []
            for b in range(done + 1 - per, done + 1):
                for side in range(2):
                    needed.append(went[b][side])
                    needed.extend(arrived[b + n - 2 + k][side] for k in range(1, n))
            outs.append(
                output_block(as_int(here)[None], needed, n, gain, output_projection_weight, ch)
            )
            pending = len(outs) - 1
        elif pending is not None and block + 1 < blocks:
            state, outs[pending] = lax.optimization_barrier((state, outs[pending]))
            pending = None

    landed = [jnp.where(at_first, states[0], states[n - 1])]
    for k in range(1, n):
        leaving = jnp.where(at_first, states[k], states[n - 1 - k])
        landed.append(lax.ppermute(leaving, "seq", [(0, k), (n - 1, n - 1 - k)]))
    landed = jnp.stack(landed)
    finish = jnp.concatenate(
        [
            lax.dynamic_index_in_dim(landed, which, 0, False).T.reshape(heads, HEAD_DIM, STATE)
            for which in (here, n - 1 - here)
        ],
        axis=0,
    ).astype(f32)

    chips = shards // 2
    chip = shard // 2
    if chips == 2:
        total = None
        for t in range(shards):
            give = [(j, j ^ 1) for j in range(shards) if j % 2 != t % 2]
            both = added(outs[t], lax.ppermute(outs[t], "tensor", give))
            came = lax.ppermute(both, "tensor", [(t ^ 2, t)])
            both = both.astype(f32) + came.astype(f32)
            total = both if total is None else jnp.where(shard == t, both, total)
    else:
        halves = []
        for k in range(chips):
            keep = jnp.where(core == 0, outs[2 * k], outs[2 * k + 1])
            give = jnp.where(core == 0, outs[2 * k + 1], outs[2 * k])
            halves.append(added(keep, lax.ppermute(give, "tensor", swap)))
        halves = jnp.stack(halves)
        total = lax.dynamic_index_in_dim(halves, chip, 0, False).astype(f32)
        for k in range(1, chips):
            pairs = [(j, (j + 2 * k) % shards) for j in range(shards)]
            give = lax.dynamic_index_in_dim(halves, (chip + k) % chips, 0, False)
            total = total + lax.ppermute(give, "tensor", pairs).astype(f32)
    width = output_projection_weight.shape[1]
    scale = lax.rsqrt(total[:, width : width + 1] / (HEADS * HEAD_DIM) + 1e-05)
    mixed = (total[:, :width] * scale).astype(bf16)
    return (mixed, finish[None])


def solution(mesh):
    return jax.shard_map(
        per_device,
        mesh=mesh,
        in_specs=(
            P(("groups", "seq"), None),
            P(("groups", "seq")),
            P("seq", None, "tensor"),
            P("seq", None, None),
            P("seq", "tensor"),
            P("seq", None),
            P(None, None, "tensor"),
            P(None, "tensor"),
            P(),
            P("groups", "tensor"),
            P("groups", None, None),
            P("tensor"),
            P(None, "tensor"),
            P("tensor"),
            P(("groups", "tensor"), None, None),
            P("tensor"),
            P("tensor", "seq"),
        ),
        out_specs=(P(("groups", "tensor"), "seq"), P(("groups", "seq"), "tensor", None, None)),
        check_vma=False,
    )
```

```python
import functools
import jax
import jax.numpy as jnp
from jax import lax
from jax.experimental import pallas as pl
from jax.experimental.pallas import tpu as pltpu
from jax.sharding import PartitionSpec as P


HEADS = 128
HEAD_DIM = 64
STATE = 128
HEAD_SETS = 8
ADAPTER_COUNT = 16
ADAPTER_RANK = 16
CONV = 4
BLOCK = 128
LANES = 128


bf16 = jnp.bfloat16
f32 = jnp.float32


def silu(v):
    return v / (1.0 + jnp.exp(-v))


def project_kernel(where, mine, other, down, weight, up, small, mixed_out, gate_out, values, held, *, rows):
    half = mine.shape[2]
    count = mine.shape[0]
    depth = 2 * half
    core = where[0]
    step = pl.program_id(0)
    ch = gate_out.shape[2]
    tile = held.shape[1]
    per_end = ch // tile

    def plane(end):
        return jnp.where(where[1] == 1, 1 - end, end)

    @pl.when(step == 0)
    def _():
        rank = down.shape[1]
        span = min(half, rows)
        owner = lax.broadcasted_iota(jnp.int32, (rank, span), 0) // ADAPTER_RANK
        near = pl.ds(pl.multiple_of(core * half, half), half)
        far = pl.ds(pl.multiple_of((1 - core) * half, half), half)
        masks = []
        for b in range(count):
            values[b * rows : (b + 1) * rows, near] = mine[where[2 + b], :rows, :]
            values[b * rows : (b + 1) * rows, far] = other[where[2 + b], :rows, :]
            for part in range(rows // span):
                index = mine[where[2 + b], rows : rows + 16, :span].astype(f32)
                index = index[part : part + 1].astype(jnp.int32)
                masks.append((owner == index).astype(f32).T)
        mask = masks[0] if len(masks) == 1 else jnp.concatenate(masks, axis=0)
        full = jnp.dot(values[:, :depth], down[...], preferred_element_type=f32)
        values[:, depth:] = jnp.where(mask > 0.5, full, 0.0).astype(bf16)
        for end in range(2):
            mixed_out[plane(end), :, ch:] = jnp.dot(
                values[:, :depth], small[end], preferred_element_type=f32
            ).astype(bf16)

    end = step // per_end
    dst = pl.ds(pl.multiple_of((step - end * per_end) * tile, tile), tile)
    for pair, out in ((0, gate_out), (1, mixed_out)):
        held[:depth, :] = weight[:, pair].reshape(depth, tile)
        held[depth:, :] = up[:, pair].reshape(held.shape[0] - depth, tile)
        chunk = min(512, values.shape[0])

        def some_rows(at, carry):
            part = pl.ds(pl.multiple_of(at * chunk, chunk), chunk)
            out[plane(end), part, dst] = jnp.dot(
                values[part, :], held[...], preferred_element_type=f32
            ).astype(bf16)
            return carry

        lax.fori_loop(0, values.shape[0] // chunk, some_rows, 0)


def project(where, mine, other, down, weight, up, small, rows, ch):
    n, _, half = mine.shape
    tile = min(256, ch)
    whole = lambda a: pl.BlockSpec(a.shape, lambda b, w: (0,) * a.ndim)
    striped = lambda a: pl.BlockSpec((*a.shape[:3], tile), lambda b, w: (0, 0, 0, b))
    wide = ch + small.shape[2]
    held = lambda c: pl.BlockSpec((2, n * rows, c), lambda b, w: (0, 0, 0))
    full = 2 * half + down.shape[1]
    return pl.pallas_call(
        functools.partial(project_kernel, rows=rows),
        out_shape=(
            jax.ShapeDtypeStruct((2, n * rows, wide), bf16),
            jax.ShapeDtypeStruct((2, n * rows, ch), bf16),
        ),
        grid_spec=pltpu.PrefetchScalarGridSpec(
            num_scalar_prefetch=1,
            grid=(2 * ch // tile,),
            in_specs=[
                whole(mine), whole(other), whole(down), striped(weight), striped(up), whole(small)
            ],
            out_specs=[held(wide), held(ch)],
            scratch_shapes=[pltpu.VMEM((n * rows, full), bf16), pltpu.VMEM((full, tile), bf16)],
        ),
        cost_estimate=pl.CostEstimate(
            flops=4 * n * rows * full * (ch + wide),
            bytes_accessed=2 * weight.size + 4 * n * rows * (ch + wide),
            transcendentals=0,
        ),
        name="project",
    )(where, mine, other, down, weight, up, small)


def merge_kernel(where, gate_a, gate_b, came_a, came_b, gated, go_a, go_b, *, passing):
    ch = gated.shape[1]
    go_a[:, :ch] = (gate_a[0].astype(f32) + came_b[:, :ch].astype(f32)).astype(bf16)
    go_b[:, :ch] = (gate_b[0].astype(f32) + came_a[:, :ch].astype(f32)).astype(bf16)
    own = gated[...]
    if passing:
        own = jnp.where(where[0] == 1, own.astype(f32), came_b[:, ch:].astype(f32)).astype(bf16)
        go_b[:, ch:] = came_a[:, ch:]
    else:
        go_b[:, ch:] = own
    go_a[:, ch:] = own


def merge(where, gates, came, gated):
    ch = gated.shape[1]
    passing = came[0].shape[1] > ch
    whole = lambda a: pl.BlockSpec(a.shape, lambda b, w: (0,) * a.ndim)
    out = jax.ShapeDtypeStruct((BLOCK, 2 * ch), bf16)
    return pl.pallas_call(
        functools.partial(merge_kernel, passing=passing),
        out_shape=(out, out),
        grid_spec=pltpu.PrefetchScalarGridSpec(
            num_scalar_prefetch=1,
            grid=(1,),
            in_specs=[
                pl.BlockSpec((1, BLOCK, ch), lambda b, w: (0, w[1], 0)),
                pl.BlockSpec((1, BLOCK, ch), lambda b, w: (1, w[2], 0)),
                whole(came[0]), whole(came[1]), whole(gated),
            ],
            out_specs=[whole(out), whole(out)],
        ),
        cost_estimate=pl.CostEstimate(
            flops=4 * BLOCK * ch, bytes_accessed=22 * BLOCK * ch, transcendentals=0
        ),
        name="merge",
    )(where, gates, gates, *came, gated)


def scan_kernel(
    gates, sums, tail, state, index, table, rate, taps,
    gated_out, state_out, tail_out, rows, cum_rows, step_rows,
):
    ch = state.shape[1]
    wide = ch + 2 * STATE
    rows[0:8, :] = tail[...]
    rows[8 : 8 + BLOCK, :] = sums[:, :wide].astype(f32)
    tail_out[...] = rows[BLOCK : BLOCK + 8, :]

    def conv(at):
        total = jnp.zeros((BLOCK, LANES), f32)
        for k in range(CONV):
            begin = 8 - (CONV - 1) + k
            total = total + taps[k : k + 1, at] * rows[begin : begin + BLOCK, at]
        return silu(total).astype(bf16)

    input_vec = conv(pl.ds(ch, STATE))
    output_vec = conv(pl.ds(ch + STATE, STATE))
    row = lax.broadcasted_iota(jnp.int32, (BLOCK, BLOCK), 0)
    col = lax.broadcasted_iota(jnp.int32, (BLOCK, BLOCK), 1)
    causal = row >= col
    chosen = (row == index[...].astype(jnp.int32)).astype(f32).T
    shift = jnp.dot(
        chosen, table[...], precision=lax.Precision.HIGHEST, preferred_element_type=f32
    )
    raw = sums[:, wide:].astype(f32) + shift
    step = jnp.maximum(raw, 0.0) + jnp.log1p(jnp.exp(-jnp.abs(raw)))
    cum = jnp.dot(
        causal.astype(f32),
        -rate[...] * step,
        precision=lax.Precision.HIGHEST,
        preferred_element_type=f32,
    )
    cum_rows[...] = cum.T
    step_rows[...] = step.T
    scores = lax.dot_general(
        output_vec, input_vec, (((1,), (1,)), ((), ())), preferred_element_type=f32
    )
    scores = jnp.where(causal, scores, 0.0)
    first_half = col < HEAD_DIM
    input_t = input_vec.T

    def two_heads(pair, carry):
        lanes = pl.ds(pl.multiple_of(pair * LANES, LANES), LANES)
        x = conv(lanes)
        held = state[:, lanes]
        high = held.astype(bf16)
        low = (held - high.astype(f32)).astype(bf16)
        inter = jnp.dot(output_vec, high, preferred_element_type=f32) + jnp.dot(
            output_vec, low, preferred_element_type=f32
        )
        turned = LANES - 2 * pair
        cum_here = pltpu.roll(cum, turned, 1)
        step_here = pltpu.roll(step, turned, 1)
        cums, steps, outs = [], [], []
        for h in range(2):
            row_of = pl.ds(2 * pair + h, 1)
            cum_i = jnp.broadcast_to(cum_here[:, h : h + 1], (BLOCK, BLOCK))
            weight = jnp.exp(jnp.minimum(cum_i - cum_rows[row_of, :], 0.0))
            mixing = (scores * weight * step_rows[row_of, :]).astype(bf16)
            outs.append(jnp.dot(mixing, x, preferred_element_type=f32))
            cums.append(cum_i)
            steps.append(jnp.broadcast_to(step_here[:, h : h + 1], (BLOCK, BLOCK)))
        cum_i = jnp.where(first_half, cums[0], cums[1])
        total = cum_i[BLOCK - 1 :, :]
        out = jnp.where(first_half, outs[0], outs[1]) + jnp.exp(cum_i) * inter
        gated_out[:, lanes] = (out * silu(gates[:, lanes].astype(f32))).astype(bf16)
        factor = jnp.where(first_half, steps[0], steps[1]) * jnp.exp(total - cum_i)
        scaled = (x.astype(f32) * factor).astype(bf16)
        state_out[:, lanes] = jnp.exp(total) * held + jnp.dot(
            input_t, scaled, preferred_element_type=f32
        )
        return carry

    lax.fori_loop(0, ch // LANES, two_heads, 0, unroll=2)


def scan_block(gates, sums, tail, state, index, table, rate, taps):
    ch = state.shape[1]
    wide = ch + 2 * STATE
    whole = lambda a: pl.BlockSpec(a.shape, lambda b: (0,) * a.ndim)
    others = (sums, tail, state, index, table, rate, taps)
    outs = (
        jax.ShapeDtypeStruct((BLOCK, ch), bf16),
        jax.ShapeDtypeStruct((STATE, ch), f32),
        jax.ShapeDtypeStruct((8, wide), f32),
    )
    return pl.pallas_call(
        scan_kernel,
        out_shape=outs,
        grid=(1,),
        in_specs=[pl.BlockSpec((BLOCK, ch), lambda b: (0, 0)), *map(whole, others)],
        out_specs=[whole(o) for o in outs],
        scratch_shapes=[
            pltpu.VMEM((BLOCK + 8, wide), f32),
            pltpu.VMEM((LANES, BLOCK), f32),
            pltpu.VMEM((LANES, BLOCK), f32),
        ],
        cost_estimate=pl.CostEstimate(
            flops=8 * BLOCK * BLOCK * ch,
            bytes_accessed=16 * BLOCK * ch,
            transcendentals=2 * BLOCK * BLOCK * ch // HEAD_DIM,
        ),
        name="scan_block",
    )(gates, *others)


def output_kernel(where, *refs, n, count):
    blocks = refs[: 2 * n * count]
    gain, weight, out, held, sems = refs[2 * n * count :]
    ch = held.shape[1] // 2
    width = weight.shape[1]
    here = where[0]

    def fetch(act):
        for block in range(count):
            for side in range(2):
                place = here if side == 0 else n - 1 - here
                for k in range(n):
                    source = blocks[(block * 2 + side) * n + k]
                    start = source.shape[1] - ch

                    @pl.when(place == k)
                    def _():
                        act(
                            pltpu.make_async_copy(
                                source.at[:, start:],
                                held.at[pl.ds(block * BLOCK, BLOCK), pl.ds(side * ch, ch)],
                                sems.at[block, side],
                            )
                        )

    fetch(lambda copy: copy.start())
    fetch(lambda copy: copy.wait())
    values = held[...].astype(f32)
    squares = jnp.sum(values * values, axis=1, keepdims=True)
    held[...] = (values * gain[...]).astype(bf16)
    tile = min(256, width)

    def some_columns(at, carry):
        part = pl.ds(pl.multiple_of(at * tile, tile), tile)
        out[:, part] = jnp.dot(
            held[...], weight[:, part], preferred_element_type=f32
        ).astype(bf16)
        return carry

    lax.fori_loop(0, width // tile, some_columns, 0)
    out[:, width:] = jnp.broadcast_to(squares, (count * BLOCK, LANES)).astype(bf16)


def output_block(where, blocks, n, gain, weight, ch):
    count = len(blocks) // (2 * n)
    width = weight.shape[1]
    whole = lambda a: pl.BlockSpec(a.shape, lambda b, w: (0, 0))
    return pl.pallas_call(
        functools.partial(output_kernel, n=n, count=count),
        out_shape=jax.ShapeDtypeStruct((count * BLOCK, width + LANES), bf16),
        grid_spec=pltpu.PrefetchScalarGridSpec(
            num_scalar_prefetch=1,
            grid=(1,),
            in_specs=[*(pl.BlockSpec(memory_space=pl.ANY) for _ in blocks), whole(gain), whole(weight)],
            out_specs=pl.BlockSpec((count * BLOCK, width + LANES), lambda b, w: (0, 0)),
            scratch_shapes=[
                pltpu.VMEM((count * BLOCK, 2 * ch), bf16),
                pltpu.SemaphoreType.DMA((count, 2)),
            ],
        ),
        cost_estimate=pl.CostEstimate(
            flops=4 * count * BLOCK * ch * width, bytes_accessed=4 * ch * width + 8 * count * BLOCK * ch, transcendentals=0
        ),
        name="output_block",
    )(where, *blocks, gain, weight)


def per_device(
    activations,
    token_adapter_index,
    gate_scanned_weight,
    state_vector_weight,
    time_step_weight,
    adapter_down_maps,
    adapter_up_maps,
    scanned_channel_taps,
    state_vector_taps,
    earlier_scanned_channels,
    earlier_state_vectors,
    head_step_bias,
    adapter_step_shift,
    head_decay_rate,
    starting_head_state,
    gated_norm_gain,
    output_projection_weight,
):
    n = lax.axis_size("seq")
    here = lax.axis_index("seq")
    shards = lax.axis_size("tensor")
    shard = lax.axis_index("tensor")
    core = shard % 2
    rows = activations.shape[0]
    tokens = rows * n
    depth = gate_scanned_weight.shape[0]
    heads_here = time_step_weight.shape[1]
    heads = heads_here // 2
    ch = heads * HEAD_DIM
    per_set = HEADS // HEAD_SETS
    size = tokens // shards
    assert per_set % heads == 0 and n % 2 == 0 and shards % 2 == 0 and size % BLOCK == 0
    blocks = tokens // BLOCK
    pairs_a = [(j, j ^ 1) for j in range(n)]
    pairs_b = [(j, ((j - 1) ^ 1) + 1) for j in range(1, n - 1)]
    swap = [(j, j ^ 1) for j in range(shards)]
    at_first = here == 0
    at_end = at_first | (here == n - 1)
    odd = here % 2
    as_int = lambda v: v.astype(jnp.int32)

    def own(array, start, count, axis):
        return lax.dynamic_slice_in_dim(array, start, count, axis)

    half = depth // 2
    index_rows = 16 * -(-rows // (16 * half))
    index_pad = jnp.pad(
        token_adapter_index.astype(bf16), (0, index_rows * half - rows)
    ).reshape(index_rows, half)

    def piece(dest):
        part = lax.dynamic_slice(activations, (0, dest * depth + core * half), (rows, half))
        return jnp.concatenate([part, index_pad], axis=0)

    pieces = [piece(here)]
    for k in range(1, n):
        pairs = [(j, (j + k) % n) for j in range(n)]
        pieces.append(lax.ppermute(piece((here + k) % n), "seq", pairs))

    def by_pair(array):
        split = array.reshape(array.shape[0] // 16, 16, 2, array.shape[2])
        return jnp.swapaxes(split, 1, 2)

    weight = by_pair(gate_scanned_weight)
    up = by_pair(adapter_up_maps)

    def small_of(end):
        first = (shard * heads_here + end * heads) // per_set * STATE
        io = own(state_vector_weight, first, STATE, 2).reshape(depth, 2 * STATE)
        steps = time_step_weight[:, end * heads : (end + 1) * heads]
        return jnp.concatenate([io, jnp.pad(steps, ((0, 0), (0, LANES - heads)))], axis=1)

    small = jnp.stack([small_of(0), small_of(1)])
    mine, weight, up, small = lax.optimization_barrier((jnp.stack(pieces), weight, up, small))
    other = lax.ppermute(mine, "tensor", swap)
    index = mine[:, rows:].reshape(n, -1)[:, :rows]
    index = jnp.concatenate(
        [lax.dynamic_index_in_dim(index, (here - b) % n, 0, False) for b in range(n)]
    ).astype(f32).reshape(blocks, 1, BLOCK)

    order = [as_int(core), as_int(1 - odd)] + [as_int((here - b) % n) for b in range(n)]
    mixed, gates = project(
        jnp.stack(order), mine, other, adapter_down_maps, weight, up, small, rows, ch
    )

    end = jnp.where(at_first, 0, 1)
    first_head = end * heads
    first_ch = end * ch
    first_io = (shard * heads_here + first_head) // per_set * STATE
    taps = jnp.concatenate(
        [
            own(scanned_channel_taps, first_ch, ch, 1),
            own(state_vector_taps, first_io, STATE, 2).reshape(CONV, 2 * STATE),
        ],
        axis=1,
    )
    tail = jnp.concatenate(
        [
            own(earlier_scanned_channels, first_ch, ch, 1),
            own(earlier_state_vectors, first_io, STATE, 2).reshape(CONV - 1, 2 * STATE),
        ],
        axis=1,
    ).astype(f32)
    tail = jnp.pad(tail, ((8 - (CONV - 1), 0), (0, 0)))
    table = own(adapter_step_shift + head_step_bias, first_head, heads, 1)
    table = jnp.pad(table, ((0, LANES - ADAPTER_COUNT), (0, LANES - heads)))
    rate = jnp.pad(own(head_decay_rate, first_head, heads, 0), (0, LANES - heads))[None]
    state = own(starting_head_state, first_head, heads, 0).reshape(ch, STATE).T
    gain = gated_norm_gain[None]

    def turn(step):
        to_last = jnp.clip(step - here, 0, blocks - 1)
        to_first = jnp.clip(step - (n - 1 - here), 0, blocks - 1)
        return jnp.where(odd == 0, to_last, to_first), jnp.where(odd == 0, to_first, to_last)

    def taken(array, step):
        shape = (1, BLOCK, array.shape[2])
        return tuple(
            lax.dynamic_slice(array, (side, at * BLOCK, 0), shape)[0]
            for side, at in enumerate(turn(step))
        )

    def added(a, b):
        return (a.astype(f32) + b.astype(f32)).astype(bf16)

    def onward(pair):
        from_a = lax.ppermute(pair[0], "seq", pairs_a)
        from_b = lax.ppermute(pair[1], "seq", pairs_b)
        return from_a, from_b

    def tied(*pairs):
        flat = lax.optimization_barrier(tuple(a for pair in pairs for a in pair))
        return [tuple(flat[k : k + 2]) for k in range(0, len(flat), 2)]

    sends = blocks + n - 2
    last_step = blocks + 2 * n - 3
    per = size // BLOCK
    sums = came = before = gated = None
    went, arrived, states, outs = {}, {}, [], []
    pending = None
    for step in range(last_step + 1):
        block = step - (n - 1)
        if step <= sends:
            go = taken(mixed, step)
            if step > 1:
                sums, before = tied(sums, before)
            if step > 0:
                go = added(go[0], sums[1]), added(go[1], sums[0])
                came, sums = tied(came, sums)
            before = came
            if step < sends:
                sums = onward(go)
        else:
            (came,) = tied(came)
        if step < n:
            gate = taken(gates, step)
            if step > 0:
                gate = added(gate[0], came[1]), added(gate[1], came[0])
            onto = gate
            if step == n - 1 and sends > step:
                onto = gate
        if n <= step < sends:
            where = jnp.stack([as_int(at_end), *map(as_int, turn(step))])
            onto = gate = merge(where, gates, came, gated)
        elif step == sends:
            gate = (None, added(taken(gates, step)[1], came[0][:, :ch]))
        if step >= max(n, sends):
            onto = came[1][:, -ch:], came[0][:, -ch:]
            if gated is not None:
                onto = jnp.where(at_end, gated, onto[0]), onto[1]
        came = onward(onto)
        arrived[step] = came
        if block >= 0:
            if gated is not None:
                went[block - 1] = onto[0]
            gated = None
        if 0 <= block < blocks:
            gated, state, tail = scan_block(
                gate[1], go[1], tail, state, index[block], table, rate, taps
            )
            if pending is not None:
                state, outs[pending] = lax.optimization_barrier((state, outs[pending]))
                pending = None
            if (block + 1) * BLOCK % rows == 0:
                states.append(state.astype(bf16).T)
        elif pending is not None:
            came, (outs[pending], _) = tied(came, (outs[pending], state))
            pending = None
        done = step - (2 * n - 2)
        if done >= 0 and (done + 1) % per == 0:
            needed = []
            for b in range(done + 1 - per, done + 1):
                for _ in range(2):
                    needed.append(went[b])
                    needed.extend(arrived[b + n - 1 + k][1 - k % 2] for k in range(1, n))
            outs.append(
                output_block(as_int(here)[None], needed, n, gain, output_projection_weight, ch)
            )
            pending = len(outs) - 1

    landed = [jnp.where(at_first, states[0], states[n - 1])]
    for k in range(1, n):
        leaving = jnp.where(at_first, states[k], states[n - 1 - k])
        landed.append(lax.ppermute(leaving, "seq", [(0, k), (n - 1, n - 1 - k)]))
    landed = jnp.stack(landed)
    finish = jnp.concatenate(
        [lax.dynamic_index_in_dim(landed, which, 0, False) for which in (here, n - 1 - here)], axis=0
    ).astype(f32).reshape(heads_here, HEAD_DIM, STATE)

    chips = shards // 2
    chip = shard // 2
    if chips == 2:
        total = None
        for t in range(shards):
            give = [(j, j ^ 1) for j in range(shards) if j % 2 != t % 2]
            both = added(outs[t], lax.ppermute(outs[t], "tensor", give))
            came = lax.ppermute(both, "tensor", [(t ^ 2, t)])
            both = both.astype(f32) + came.astype(f32)
            total = both if total is None else jnp.where(shard == t, both, total)
    else:
        halves = []
        for k in range(chips):
            keep = jnp.where(core == 0, outs[2 * k], outs[2 * k + 1])
            give = jnp.where(core == 0, outs[2 * k + 1], outs[2 * k])
            halves.append(added(keep, lax.ppermute(give, "tensor", swap)))
        halves = jnp.stack(halves)
        total = lax.dynamic_index_in_dim(halves, chip, 0, False).astype(f32)
        for k in range(1, chips):
            pairs = [(j, (j + 2 * k) % shards) for j in range(shards)]
            give = lax.dynamic_index_in_dim(halves, (chip + k) % chips, 0, False)
            total = total + lax.ppermute(give, "tensor", pairs).astype(f32)
    width = output_projection_weight.shape[1]
    scale = lax.rsqrt(total[:, width : width + 1] / (HEADS * HEAD_DIM) + 1e-05)
    mixed = (total[:, :width] * scale).astype(bf16)
    return (mixed, finish[None])


def solution(mesh):
    return jax.shard_map(
        per_device,
        mesh=mesh,
        in_specs=(
            P(("groups", "seq"), None),
            P(("groups", "seq")),
            P("seq", None, "tensor"),
            P("seq", None, None),
            P("seq", "tensor"),
            P("seq", None),
            P(None, None, "tensor"),
            P(None, "tensor"),
            P(),
            P("groups", "tensor"),
            P("groups", None, None),
            P("tensor"),
            P(None, "tensor"),
            P("tensor"),
            P(("groups", "tensor"), None, None),
            P("tensor"),
            P("tensor", "seq"),
        ),
        out_specs=(P(("groups", "tensor"), "seq"), P(("groups", "seq"), "tensor", None, None)),
        check_vma=False,
    )
```

```python
import functools
import jax
import jax.numpy as jnp
from jax import lax
from jax.experimental import pallas as pl
from jax.experimental.pallas import tpu as pltpu
from jax.sharding import PartitionSpec as P


HEADS = 128
HEAD_DIM = 64
STATE = 128
HEAD_SETS = 8
ADAPTER_COUNT = 16
ADAPTER_RANK = 16
CONV = 4
BLOCK = 128
LANES = 128


bf16 = jnp.bfloat16
f32 = jnp.float32


def silu(v):
    return v / (1.0 + jnp.exp(-v))


def project_kernel(where, *refs, rows, first, count):
    mine, other, down, weight, up, small, *refs = refs
    earlier, (mixed_out, gate_out, values, held) = refs[:-4], refs[-4:]
    half = mine.shape[2]
    begin = first * rows
    depth = 2 * half
    core = where[0]
    step = pl.program_id(0)
    ch = gate_out.shape[2]
    tile = held.shape[1]
    per_end = ch // tile

    def plane(end):
        return jnp.where(where[1] == 1, 1 - end, end)

    @pl.when(step == 0)
    def _():
        rank = down.shape[1]
        span = min(half, rows)
        owner = lax.broadcasted_iota(jnp.int32, (rank, span), 0) // ADAPTER_RANK
        near = pl.ds(pl.multiple_of(core * half, half), half)
        far = pl.ds(pl.multiple_of((1 - core) * half, half), half)
        masks = []
        if earlier:
            mixed_out[:, :begin, :] = earlier[0][...]
            gate_out[:, :begin, :] = earlier[1][...]
        for b in range(count):
            source = where[2 + first + b]
            values[b * rows : (b + 1) * rows, near] = mine[source, :rows, :]
            values[b * rows : (b + 1) * rows, far] = other[source, :rows, :]
            for part in range(rows // span):
                index = mine[source, rows : rows + 16, :span].astype(f32)
                index = index[part : part + 1].astype(jnp.int32)
                masks.append((owner == index).astype(f32).T)
        mask = masks[0] if len(masks) == 1 else jnp.concatenate(masks, axis=0)
        full = jnp.dot(values[:, :depth], down[...], preferred_element_type=f32)
        values[:, depth:] = jnp.where(mask > 0.5, full, 0.0).astype(bf16)
        for end in range(2):
            mixed_out[plane(end), begin:, ch:] = jnp.dot(
                values[:, :depth], small[end], preferred_element_type=f32
            ).astype(bf16)

    end = step // per_end
    dst = pl.ds(pl.multiple_of((step - end * per_end) * tile, tile), tile)
    for pair, out in ((0, gate_out), (1, mixed_out)):
        held[:depth, :] = weight[:, pair].reshape(depth, tile)
        held[depth:, :] = up[:, pair].reshape(held.shape[0] - depth, tile)
        chunk = min(512, values.shape[0])

        def some_rows(at, carry):
            part = pl.ds(pl.multiple_of(at * chunk, chunk), chunk)
            onto = pl.ds(pl.multiple_of(begin + at * chunk, 256), chunk)
            out[plane(end), onto, dst] = jnp.dot(
                values[part, :], held[...], preferred_element_type=f32
            ).astype(bf16)
            return carry

        lax.fori_loop(0, values.shape[0] // chunk, some_rows, 0)


def project(where, mine, other, down, weight, up, small, rows, ch, count, earlier=()):
    half = mine.shape[2]
    first = earlier[0].shape[1] // rows if earlier else 0
    n = first + count
    tile = min(256, ch)
    whole = lambda a: pl.BlockSpec(a.shape, lambda b, w: (0,) * a.ndim)
    striped = lambda a: pl.BlockSpec((*a.shape[:3], tile), lambda b, w: (0, 0, 0, b))
    wide = ch + small.shape[2]
    held = lambda c: pl.BlockSpec((2, n * rows, c), lambda b, w: (0, 0, 0))
    full = 2 * half + down.shape[1]
    return pl.pallas_call(
        functools.partial(project_kernel, rows=rows, first=first, count=count),
        out_shape=(
            jax.ShapeDtypeStruct((2, n * rows, wide), bf16),
            jax.ShapeDtypeStruct((2, n * rows, ch), bf16),
        ),
        grid_spec=pltpu.PrefetchScalarGridSpec(
            num_scalar_prefetch=1,
            grid=(2 * ch // tile,),
            in_specs=[
                whole(mine), whole(other), whole(down), striped(weight), striped(up), whole(small),
                *map(whole, earlier),
            ],
            out_specs=[held(wide), held(ch)],
            scratch_shapes=[pltpu.VMEM((count * rows, full), bf16), pltpu.VMEM((full, tile), bf16)],
        ),
        cost_estimate=pl.CostEstimate(
            flops=4 * count * rows * full * (ch + wide),
            bytes_accessed=2 * weight.size + 4 * n * rows * (ch + wide),
            transcendentals=0,
        ),
        name="project",
    )(where, mine, other, down, weight, up, small, *earlier)


def merge_kernel(where, gate_a, gate_b, came_a, came_b, gated, go_a, go_b, *, passing):
    ch = gated.shape[1]
    go_a[:, :ch] = (gate_a[0].astype(f32) + came_b[:, :ch].astype(f32)).astype(bf16)
    go_b[:, :ch] = (gate_b[0].astype(f32) + came_a[:, :ch].astype(f32)).astype(bf16)
    own = gated[...]
    if passing:
        own = jnp.where(where[0] == 1, own.astype(f32), came_b[:, ch:].astype(f32)).astype(bf16)
        go_b[:, ch:] = came_a[:, ch:]
    else:
        go_b[:, ch:] = own
    go_a[:, ch:] = own


def merge(where, gates, came, gated):
    ch = gated.shape[1]
    passing = came[0].shape[1] > ch
    whole = lambda a: pl.BlockSpec(a.shape, lambda b, w: (0,) * a.ndim)
    out = jax.ShapeDtypeStruct((BLOCK, 2 * ch), bf16)
    return pl.pallas_call(
        functools.partial(merge_kernel, passing=passing),
        out_shape=(out, out),
        grid_spec=pltpu.PrefetchScalarGridSpec(
            num_scalar_prefetch=1,
            grid=(1,),
            in_specs=[
                pl.BlockSpec((1, BLOCK, ch), lambda b, w: (0, w[1], 0)),
                pl.BlockSpec((1, BLOCK, ch), lambda b, w: (1, w[2], 0)),
                whole(came[0]), whole(came[1]), whole(gated),
            ],
            out_specs=[whole(out), whole(out)],
        ),
        cost_estimate=pl.CostEstimate(
            flops=4 * BLOCK * ch, bytes_accessed=22 * BLOCK * ch, transcendentals=0
        ),
        name="merge",
    )(where, gates, gates, *came, gated)


def scan_kernel(
    gates, sums, tail, state, index, table, rate, taps,
    gated_out, state_out, tail_out, rows, cum_rows, step_rows,
):
    ch = state.shape[1]
    wide = ch + 2 * STATE
    rows[0:8, :] = tail[...]
    rows[8 : 8 + BLOCK, :] = sums[:, :wide].astype(f32)
    tail_out[...] = rows[BLOCK : BLOCK + 8, :]

    def conv(at):
        total = jnp.zeros((BLOCK, LANES), f32)
        for k in range(CONV):
            begin = 8 - (CONV - 1) + k
            total = total + taps[k : k + 1, at] * rows[begin : begin + BLOCK, at]
        return silu(total).astype(bf16)

    input_vec = conv(pl.ds(ch, STATE))
    output_vec = conv(pl.ds(ch + STATE, STATE))
    row = lax.broadcasted_iota(jnp.int32, (BLOCK, BLOCK), 0)
    col = lax.broadcasted_iota(jnp.int32, (BLOCK, BLOCK), 1)
    causal = row >= col
    chosen = (row == index[...].astype(jnp.int32)).astype(f32).T
    shift = jnp.dot(
        chosen, table[...], precision=lax.Precision.HIGHEST, preferred_element_type=f32
    )
    raw = sums[:, wide:].astype(f32) + shift
    step = jnp.maximum(raw, 0.0) + jnp.log1p(jnp.exp(-jnp.abs(raw)))
    cum = jnp.dot(
        causal.astype(f32),
        -rate[...] * step,
        precision=lax.Precision.HIGHEST,
        preferred_element_type=f32,
    )
    cum_rows[...] = cum.T
    step_rows[...] = step.T
    scores = lax.dot_general(
        output_vec, input_vec, (((1,), (1,)), ((), ())), preferred_element_type=f32
    )
    scores = jnp.where(causal, scores, 0.0)
    first_half = col < HEAD_DIM
    input_t = input_vec.T

    def two_heads(pair, carry):
        lanes = pl.ds(pl.multiple_of(pair * LANES, LANES), LANES)
        x = conv(lanes)
        held = state[:, lanes]
        high = held.astype(bf16)
        low = (held - high.astype(f32)).astype(bf16)
        inter = jnp.dot(output_vec, high, preferred_element_type=f32) + jnp.dot(
            output_vec, low, preferred_element_type=f32
        )
        turned = LANES - 2 * pair
        cum_here = pltpu.roll(cum, turned, 1)
        step_here = pltpu.roll(step, turned, 1)
        cums, steps, outs = [], [], []
        for h in range(2):
            row_of = pl.ds(2 * pair + h, 1)
            cum_i = jnp.broadcast_to(cum_here[:, h : h + 1], (BLOCK, BLOCK))
            weight = jnp.exp(jnp.minimum(cum_i - cum_rows[row_of, :], 0.0))
            mixing = (scores * weight * step_rows[row_of, :]).astype(bf16)
            outs.append(jnp.dot(mixing, x, preferred_element_type=f32))
            cums.append(cum_i)
            steps.append(jnp.broadcast_to(step_here[:, h : h + 1], (BLOCK, BLOCK)))
        cum_i = jnp.where(first_half, cums[0], cums[1])
        total = cum_i[BLOCK - 1 :, :]
        out = jnp.where(first_half, outs[0], outs[1]) + jnp.exp(cum_i) * inter
        gated_out[:, lanes] = (out * silu(gates[:, lanes].astype(f32))).astype(bf16)
        factor = jnp.where(first_half, steps[0], steps[1]) * jnp.exp(total - cum_i)
        scaled = (x.astype(f32) * factor).astype(bf16)
        state_out[:, lanes] = jnp.exp(total) * held + jnp.dot(
            input_t, scaled, preferred_element_type=f32
        )
        return carry

    lax.fori_loop(0, ch // LANES, two_heads, 0, unroll=2)


def scan_block(gates, sums, tail, state, index, table, rate, taps):
    ch = state.shape[1]
    wide = ch + 2 * STATE
    whole = lambda a: pl.BlockSpec(a.shape, lambda b: (0,) * a.ndim)
    others = (sums, tail, state, index, table, rate, taps)
    outs = (
        jax.ShapeDtypeStruct((BLOCK, ch), bf16),
        jax.ShapeDtypeStruct((STATE, ch), f32),
        jax.ShapeDtypeStruct((8, wide), f32),
    )
    return pl.pallas_call(
        scan_kernel,
        out_shape=outs,
        grid=(1,),
        in_specs=[pl.BlockSpec((BLOCK, ch), lambda b: (0, 0)), *map(whole, others)],
        out_specs=[whole(o) for o in outs],
        scratch_shapes=[
            pltpu.VMEM((BLOCK + 8, wide), f32),
            pltpu.VMEM((LANES, BLOCK), f32),
            pltpu.VMEM((LANES, BLOCK), f32),
        ],
        cost_estimate=pl.CostEstimate(
            flops=8 * BLOCK * BLOCK * ch,
            bytes_accessed=16 * BLOCK * ch,
            transcendentals=2 * BLOCK * BLOCK * ch // HEAD_DIM,
        ),
        name="scan_block",
    )(gates, *others)


def output_kernel(where, *refs, n, count):
    blocks = refs[: 2 * n * count]
    gain, weight_source, out, held, weight, sems, weight_sem = refs[2 * n * count :]
    ch = held.shape[1] // 2
    width = weight.shape[1]
    here = where[0]

    def fetch(act):
        for block in range(count):
            for side in range(2):
                place = here if side == 0 else n - 1 - here
                for k in range(n):
                    source = blocks[(block * 2 + side) * n + k]
                    start = source.shape[1] - ch

                    @pl.when(place == k)
                    def _():
                        act(
                            pltpu.make_async_copy(
                                source.at[:, start:],
                                held.at[pl.ds(block * BLOCK, BLOCK), pl.ds(side * ch, ch)],
                                sems.at[block, side],
                            )
                        )

    fetch(lambda copy: copy.start())
    bring = pltpu.make_async_copy(weight_source, weight, weight_sem)
    bring.start()
    fetch(lambda copy: copy.wait())
    values = held[...].astype(f32)
    squares = jnp.sum(values * values, axis=1, keepdims=True)
    held[...] = (values * gain[...]).astype(bf16)
    tile = min(256, width)
    bring.wait()

    def some_columns(at, carry):
        part = pl.ds(pl.multiple_of(at * tile, tile), tile)
        out[:, part] = jnp.dot(
            held[...], weight[:, part], preferred_element_type=f32
        ).astype(bf16)
        return carry

    lax.fori_loop(0, width // tile, some_columns, 0)
    out[:, width:] = jnp.broadcast_to(squares, (count * BLOCK, LANES)).astype(bf16)


def output_block(where, blocks, n, gain, weight, ch):
    count = len(blocks) // (2 * n)
    width = weight.shape[1]
    whole = lambda a: pl.BlockSpec(a.shape, lambda b, w: (0, 0))
    return pl.pallas_call(
        functools.partial(output_kernel, n=n, count=count),
        out_shape=jax.ShapeDtypeStruct((count * BLOCK, width + LANES), bf16),
        grid_spec=pltpu.PrefetchScalarGridSpec(
            num_scalar_prefetch=1,
            grid=(1,),
            in_specs=[*(pl.BlockSpec(memory_space=pl.ANY) for _ in blocks), whole(gain), pl.BlockSpec(memory_space=pl.ANY)],
            out_specs=pl.BlockSpec((count * BLOCK, width + LANES), lambda b, w: (0, 0)),
            scratch_shapes=[
                pltpu.VMEM((count * BLOCK, 2 * ch), bf16),
                pltpu.VMEM(weight.shape, bf16),
                pltpu.SemaphoreType.DMA((count, 2)),
                pltpu.SemaphoreType.DMA,
            ],
        ),
        cost_estimate=pl.CostEstimate(
            flops=4 * count * BLOCK * ch * width, bytes_accessed=4 * ch * width + 8 * count * BLOCK * ch, transcendentals=0
        ),
        name="output_block",
    )(where, *blocks, gain, weight)


def per_device(
    activations,
    token_adapter_index,
    gate_scanned_weight,
    state_vector_weight,
    time_step_weight,
    adapter_down_maps,
    adapter_up_maps,
    scanned_channel_taps,
    state_vector_taps,
    earlier_scanned_channels,
    earlier_state_vectors,
    head_step_bias,
    adapter_step_shift,
    head_decay_rate,
    starting_head_state,
    gated_norm_gain,
    output_projection_weight,
):
    n = lax.axis_size("seq")
    here = lax.axis_index("seq")
    shards = lax.axis_size("tensor")
    shard = lax.axis_index("tensor")
    core = shard % 2
    rows = activations.shape[0]
    tokens = rows * n
    depth = gate_scanned_weight.shape[0]
    heads_here = time_step_weight.shape[1]
    heads = heads_here // 2
    ch = heads * HEAD_DIM
    per_set = HEADS // HEAD_SETS
    size = tokens // shards
    assert per_set % heads == 0 and n % 2 == 0 and shards % 2 == 0 and size % BLOCK == 0
    blocks = tokens // BLOCK
    pairs_a = [(j, j ^ 1) for j in range(n)]
    pairs_b = [(j, ((j - 1) ^ 1) + 1) for j in range(1, n - 1)]
    swap = [(j, j ^ 1) for j in range(shards)]
    at_first = here == 0
    at_end = at_first | (here == n - 1)
    odd = here % 2
    as_int = lambda v: v.astype(jnp.int32)

    def own(array, start, count, axis):
        return lax.dynamic_slice_in_dim(array, start, count, axis)

    half = depth // 2
    index_rows = 16 * -(-rows // (16 * half))
    index_pad = jnp.pad(
        token_adapter_index.astype(bf16), (0, index_rows * half - rows)
    ).reshape(index_rows, half)

    def piece(dest):
        part = lax.dynamic_slice(activations, (0, dest * depth + core * half), (rows, half))
        return jnp.concatenate([part, index_pad], axis=0)

    pieces = [piece(here)]
    for k in range(1, n):
        pairs = [(j, (j + k) % n) for j in range(n)]
        pieces.append(lax.ppermute(piece((here + k) % n), "seq", pairs))

    def by_pair(array):
        split = array.reshape(array.shape[0] // 16, 16, 2, array.shape[2])
        return jnp.swapaxes(split, 1, 2)

    weight = by_pair(gate_scanned_weight)
    up = by_pair(adapter_up_maps)

    def small_of(end):
        first = (shard * heads_here + end * heads) // per_set * STATE
        io = own(state_vector_weight, first, STATE, 2).reshape(depth, 2 * STATE)
        steps = time_step_weight[:, end * heads : (end + 1) * heads]
        return jnp.concatenate([io, jnp.pad(steps, ((0, 0), (0, LANES - heads)))], axis=1)

    small = jnp.stack([small_of(0), small_of(1)])
    mine, weight, up, small = lax.optimization_barrier((jnp.stack(pieces), weight, up, small))
    other = lax.ppermute(mine, "tensor", swap)
    index = mine[:, rows:].reshape(n, -1)[:, :rows]
    index = jnp.concatenate(
        [lax.dynamic_index_in_dim(index, (here - b) % n, 0, False) for b in range(n)]
    ).astype(f32).reshape(blocks, 1, BLOCK)

    order = [as_int(core), as_int(1 - odd)] + [as_int((here - b) % n) for b in range(n)]
    order = jnp.stack(order)
    projected = ()
    versions = []
    for count in (1, 1, n - 2) if n > 2 else (1, 1):
        projected = project(
            order, mine, other, adapter_down_maps, weight, up, small, rows, ch, count, projected
        )
        versions.append(projected)

    end = jnp.where(at_first, 0, 1)
    first_head = end * heads
    first_ch = end * ch
    first_io = (shard * heads_here + first_head) // per_set * STATE
    taps = jnp.concatenate(
        [
            own(scanned_channel_taps, first_ch, ch, 1),
            own(state_vector_taps, first_io, STATE, 2).reshape(CONV, 2 * STATE),
        ],
        axis=1,
    )
    tail = jnp.concatenate(
        [
            own(earlier_scanned_channels, first_ch, ch, 1),
            own(earlier_state_vectors, first_io, STATE, 2).reshape(CONV - 1, 2 * STATE),
        ],
        axis=1,
    ).astype(f32)
    tail = jnp.pad(tail, ((8 - (CONV - 1), 0), (0, 0)))
    table = own(adapter_step_shift + head_step_bias, first_head, heads, 1)
    table = jnp.pad(table, ((0, LANES - ADAPTER_COUNT), (0, LANES - heads)))
    rate = jnp.pad(own(head_decay_rate, first_head, heads, 0), (0, LANES - heads))[None]
    state = own(starting_head_state, first_head, heads, 0).reshape(ch, STATE).T
    gain = gated_norm_gain[None]

    def made(step):
        return versions[min(step * BLOCK // rows, len(versions) - 1)]

    def turn(step):
        limit = made(step)[0].shape[1] // BLOCK
        to_last = jnp.clip(step - here, 0, limit - 1)
        to_first = jnp.clip(step - (n - 1 - here), 0, limit - 1)
        return jnp.where(odd == 0, to_last, to_first), jnp.where(odd == 0, to_first, to_last)

    def taken(array, step):
        shape = (1, BLOCK, array.shape[2])
        return tuple(
            lax.dynamic_slice(array, (side, at * BLOCK, 0), shape)[0]
            for side, at in enumerate(turn(step))
        )

    def added(a, b):
        return (a.astype(f32) + b.astype(f32)).astype(bf16)

    def onward(pair):
        from_a = lax.ppermute(pair[0], "seq", pairs_a)
        from_b = lax.ppermute(pair[1], "seq", pairs_b)
        return from_a, from_b

    def tied(*pairs):
        flat = lax.optimization_barrier(tuple(a for pair in pairs for a in pair))
        return [tuple(flat[k : k + 2]) for k in range(0, len(flat), 2)]

    sends = blocks + n - 2
    last_step = blocks + 2 * n - 3
    per = size // BLOCK
    sums = came = before = gated = None
    went, arrived, states, outs = {}, {}, [], []
    pending = None
    for step in range(last_step + 1):
        block = step - (n - 1)
        if step <= sends:
            go = taken(made(step)[0], step)
            if step > 1:
                sums, before = tied(sums, before)
            if step > 0:
                go = added(go[0], sums[1]), added(go[1], sums[0])
                came, sums = tied(came, sums)
            before = came
            if step < sends:
                sums = onward(go)
        else:
            (came,) = tied(came)
        if step < n:
            gate = taken(made(step)[1], step)
            if step > 0:
                gate = added(gate[0], came[1]), added(gate[1], came[0])
            onto = gate
            if step == n - 1 and sends > step:
                onto = gate
        if n <= step < sends:
            where = jnp.stack([as_int(at_end), *map(as_int, turn(step))])
            onto = gate = merge(where, made(step)[1], came, gated)
        elif step == sends:
            gate = (None, added(taken(made(step)[1], step)[1], came[0][:, :ch]))
        if step >= max(n, sends):
            onto = came[1][:, -ch:], came[0][:, -ch:]
            if gated is not None:
                onto = jnp.where(at_end, gated, onto[0]), onto[1]
        came = onward(onto)
        arrived[step] = came
        if block >= 0:
            if gated is not None:
                went[block - 1] = onto[0]
            gated = None
        if 0 <= block < blocks:
            gated, state, tail = scan_block(
                gate[1], go[1], tail, state, index[block], table, rate, taps
            )
            if pending is not None and block + 1 < blocks:
                state, outs[pending] = lax.optimization_barrier((state, outs[pending]))
                pending = None
            if (block + 1) * BLOCK % rows == 0:
                states.append(state.astype(bf16).T)
        if pending is not None and step < last_step:
            came, (outs[pending], _) = tied(came, (outs[pending], state))
            pending = None
        done = step - (2 * n - 2)
        if done >= 0 and (done + 1) % per == 0:
            needed = []
            for b in range(done + 1 - per, done + 1):
                for _ in range(2):
                    needed.append(went[b])
                    needed.extend(arrived[b + n - 1 + k][1 - k % 2] for k in range(1, n))
            pending = len(outs)
            outs.append(
                output_block(as_int(here)[None], needed, n, gain, output_projection_weight, ch)
            )

    landed = [jnp.where(at_first, states[0], states[n - 1])]
    for k in range(1, n):
        leaving = jnp.where(at_first, states[k], states[n - 1 - k])
        landed.append(lax.ppermute(leaving, "seq", [(0, k), (n - 1, n - 1 - k)]))
    landed = jnp.stack(landed)
    finish = jnp.concatenate(
        [lax.dynamic_index_in_dim(landed, which, 0, False) for which in (here, n - 1 - here)], axis=0
    ).astype(f32).reshape(heads_here, HEAD_DIM, STATE)

    chips = shards // 2
    chip = shard // 2
    if chips == 2:
        keep = jnp.where(core == 0, outs[0], outs[1])
        give = jnp.where(core == 0, outs[1], outs[0])
        both = added(keep, lax.ppermute(give, "tensor", swap))
        came = lax.ppermute(both, "tensor", [(2, 0), (3, 1)])
        total = both.astype(f32) + came.astype(f32)
        for t in range(2, shards):
            give = [(j, j ^ 1) for j in range(shards) if j % 2 != t % 2]
            both = added(outs[t], lax.ppermute(outs[t], "tensor", give))
            came = lax.ppermute(both, "tensor", [(t ^ 2, t)])
            both = both.astype(f32) + came.astype(f32)
            total = jnp.where(shard == t, both, total)
            if t == shards - 2:
                total = lax.optimization_barrier(total)
    else:
        halves = []
        for k in range(chips):
            keep = jnp.where(core == 0, outs[2 * k], outs[2 * k + 1])
            give = jnp.where(core == 0, outs[2 * k + 1], outs[2 * k])
            halves.append(added(keep, lax.ppermute(give, "tensor", swap)))
        halves = jnp.stack(halves)
        total = lax.dynamic_index_in_dim(halves, chip, 0, False).astype(f32)
        for k in range(1, chips):
            pairs = [(j, (j + 2 * k) % shards) for j in range(shards)]
            give = lax.dynamic_index_in_dim(halves, (chip + k) % chips, 0, False)
            total = total + lax.ppermute(give, "tensor", pairs).astype(f32)
    width = output_projection_weight.shape[1]
    scale = lax.rsqrt(total[:, width : width + 1] / (HEADS * HEAD_DIM) + 1e-05)
    mixed = (total[:, :width] * scale).astype(bf16)
    return (mixed, finish[None])


def solution(mesh):
    return jax.shard_map(
        per_device,
        mesh=mesh,
        in_specs=(
            P(("groups", "seq"), None),
            P(("groups", "seq")),
            P("seq", None, "tensor"),
            P("seq", None, None),
            P("seq", "tensor"),
            P("seq", None),
            P(None, None, "tensor"),
            P(None, "tensor"),
            P(),
            P("groups", "tensor"),
            P("groups", None, None),
            P("tensor"),
            P(None, "tensor"),
            P("tensor"),
            P(("groups", "tensor"), None, None),
            P("tensor"),
            P("tensor", "seq"),
        ),
        out_specs=(P(("groups", "tensor"), "seq"), P(("groups", "seq"), "tensor", None, None)),
        check_vma=False,
    )
```

```python
import functools
import jax
import jax.numpy as jnp
from jax import lax
from jax.experimental import pallas as pl
from jax.experimental.pallas import tpu as pltpu
from jax.sharding import PartitionSpec as P


HEADS = 128
HEAD_DIM = 64
STATE = 128
HEAD_SETS = 8
ADAPTER_COUNT = 16
ADAPTER_RANK = 16
CONV = 4
BLOCK = 128
LANES = 128


bf16 = jnp.bfloat16
f32 = jnp.float32


def silu(v):
    return v / (1.0 + jnp.exp(-v))


def project_kernel(where, *refs, rows, first, count):
    mine, other, down, weight, up, small, *refs = refs
    earlier, (mixed_out, gate_out, values) = refs[:-3], refs[-3:]
    half = mine.shape[2]
    begin = first * rows
    depth = 2 * half
    core = where[0]
    step = pl.program_id(0)
    tile = gate_out.shape[2]
    per_end = pl.num_programs(0) // 2
    ch = mixed_out.shape[2] - small.shape[2]

    def plane(end):
        return jnp.where(where[1] == 1, 1 - end, end)

    @pl.when(step == 0)
    def _():
        rank = down.shape[1]
        span = min(half, rows)
        owner = lax.broadcasted_iota(jnp.int32, (rank, span), 0) // ADAPTER_RANK
        near = pl.ds(pl.multiple_of(core * half, half), half)
        far = pl.ds(pl.multiple_of((1 - core) * half, half), half)
        masks = []
        if earlier:
            mixed_out[:, :begin, :] = earlier[0][...]
        for b in range(count):
            source = where[2 + first + b] if count > 1 else 0
            values[b * rows : (b + 1) * rows, near] = mine[source, :rows, :]
            values[b * rows : (b + 1) * rows, far] = other[source, :rows, :]
            for part in range(rows // span):
                index = mine[source, rows : rows + 16, :span].astype(f32)
                index = index[part : part + 1].astype(jnp.int32)
                masks.append((owner == index).astype(f32).T)
        mask = masks[0] if len(masks) == 1 else jnp.concatenate(masks, axis=0)
        full = jnp.dot(values[:, :depth], down[...], preferred_element_type=f32)
        values[:, depth:] = jnp.where(mask > 0.5, full, 0.0).astype(bf16)
        for end in range(2):
            mixed_out[plane(end), begin:, ch:] = jnp.dot(
                values[:, :depth], small[end], preferred_element_type=f32
            ).astype(bf16)

    end = step // per_end
    dst = pl.ds(pl.multiple_of((step - end * per_end) * tile, tile), tile)
    if earlier:
        gate_out[0, :begin, :] = earlier[1][0]

    def columns(part, pair):
        total = jnp.dot(
            values[part, :depth],
            weight[:, pair].reshape(depth, tile),
            preferred_element_type=f32,
        )
        return (
            total
            + jnp.dot(
                values[part, depth:],
                up[:, pair].reshape(values.shape[1] - depth, tile),
                preferred_element_type=f32,
            )
        ).astype(bf16)

    def some_rows(at, carry):
        part = pl.ds(pl.multiple_of(at * rows, rows), rows)
        onto = pl.ds(pl.multiple_of(begin + at * rows, rows), rows)
        gate_out[0, onto, :] = columns(part, 0)
        mixed_out[plane(end), onto, dst] = columns(part, 1)
        return carry

    lax.fori_loop(0, count, some_rows, 0)


def project(where, mine, other, down, weight, up, small, rows, ch, count, earlier=()):
    height, half = mine.shape[1:]
    first = earlier[0].shape[1] // rows if earlier else 0
    n = first + count
    tile = min(512, ch)
    per_end = ch // tile
    whole = lambda a: pl.BlockSpec(a.shape, lambda b, w: (0,) * a.ndim)
    picked = lambda a: (
        whole(a)
        if count > 1
        else pl.BlockSpec((1, height, half), lambda b, w: (w[2 + first], 0, 0))
    )
    striped = lambda a: pl.BlockSpec((*a.shape[:3], tile), lambda b, w: (0, 0, 0, b))
    gate_spot = lambda r: pl.BlockSpec(
        (1, r, tile),
        lambda b, w: (jnp.where(w[1] == 1, 1 - b // per_end, b // per_end), 0, b % per_end),
    )
    wide = ch + small.shape[2]
    full = 2 * half + down.shape[1]
    return pl.pallas_call(
        functools.partial(project_kernel, rows=rows, first=first, count=count),
        out_shape=(
            jax.ShapeDtypeStruct((2, n * rows, wide), bf16),
            jax.ShapeDtypeStruct((2, n * rows, ch), bf16),
        ),
        grid_spec=pltpu.PrefetchScalarGridSpec(
            num_scalar_prefetch=1,
            grid=(2 * per_end,),
            in_specs=[
                picked(mine), picked(other), whole(down), striped(weight), striped(up), whole(small),
                *((whole(earlier[0]), gate_spot(first * rows)) if earlier else ()),
            ],
            out_specs=[
                pl.BlockSpec((2, n * rows, wide), lambda b, w: (0, 0, 0)),
                gate_spot(n * rows),
            ],
            scratch_shapes=[pltpu.VMEM((count * rows, full), bf16)],
        ),
        cost_estimate=pl.CostEstimate(
            flops=4 * count * rows * full * (ch + wide),
            bytes_accessed=2 * weight.size + 4 * n * rows * (ch + wide),
            transcendentals=0,
        ),
        name="project",
    )(where, mine, other, down, weight, up, small, *earlier)


def merge_kernel(where, gate_a, gate_b, came_a, came_b, gated, go_a, go_b, *, passing):
    ch = gated.shape[1]
    go_a[:, :ch] = (gate_a[0].astype(f32) + came_b[:, :ch].astype(f32)).astype(bf16)
    go_b[:, :ch] = (gate_b[0].astype(f32) + came_a[:, :ch].astype(f32)).astype(bf16)
    own = gated[...]
    if passing:
        own = jnp.where(where[0] == 1, own.astype(f32), came_b[:, ch:].astype(f32)).astype(bf16)
        go_b[:, ch:] = came_a[:, ch:]
    else:
        go_b[:, ch:] = own
    go_a[:, ch:] = own


def merge(where, gates, came, gated):
    ch = gated.shape[1]
    passing = came[0].shape[1] > ch
    whole = lambda a: pl.BlockSpec(a.shape, lambda b, w: (0,) * a.ndim)
    out = jax.ShapeDtypeStruct((BLOCK, 2 * ch), bf16)
    return pl.pallas_call(
        functools.partial(merge_kernel, passing=passing),
        out_shape=(out, out),
        grid_spec=pltpu.PrefetchScalarGridSpec(
            num_scalar_prefetch=1,
            grid=(1,),
            in_specs=[
                pl.BlockSpec((1, BLOCK, ch), lambda b, w: (0, w[1], 0)),
                pl.BlockSpec((1, BLOCK, ch), lambda b, w: (1, w[2], 0)),
                whole(came[0]), whole(came[1]), whole(gated),
            ],
            out_specs=[whole(out), whole(out)],
        ),
        cost_estimate=pl.CostEstimate(
            flops=4 * BLOCK * ch, bytes_accessed=22 * BLOCK * ch, transcendentals=0
        ),
        name="merge",
    )(where, gates, gates, *came, gated)


def scan_kernel(
    gates, sums, tail, state, index, table, rate, taps,
    gated_out, state_out, tail_out, rows, cum_rows, step_rows,
):
    ch = state.shape[1]
    wide = ch + 2 * STATE
    rows[0:8, :] = tail[...]
    rows[8 : 8 + BLOCK, :] = sums[:, :wide].astype(f32)
    tail_out[...] = rows[BLOCK : BLOCK + 8, :]

    def conv(at):
        total = jnp.zeros((BLOCK, LANES), f32)
        for k in range(CONV):
            begin = 8 - (CONV - 1) + k
            total = total + taps[k : k + 1, at] * rows[begin : begin + BLOCK, at]
        return silu(total).astype(bf16)

    input_vec = conv(pl.ds(ch, STATE))
    output_vec = conv(pl.ds(ch + STATE, STATE))
    row = lax.broadcasted_iota(jnp.int32, (BLOCK, BLOCK), 0)
    col = lax.broadcasted_iota(jnp.int32, (BLOCK, BLOCK), 1)
    causal = row >= col
    chosen = (row == index[...].astype(jnp.int32)).astype(f32).T
    shift = jnp.dot(
        chosen, table[...], precision=lax.Precision.HIGHEST, preferred_element_type=f32
    )
    raw = sums[:, wide:].astype(f32) + shift
    step = jnp.maximum(raw, 0.0) + jnp.log1p(jnp.exp(-jnp.abs(raw)))
    cum = jnp.dot(
        causal.astype(f32),
        -rate[...] * step,
        precision=lax.Precision.HIGHEST,
        preferred_element_type=f32,
    )
    cum_rows[...] = cum.T
    step_rows[...] = step.T
    scores = lax.dot_general(
        output_vec, input_vec, (((1,), (1,)), ((), ())), preferred_element_type=f32
    )
    scores = jnp.where(causal, scores, 0.0)
    first_half = col < HEAD_DIM
    input_t = input_vec.T

    def two_heads(pair, carry):
        lanes = pl.ds(pl.multiple_of(pair * LANES, LANES), LANES)
        x = conv(lanes)
        held = state[:, lanes]
        high = held.astype(bf16)
        low = (held - high.astype(f32)).astype(bf16)
        inter = jnp.dot(output_vec, high, preferred_element_type=f32) + jnp.dot(
            output_vec, low, preferred_element_type=f32
        )
        turned = LANES - 2 * pair
        cum_here = pltpu.roll(cum, turned, 1)
        step_here = pltpu.roll(step, turned, 1)
        cums, steps, outs = [], [], []
        for h in range(2):
            row_of = pl.ds(2 * pair + h, 1)
            cum_i = jnp.broadcast_to(cum_here[:, h : h + 1], (BLOCK, BLOCK))
            weight = jnp.exp(jnp.minimum(cum_i - cum_rows[row_of, :], 0.0))
            mixing = (scores * weight * step_rows[row_of, :]).astype(bf16)
            outs.append(jnp.dot(mixing, x, preferred_element_type=f32))
            cums.append(cum_i)
            steps.append(jnp.broadcast_to(step_here[:, h : h + 1], (BLOCK, BLOCK)))
        cum_i = jnp.where(first_half, cums[0], cums[1])
        total = cum_i[BLOCK - 1 :, :]
        out = jnp.where(first_half, outs[0], outs[1]) + jnp.exp(cum_i) * inter
        gated_out[:, lanes] = (out * silu(gates[:, lanes].astype(f32))).astype(bf16)
        factor = jnp.where(first_half, steps[0], steps[1]) * jnp.exp(total - cum_i)
        scaled = (x.astype(f32) * factor).astype(bf16)
        state_out[:, lanes] = jnp.exp(total) * held + jnp.dot(
            input_t, scaled, preferred_element_type=f32
        )
        return carry

    lax.fori_loop(0, ch // LANES, two_heads, 0, unroll=2)


def scan_block(gates, sums, tail, state, index, table, rate, taps):
    ch = state.shape[1]
    wide = ch + 2 * STATE
    whole = lambda a: pl.BlockSpec(a.shape, lambda b: (0,) * a.ndim)
    others = (sums, tail, state, index, table, rate, taps)
    outs = (
        jax.ShapeDtypeStruct((BLOCK, ch), bf16),
        jax.ShapeDtypeStruct((STATE, ch), f32),
        jax.ShapeDtypeStruct((8, wide), f32),
    )
    return pl.pallas_call(
        scan_kernel,
        out_shape=outs,
        grid=(1,),
        in_specs=[pl.BlockSpec((BLOCK, ch), lambda b: (0, 0)), *map(whole, others)],
        out_specs=[whole(o) for o in outs],
        scratch_shapes=[
            pltpu.VMEM((BLOCK + 8, wide), f32),
            pltpu.VMEM((LANES, BLOCK), f32),
            pltpu.VMEM((LANES, BLOCK), f32),
        ],
        cost_estimate=pl.CostEstimate(
            flops=8 * BLOCK * BLOCK * ch,
            bytes_accessed=16 * BLOCK * ch,
            transcendentals=2 * BLOCK * BLOCK * ch // HEAD_DIM,
        ),
        name="scan_block",
    )(gates, *others)


def output_kernel(where, *refs, n, count):
    blocks = refs[: 2 * n * count]
    gain, weight_source, out, held, weight, sems, weight_sems = refs[2 * n * count :]
    ch = held.shape[1] // 2
    width = weight.shape[1]
    here = where[0]

    def fetch(act):
        for block in range(count):
            for side in range(2):
                place = here if side == 0 else n - 1 - here
                for k in range(n):
                    source = blocks[(block * 2 + side) * n + k]
                    start = source.shape[1] - ch

                    @pl.when(place == k)
                    def _():
                        act(
                            pltpu.make_async_copy(
                                source.at[:, start:],
                                held.at[pl.ds(block * BLOCK, BLOCK), pl.ds(side * ch, ch)],
                                sems.at[block, side],
                            )
                        )

    fetch(lambda copy: copy.start())
    tile = min(256, width)
    tiles = width // tile
    for k in range(tiles):
        columns = pl.ds(k * tile, tile)
        pltpu.make_async_copy(
            weight_source.at[:, columns], weight.at[:, columns], weight_sems.at[k]
        ).start()
    fetch(lambda copy: copy.wait())
    values = held[...].astype(f32)
    squares = jnp.sum(values * values, axis=1, keepdims=True)
    held[...] = (values * gain[...]).astype(bf16)

    def some_columns(at, carry):
        part = pl.ds(pl.multiple_of(at * tile, tile), tile)
        pltpu.make_async_copy(
            weight_source.at[:, part], weight.at[:, part], weight_sems.at[at]
        ).wait()
        out[:, part] = jnp.dot(
            held[...], weight[:, part], preferred_element_type=f32
        ).astype(bf16)
        return carry

    lax.fori_loop(0, tiles, some_columns, 0)
    out[:, width:] = jnp.broadcast_to(squares, (count * BLOCK, LANES)).astype(bf16)


def output_block(where, blocks, n, gain, weight, ch):
    count = len(blocks) // (2 * n)
    width = weight.shape[1]
    whole = lambda a: pl.BlockSpec(a.shape, lambda b, w: (0, 0))
    return pl.pallas_call(
        functools.partial(output_kernel, n=n, count=count),
        out_shape=jax.ShapeDtypeStruct((count * BLOCK, width + LANES), bf16),
        grid_spec=pltpu.PrefetchScalarGridSpec(
            num_scalar_prefetch=1,
            grid=(1,),
            in_specs=[*(pl.BlockSpec(memory_space=pl.ANY) for _ in blocks), whole(gain), pl.BlockSpec(memory_space=pl.ANY)],
            out_specs=pl.BlockSpec((count * BLOCK, width + LANES), lambda b, w: (0, 0)),
            scratch_shapes=[
                pltpu.VMEM((count * BLOCK, 2 * ch), bf16),
                pltpu.VMEM(weight.shape, bf16),
                pltpu.SemaphoreType.DMA((count, 2)),
                pltpu.SemaphoreType.DMA((max(1, width // 256),)),
            ],
        ),
        cost_estimate=pl.CostEstimate(
            flops=4 * count * BLOCK * ch * width, bytes_accessed=4 * ch * width + 8 * count * BLOCK * ch, transcendentals=0
        ),
        name="output_block",
    )(where, *blocks, gain, weight)


def per_device(
    activations,
    token_adapter_index,
    gate_scanned_weight,
    state_vector_weight,
    time_step_weight,
    adapter_down_maps,
    adapter_up_maps,
    scanned_channel_taps,
    state_vector_taps,
    earlier_scanned_channels,
    earlier_state_vectors,
    head_step_bias,
    adapter_step_shift,
    head_decay_rate,
    starting_head_state,
    gated_norm_gain,
    output_projection_weight,
):
    n = lax.axis_size("seq")
    here = lax.axis_index("seq")
    shards = lax.axis_size("tensor")
    shard = lax.axis_index("tensor")
    core = shard % 2
    rows = activations.shape[0]
    tokens = rows * n
    depth = gate_scanned_weight.shape[0]
    heads_here = time_step_weight.shape[1]
    heads = heads_here // 2
    ch = heads * HEAD_DIM
    per_set = HEADS // HEAD_SETS
    size = tokens // shards
    assert per_set % heads == 0 and n % 2 == 0 and shards % 2 == 0 and size % BLOCK == 0
    blocks = tokens // BLOCK
    pairs_a = [(j, j ^ 1) for j in range(n)]
    pairs_b = [(j, ((j - 1) ^ 1) + 1) for j in range(1, n - 1)]
    swap = [(j, j ^ 1) for j in range(shards)]
    at_first = here == 0
    at_end = at_first | (here == n - 1)
    odd = here % 2
    as_int = lambda v: v.astype(jnp.int32)

    def own(array, start, count, axis):
        return lax.dynamic_slice_in_dim(array, start, count, axis)

    half = depth // 2
    index_rows = 16 * -(-rows // (16 * half))
    index_pad = jnp.pad(
        token_adapter_index.astype(bf16), (0, index_rows * half - rows)
    ).reshape(index_rows, half)

    def piece(dest):
        part = lax.dynamic_slice(activations, (0, dest * depth + core * half), (rows, half))
        return jnp.concatenate([part, index_pad], axis=0)

    pieces = [piece(here)]
    for k in range(1, n):
        pairs = [(j, (j + k) % n) for j in range(n)]
        pieces.append(lax.ppermute(piece((here + k) % n), "seq", pairs))

    def by_pair(array):
        split = array.reshape(array.shape[0] // 16, 16, 2, array.shape[2])
        return jnp.swapaxes(split, 1, 2)

    weight = by_pair(gate_scanned_weight)
    up = by_pair(adapter_up_maps)

    def small_of(end):
        first = (shard * heads_here + end * heads) // per_set * STATE
        io = own(state_vector_weight, first, STATE, 2).reshape(depth, 2 * STATE)
        steps = time_step_weight[:, end * heads : (end + 1) * heads]
        return jnp.concatenate([io, jnp.pad(steps, ((0, 0), (0, LANES - heads)))], axis=1)

    small = jnp.stack([small_of(0), small_of(1)])
    mine, weight, up, small = lax.optimization_barrier((jnp.stack(pieces), weight, up, small))
    other = lax.ppermute(mine, "tensor", swap)
    index = mine[:, rows:].reshape(n, -1)[:, :rows]
    index = jnp.concatenate(
        [lax.dynamic_index_in_dim(index, (here - b) % n, 0, False) for b in range(n)]
    ).astype(f32).reshape(blocks, 1, BLOCK)

    order = [as_int(core), as_int(1 - odd)] + [as_int((here - b) % n) for b in range(n)]
    order = jnp.stack(order)
    projected = ()
    versions = []
    for count in (1, n - 1):
        projected = project(
            order, mine, other, adapter_down_maps, weight, up, small, rows, ch, count, projected
        )
        versions.append(projected)

    end = jnp.where(at_first, 0, 1)
    first_head = end * heads
    first_ch = end * ch
    first_io = (shard * heads_here + first_head) // per_set * STATE
    taps = jnp.concatenate(
        [
            own(scanned_channel_taps, first_ch, ch, 1),
            own(state_vector_taps, first_io, STATE, 2).reshape(CONV, 2 * STATE),
        ],
        axis=1,
    )
    tail = jnp.concatenate(
        [
            own(earlier_scanned_channels, first_ch, ch, 1),
            own(earlier_state_vectors, first_io, STATE, 2).reshape(CONV - 1, 2 * STATE),
        ],
        axis=1,
    ).astype(f32)
    tail = jnp.pad(tail, ((8 - (CONV - 1), 0), (0, 0)))
    table = own(adapter_step_shift + head_step_bias, first_head, heads, 1)
    table = jnp.pad(table, ((0, LANES - ADAPTER_COUNT), (0, LANES - heads)))
    rate = jnp.pad(own(head_decay_rate, first_head, heads, 0), (0, LANES - heads))[None]
    state = own(starting_head_state, first_head, heads, 0).reshape(ch, STATE).T
    gain = gated_norm_gain[None]

    def made(step):
        return versions[min(step * BLOCK // rows, len(versions) - 1)]

    def turn(step):
        limit = made(step)[0].shape[1] // BLOCK
        to_last = jnp.clip(step - here, 0, limit - 1)
        to_first = jnp.clip(step - (n - 1 - here), 0, limit - 1)
        return jnp.where(odd == 0, to_last, to_first), jnp.where(odd == 0, to_first, to_last)

    def taken(array, step):
        shape = (1, BLOCK, array.shape[2])
        return tuple(
            lax.dynamic_slice(array, (side, at * BLOCK, 0), shape)[0]
            for side, at in enumerate(turn(step))
        )

    def added(a, b):
        return (a.astype(f32) + b.astype(f32)).astype(bf16)

    def onward(pair):
        from_a = lax.ppermute(pair[0], "seq", pairs_a)
        from_b = lax.ppermute(pair[1], "seq", pairs_b)
        return from_a, from_b

    def tied(*pairs):
        flat = lax.optimization_barrier(tuple(a for pair in pairs for a in pair))
        return [tuple(flat[k : k + 2]) for k in range(0, len(flat), 2)]

    sends = blocks + n - 2
    last_step = blocks + 2 * n - 3
    per = size // BLOCK
    sums = came = before = gated = None
    went, arrived, states, outs = {}, {}, [], []
    pending = None
    for step in range(last_step + 1):
        block = step - (n - 1)
        if step <= sends:
            go = taken(made(step)[0], step)
            if step > 1:
                sums, before = tied(sums, before)
            if step > 0:
                go = added(go[0], sums[1]), added(go[1], sums[0])
                came, sums = tied(came, sums)
            before = came
            if step < sends:
                sums = onward(go)
        else:
            (came,) = tied(came)
        if step < n:
            gate = taken(made(step)[1], step)
            if step > 0:
                gate = added(gate[0], came[1]), added(gate[1], came[0])
            onto = gate
            if step == n - 1 and sends > step:
                onto = gate
        if n <= step < sends:
            where = jnp.stack([as_int(at_end), *map(as_int, turn(step))])
            onto = gate = merge(where, made(step)[1], came, gated)
        elif step == sends:
            gate = (None, added(taken(made(step)[1], step)[1], came[0][:, :ch]))
        if step >= max(n, sends):
            onto = came[1][:, -ch:], came[0][:, -ch:]
            if gated is not None:
                onto = jnp.where(at_end, gated, onto[0]), onto[1]
        came = onward(onto)
        arrived[step] = came
        if block >= 0:
            if gated is not None:
                went[block - 1] = onto[0]
            gated = None
        if 0 <= block < blocks:
            gated, state, tail = scan_block(
                gate[1], go[1], tail, state, index[block], table, rate, taps
            )
            if pending is not None and block + 1 < blocks:
                state, outs[pending] = lax.optimization_barrier((state, outs[pending]))
                pending = None
            if (block + 1) * BLOCK % rows == 0:
                states.append(state.astype(bf16).T)
        if pending is not None and sends < step < last_step:
            came, (outs[pending], _) = tied(came, (outs[pending], state))
            pending = None
        done = step - (2 * n - 2)
        if done >= 0 and (done + 1) % per == 0:
            needed = []
            for b in range(done + 1 - per, done + 1):
                for _ in range(2):
                    needed.append(went[b])
                    needed.extend(arrived[b + n - 1 + k][1 - k % 2] for k in range(1, n))
            pending = len(outs)
            outs.append(
                output_block(as_int(here)[None], needed, n, gain, output_projection_weight, ch)
            )

    landed = [jnp.where(at_first, states[0], states[n - 1])]
    for k in range(1, n):
        leaving = jnp.where(at_first, states[k], states[n - 1 - k])
        landed.append(lax.ppermute(leaving, "seq", [(0, k), (n - 1, n - 1 - k)]))

    chips = shards // 2
    chip = shard // 2
    if chips == 2:
        keep = jnp.where(core == 0, outs[0], outs[1])
        give = jnp.where(core == 0, outs[1], outs[0])
        back = lax.ppermute(give, "tensor", swap)
        both = added(keep, back)
        came = lax.ppermute(both, "tensor", [(2, 0), (3, 1)])
        total = both.astype(f32) + came.astype(f32)
        for t in range(2, shards):
            give = [(j, j ^ 1) for j in range(shards) if j % 2 != t % 2]
            back = lax.ppermute(outs[t], "tensor", give)
            both = added(outs[t], back)
            came = lax.ppermute(both, "tensor", [(t ^ 2, t)])
            total = jnp.where(shard == t, both.astype(f32) + came.astype(f32), total)
            if t == shards - 2:
                total = lax.optimization_barrier(total)
    else:
        halves = []
        for k in range(chips):
            keep = jnp.where(core == 0, outs[2 * k], outs[2 * k + 1])
            give = jnp.where(core == 0, outs[2 * k + 1], outs[2 * k])
            halves.append(added(keep, lax.ppermute(give, "tensor", swap)))
        both = halves[-1]
        halves = jnp.stack(halves)
        total = lax.dynamic_index_in_dim(halves, chip, 0, False).astype(f32)
        for k in range(1, chips):
            pairs = [(j, (j + 2 * k) % shards) for j in range(shards)]
            give = lax.dynamic_index_in_dim(halves, (chip + k) % chips, 0, False)
            total = total + lax.ppermute(give, "tensor", pairs).astype(f32)
    *landed, _ = lax.optimization_barrier((*landed, both))
    landed = jnp.stack(landed)
    finish = jnp.concatenate(
        [lax.dynamic_index_in_dim(landed, which, 0, False) for which in (here, n - 1 - here)], axis=0
    ).astype(f32).reshape(heads_here, HEAD_DIM, STATE)
    width = output_projection_weight.shape[1]
    scale = lax.rsqrt(total[:, width : width + 1] / (HEADS * HEAD_DIM) + 1e-05)
    mixed = (total[:, :width] * scale).astype(bf16)
    return (mixed, finish[None])


def solution(mesh):
    return jax.shard_map(
        per_device,
        mesh=mesh,
        in_specs=(
            P(("groups", "seq"), None),
            P(("groups", "seq")),
            P("seq", None, "tensor"),
            P("seq", None, None),
            P("seq", "tensor"),
            P("seq", None),
            P(None, None, "tensor"),
            P(None, "tensor"),
            P(),
            P("groups", "tensor"),
            P("groups", None, None),
            P("tensor"),
            P(None, "tensor"),
            P("tensor"),
            P(("groups", "tensor"), None, None),
            P("tensor"),
            P("tensor", "seq"),
        ),
        out_specs=(P(("groups", "tensor"), "seq"), P(("groups", "seq"), "tensor", None, None)),
        check_vma=False,
    )
```

```python
import functools
import jax
import jax.numpy as jnp
from jax import lax
from jax.experimental import pallas as pl
from jax.experimental.pallas import tpu as pltpu
from jax.sharding import PartitionSpec as P


HEADS = 128
HEAD_DIM = 64
STATE = 128
HEAD_SETS = 8
ADAPTER_COUNT = 16
ADAPTER_RANK = 16
CONV = 4
BLOCK = 128
LANES = 128


bf16 = jnp.bfloat16
f32 = jnp.float32


def silu(v):
    return v / (1.0 + jnp.exp(-v))


def project_kernel(where, *refs, rows, first, count):
    mine, other, down, weight, up, small, *refs = refs
    earlier, (mixed_out, gate_out, values) = refs[:-3], refs[-3:]
    half = mine.shape[2]
    begin = first * rows
    depth = 2 * half
    core = where[0]
    step = pl.program_id(0)
    tile = gate_out.shape[2]
    per_end = pl.num_programs(0) // 2
    ch = mixed_out.shape[2] - small.shape[2]

    def plane(end):
        return jnp.where(where[1] == 1, 1 - end, end)

    @pl.when(step == 0)
    def _():
        rank = down.shape[1]
        span = min(half, rows)
        owner = lax.broadcasted_iota(jnp.int32, (rank, span), 0) // ADAPTER_RANK
        near = pl.ds(pl.multiple_of(core * half, half), half)
        far = pl.ds(pl.multiple_of((1 - core) * half, half), half)
        masks = []
        if earlier:
            mixed_out[:, :begin, :] = earlier[0][...]
        for b in range(count):
            source = where[2 + first + b] if count > 1 else 0
            values[b * rows : (b + 1) * rows, near] = mine[source, :rows, :]
            values[b * rows : (b + 1) * rows, far] = other[source, :rows, :]
            for part in range(rows // span):
                index = mine[source, rows : rows + 16, :span].astype(f32)
                index = index[part : part + 1].astype(jnp.int32)
                masks.append((owner == index).astype(f32).T)
        mask = masks[0] if len(masks) == 1 else jnp.concatenate(masks, axis=0)
        full = jnp.dot(values[:, :depth], down[...], preferred_element_type=f32)
        values[:, depth:] = jnp.where(mask > 0.5, full, 0.0).astype(bf16)
        for end in range(2):
            mixed_out[plane(end), begin:, ch:] = jnp.dot(
                values[:, :depth], small[end], preferred_element_type=f32
            ).astype(bf16)

    end = step // per_end
    dst = pl.ds(pl.multiple_of((step - end * per_end) * tile, tile), tile)
    if earlier:
        gate_out[0, :begin, :] = earlier[1][0]

    def columns(part, pair):
        total = jnp.dot(
            values[part, :depth],
            weight[:, pair].reshape(depth, tile),
            preferred_element_type=f32,
        )
        return (
            total
            + jnp.dot(
                values[part, depth:],
                up[:, pair].reshape(values.shape[1] - depth, tile),
                preferred_element_type=f32,
            )
        ).astype(bf16)

    def some_rows(at, carry):
        part = pl.ds(pl.multiple_of(at * rows, rows), rows)
        onto = pl.ds(pl.multiple_of(begin + at * rows, rows), rows)
        gate_out[0, onto, :] = columns(part, 0)
        mixed_out[plane(end), onto, dst] = columns(part, 1)
        return carry

    lax.fori_loop(0, count, some_rows, 0)


def project(where, mine, other, down, weight, up, small, rows, ch, count, earlier=()):
    height, half = mine.shape[1:]
    first = earlier[0].shape[1] // rows if earlier else 0
    n = first + count
    tile = min(512, ch)
    per_end = ch // tile
    whole = lambda a: pl.BlockSpec(a.shape, lambda b, w: (0,) * a.ndim)
    picked = lambda a: (
        whole(a)
        if count > 1
        else pl.BlockSpec((1, height, half), lambda b, w: (w[2 + first], 0, 0))
    )
    striped = lambda a: pl.BlockSpec((*a.shape[:3], tile), lambda b, w: (0, 0, 0, b))
    gate_spot = lambda r: pl.BlockSpec(
        (1, r, tile),
        lambda b, w: (jnp.where(w[1] == 1, 1 - b // per_end, b // per_end), 0, b % per_end),
    )
    wide = ch + small.shape[2]
    full = 2 * half + down.shape[1]
    return pl.pallas_call(
        functools.partial(project_kernel, rows=rows, first=first, count=count),
        out_shape=(
            jax.ShapeDtypeStruct((2, n * rows, wide), bf16),
            jax.ShapeDtypeStruct((2, n * rows, ch), bf16),
        ),
        grid_spec=pltpu.PrefetchScalarGridSpec(
            num_scalar_prefetch=1,
            grid=(2 * per_end,),
            in_specs=[
                picked(mine), picked(other), whole(down), striped(weight), striped(up), whole(small),
                *((whole(earlier[0]), gate_spot(first * rows)) if earlier else ()),
            ],
            out_specs=[
                pl.BlockSpec((2, n * rows, wide), lambda b, w: (0, 0, 0)),
                gate_spot(n * rows),
            ],
            scratch_shapes=[pltpu.VMEM((count * rows, full), bf16)],
        ),
        cost_estimate=pl.CostEstimate(
            flops=4 * count * rows * full * (ch + wide),
            bytes_accessed=2 * weight.size + 4 * n * rows * (ch + wide),
            transcendentals=0,
        ),
        name="project",
    )(where, mine, other, down, weight, up, small, *earlier)


def merge_kernel(where, gate_a, gate_b, came_a, came_b, gated, go_a, go_b, *, passing):
    ch = gated.shape[1]
    go_a[:, :ch] = (gate_a[0].astype(f32) + came_b[:, :ch].astype(f32)).astype(bf16)
    go_b[:, :ch] = (gate_b[0].astype(f32) + came_a[:, :ch].astype(f32)).astype(bf16)
    own = gated[...]
    if passing:
        own = jnp.where(where[0] == 1, own.astype(f32), came_b[:, ch:].astype(f32)).astype(bf16)
        go_b[:, ch:] = came_a[:, ch:]
    else:
        go_b[:, ch:] = own
    go_a[:, ch:] = own


def merge(where, gates, came, gated):
    ch = gated.shape[1]
    passing = came[0].shape[1] > ch
    whole = lambda a: pl.BlockSpec(a.shape, lambda b, w: (0,) * a.ndim)
    out = jax.ShapeDtypeStruct((BLOCK, 2 * ch), bf16)
    return pl.pallas_call(
        functools.partial(merge_kernel, passing=passing),
        out_shape=(out, out),
        grid_spec=pltpu.PrefetchScalarGridSpec(
            num_scalar_prefetch=1,
            grid=(1,),
            in_specs=[
                pl.BlockSpec((1, BLOCK, ch), lambda b, w: (0, w[1], 0)),
                pl.BlockSpec((1, BLOCK, ch), lambda b, w: (1, w[2], 0)),
                whole(came[0]), whole(came[1]), whole(gated),
            ],
            out_specs=[whole(out), whole(out)],
        ),
        cost_estimate=pl.CostEstimate(
            flops=4 * BLOCK * ch, bytes_accessed=22 * BLOCK * ch, transcendentals=0
        ),
        name="merge",
    )(where, gates, gates, *came, gated)


def scan_kernel(
    gates, sums, tail, state, index, table, rate, taps,
    gated_out, state_out, tail_out, rows, cum_rows, step_rows,
):
    ch = state.shape[1]
    wide = ch + 2 * STATE
    rows[0:8, :] = tail[...]
    rows[8 : 8 + BLOCK, :] = sums[:, :wide].astype(f32)
    tail_out[...] = rows[BLOCK : BLOCK + 8, :]

    def conv(at):
        total = jnp.zeros((BLOCK, LANES), f32)
        for k in range(CONV):
            begin = 8 - (CONV - 1) + k
            total = total + taps[k : k + 1, at] * rows[begin : begin + BLOCK, at]
        return silu(total).astype(bf16)

    input_vec = conv(pl.ds(ch, STATE))
    output_vec = conv(pl.ds(ch + STATE, STATE))
    row = lax.broadcasted_iota(jnp.int32, (BLOCK, BLOCK), 0)
    col = lax.broadcasted_iota(jnp.int32, (BLOCK, BLOCK), 1)
    causal = row >= col
    chosen = (row == index[...].astype(jnp.int32)).astype(f32).T
    shift = jnp.dot(
        chosen, table[...], precision=lax.Precision.HIGHEST, preferred_element_type=f32
    )
    raw = sums[:, wide:].astype(f32) + shift
    step = jnp.maximum(raw, 0.0) + jnp.log1p(jnp.exp(-jnp.abs(raw)))
    cum = jnp.dot(
        causal.astype(f32),
        -rate[...] * step,
        precision=lax.Precision.HIGHEST,
        preferred_element_type=f32,
    )
    cum_rows[...] = cum.T
    step_rows[...] = step.T
    scores = lax.dot_general(
        output_vec, input_vec, (((1,), (1,)), ((), ())), preferred_element_type=f32
    )
    scores = jnp.where(causal, scores, 0.0)
    first_half = col < HEAD_DIM
    input_t = input_vec.T

    def two_heads(pair, carry):
        lanes = pl.ds(pl.multiple_of(pair * LANES, LANES), LANES)
        x = conv(lanes)
        held = state[:, lanes]
        high = held.astype(bf16)
        low = (held - high.astype(f32)).astype(bf16)
        inter = jnp.dot(output_vec, high, preferred_element_type=f32) + jnp.dot(
            output_vec, low, preferred_element_type=f32
        )
        turned = LANES - 2 * pair
        cum_here = pltpu.roll(cum, turned, 1)
        step_here = pltpu.roll(step, turned, 1)
        cums, steps, outs = [], [], []
        for h in range(2):
            row_of = pl.ds(2 * pair + h, 1)
            cum_i = jnp.broadcast_to(cum_here[:, h : h + 1], (BLOCK, BLOCK))
            weight = jnp.exp(jnp.minimum(cum_i - cum_rows[row_of, :], 0.0))
            mixing = (scores * weight * step_rows[row_of, :]).astype(bf16)
            outs.append(jnp.dot(mixing, x, preferred_element_type=f32))
            cums.append(cum_i)
            steps.append(jnp.broadcast_to(step_here[:, h : h + 1], (BLOCK, BLOCK)))
        cum_i = jnp.where(first_half, cums[0], cums[1])
        total = cum_i[BLOCK - 1 :, :]
        out = jnp.where(first_half, outs[0], outs[1]) + jnp.exp(cum_i) * inter
        gated_out[:, lanes] = (out * silu(gates[:, lanes].astype(f32))).astype(bf16)
        factor = jnp.where(first_half, steps[0], steps[1]) * jnp.exp(total - cum_i)
        scaled = (x.astype(f32) * factor).astype(bf16)
        state_out[:, lanes] = jnp.exp(total) * held + jnp.dot(
            input_t, scaled, preferred_element_type=f32
        )
        return carry

    lax.fori_loop(0, ch // LANES, two_heads, 0, unroll=2)


def scan_block(gates, sums, tail, state, index, table, rate, taps):
    ch = state.shape[1]
    wide = ch + 2 * STATE
    whole = lambda a: pl.BlockSpec(a.shape, lambda b: (0,) * a.ndim)
    others = (sums, tail, state, index, table, rate, taps)
    outs = (
        jax.ShapeDtypeStruct((BLOCK, ch), bf16),
        jax.ShapeDtypeStruct((STATE, ch), f32),
        jax.ShapeDtypeStruct((8, wide), f32),
    )
    return pl.pallas_call(
        scan_kernel,
        out_shape=outs,
        grid=(1,),
        in_specs=[pl.BlockSpec((BLOCK, ch), lambda b: (0, 0)), *map(whole, others)],
        out_specs=[whole(o) for o in outs],
        scratch_shapes=[
            pltpu.VMEM((BLOCK + 8, wide), f32),
            pltpu.VMEM((LANES, BLOCK), f32),
            pltpu.VMEM((LANES, BLOCK), f32),
        ],
        cost_estimate=pl.CostEstimate(
            flops=8 * BLOCK * BLOCK * ch,
            bytes_accessed=16 * BLOCK * ch,
            transcendentals=2 * BLOCK * BLOCK * ch // HEAD_DIM,
        ),
        name="scan_block",
    )(gates, *others)


def output_kernel(where, *refs, n, count):
    blocks = refs[: 2 * n * count]
    gain, weight_source, out, held, weight, sems, weight_sems = refs[2 * n * count :]
    ch = held.shape[1] // 2
    width = weight.shape[1]
    here = where[0]

    def fetch(act):
        for block in range(count):
            for side in range(2):
                place = here if side == 0 else n - 1 - here
                for k in range(n):
                    source = blocks[(block * 2 + side) * n + k]
                    start = source.shape[1] - ch

                    @pl.when(place == k)
                    def _():
                        act(
                            pltpu.make_async_copy(
                                source.at[:, start:],
                                held.at[pl.ds(block * BLOCK, BLOCK), pl.ds(side * ch, ch)],
                                sems.at[block, side],
                            )
                        )

    fetch(lambda copy: copy.start())
    tile = min(256, width)
    tiles = width // tile
    for k in range(tiles):
        columns = pl.ds(k * tile, tile)
        pltpu.make_async_copy(
            weight_source.at[:, columns], weight.at[:, columns], weight_sems.at[k]
        ).start()
    fetch(lambda copy: copy.wait())
    values = held[...].astype(f32)
    squares = jnp.sum(values * values, axis=1, keepdims=True)
    held[...] = (values * gain[...]).astype(bf16)

    def some_columns(at, carry):
        part = pl.ds(pl.multiple_of(at * tile, tile), tile)
        pltpu.make_async_copy(
            weight_source.at[:, part], weight.at[:, part], weight_sems.at[at]
        ).wait()
        out[:, part] = jnp.dot(
            held[...], weight[:, part], preferred_element_type=f32
        ).astype(bf16)
        return carry

    lax.fori_loop(0, tiles, some_columns, 0)
    out[:, width:] = jnp.broadcast_to(squares, (count * BLOCK, LANES)).astype(bf16)


def output_block(where, blocks, n, gain, weight, ch):
    count = len(blocks) // (2 * n)
    width = weight.shape[1]
    whole = lambda a: pl.BlockSpec(a.shape, lambda b, w: (0, 0))
    return pl.pallas_call(
        functools.partial(output_kernel, n=n, count=count),
        out_shape=jax.ShapeDtypeStruct((count * BLOCK, width + LANES), bf16),
        grid_spec=pltpu.PrefetchScalarGridSpec(
            num_scalar_prefetch=1,
            grid=(1,),
            in_specs=[*(pl.BlockSpec(memory_space=pl.ANY) for _ in blocks), whole(gain), pl.BlockSpec(memory_space=pl.ANY)],
            out_specs=pl.BlockSpec((count * BLOCK, width + LANES), lambda b, w: (0, 0)),
            scratch_shapes=[
                pltpu.VMEM((count * BLOCK, 2 * ch), bf16),
                pltpu.VMEM(weight.shape, bf16),
                pltpu.SemaphoreType.DMA((count, 2)),
                pltpu.SemaphoreType.DMA((max(1, width // 256),)),
            ],
        ),
        cost_estimate=pl.CostEstimate(
            flops=4 * count * BLOCK * ch * width, bytes_accessed=4 * ch * width + 8 * count * BLOCK * ch, transcendentals=0
        ),
        name="output_block",
    )(where, *blocks, gain, weight)


def per_device(
    activations,
    token_adapter_index,
    gate_scanned_weight,
    state_vector_weight,
    time_step_weight,
    adapter_down_maps,
    adapter_up_maps,
    scanned_channel_taps,
    state_vector_taps,
    earlier_scanned_channels,
    earlier_state_vectors,
    head_step_bias,
    adapter_step_shift,
    head_decay_rate,
    starting_head_state,
    gated_norm_gain,
    output_projection_weight,
):
    n = lax.axis_size("seq")
    here = lax.axis_index("seq")
    shards = lax.axis_size("tensor")
    shard = lax.axis_index("tensor")
    core = shard % 2
    rows = activations.shape[0]
    tokens = rows * n
    depth = gate_scanned_weight.shape[0]
    heads_here = time_step_weight.shape[1]
    heads = heads_here // 2
    ch = heads * HEAD_DIM
    per_set = HEADS // HEAD_SETS
    size = tokens // shards
    assert per_set % heads == 0 and n % 2 == 0 and shards % 2 == 0 and size % BLOCK == 0
    blocks = tokens // BLOCK
    pairs_a = [(j, j ^ 1) for j in range(n)]
    pairs_b = [(j, ((j - 1) ^ 1) + 1) for j in range(1, n - 1)]
    swap = [(j, j ^ 1) for j in range(shards)]
    at_first = here == 0
    at_end = at_first | (here == n - 1)
    odd = here % 2
    as_int = lambda v: v.astype(jnp.int32)

    def own(array, start, count, axis):
        return lax.dynamic_slice_in_dim(array, start, count, axis)

    half = depth // 2
    index_rows = 16 * -(-rows // (16 * half))
    index_pad = jnp.pad(
        token_adapter_index.astype(bf16), (0, index_rows * half - rows)
    ).reshape(index_rows, half)

    def piece(dest):
        part = lax.dynamic_slice(activations, (0, dest * depth + core * half), (rows, half))
        return jnp.concatenate([part, index_pad], axis=0)

    pieces = [piece(here)]
    for k in range(1, n):
        pairs = [(j, (j + k) % n) for j in range(n)]
        pieces.append(lax.ppermute(piece((here + k) % n), "seq", pairs))

    def by_pair(array):
        split = array.reshape(array.shape[0] // 16, 16, 2, array.shape[2])
        return jnp.swapaxes(split, 1, 2)

    weight = by_pair(gate_scanned_weight)
    up = by_pair(adapter_up_maps)

    def small_of(end):
        first = (shard * heads_here + end * heads) // per_set * STATE
        io = own(state_vector_weight, first, STATE, 2).reshape(depth, 2 * STATE)
        steps = time_step_weight[:, end * heads : (end + 1) * heads]
        return jnp.concatenate([io, jnp.pad(steps, ((0, 0), (0, LANES - heads)))], axis=1)

    small = jnp.stack([small_of(0), small_of(1)])
    mine, weight, up, small = lax.optimization_barrier((jnp.stack(pieces), weight, up, small))
    other = lax.ppermute(mine, "tensor", swap)
    index = mine[:, rows:].reshape(n, -1)[:, :rows]
    index = jnp.concatenate(
        [lax.dynamic_index_in_dim(index, (here - b) % n, 0, False) for b in range(n)]
    ).astype(f32).reshape(blocks, 1, BLOCK)

    order = [as_int(core), as_int(1 - odd)] + [as_int((here - b) % n) for b in range(n)]
    order = jnp.stack(order)
    projected = ()
    versions = []
    for count in (1, n - 1):
        projected = project(
            order, mine, other, adapter_down_maps, weight, up, small, rows, ch, count, projected
        )
        versions.append(projected)

    end = jnp.where(at_first, 0, 1)
    first_head = end * heads
    first_ch = end * ch
    first_io = (shard * heads_here + first_head) // per_set * STATE
    taps = jnp.concatenate(
        [
            own(scanned_channel_taps, first_ch, ch, 1),
            own(state_vector_taps, first_io, STATE, 2).reshape(CONV, 2 * STATE),
        ],
        axis=1,
    )
    tail = jnp.concatenate(
        [
            own(earlier_scanned_channels, first_ch, ch, 1),
            own(earlier_state_vectors, first_io, STATE, 2).reshape(CONV - 1, 2 * STATE),
        ],
        axis=1,
    ).astype(f32)
    tail = jnp.pad(tail, ((8 - (CONV - 1), 0), (0, 0)))
    table = own(adapter_step_shift + head_step_bias, first_head, heads, 1)
    table = jnp.pad(table, ((0, LANES - ADAPTER_COUNT), (0, LANES - heads)))
    rate = jnp.pad(own(head_decay_rate, first_head, heads, 0), (0, LANES - heads))[None]
    state = own(starting_head_state, first_head, heads, 0).reshape(ch, STATE).T
    gain = gated_norm_gain[None]

    def made(step):
        return versions[min(step * BLOCK // rows, len(versions) - 1)]

    def turn(step):
        limit = made(step)[0].shape[1] // BLOCK
        to_last = jnp.clip(step - here, 0, limit - 1)
        to_first = jnp.clip(step - (n - 1 - here), 0, limit - 1)
        return jnp.where(odd == 0, to_last, to_first), jnp.where(odd == 0, to_first, to_last)

    def taken(array, step):
        shape = (1, BLOCK, array.shape[2])
        return tuple(
            lax.dynamic_slice(array, (side, at * BLOCK, 0), shape)[0]
            for side, at in enumerate(turn(step))
        )

    def added(a, b):
        return (a.astype(f32) + b.astype(f32)).astype(bf16)

    def onward(pair):
        from_a = lax.ppermute(pair[0], "seq", pairs_a)
        from_b = lax.ppermute(pair[1], "seq", pairs_b)
        return from_a, from_b

    def tied(*pairs):
        flat = lax.optimization_barrier(tuple(a for pair in pairs for a in pair))
        return [tuple(flat[k : k + 2]) for k in range(0, len(flat), 2)]

    sends = blocks + n - 2
    last_step = blocks + 2 * n - 3
    per = size // BLOCK
    chips = shards // 2
    chip = shard // 2
    groups = [2, 1, 1] if chips == 2 else [1] * shards
    group_ends = [sum(groups[: k + 1]) for k in range(len(groups))]
    sums = came = before = gated = None
    went, arrived, states, outs = {}, {}, [], []
    pending = None
    for step in range(last_step + 1):
        block = step - (n - 1)
        if step <= sends:
            go = taken(made(step)[0], step)
            if step > 1:
                sums, before = tied(sums, before)
            if step > 0:
                go = added(go[0], sums[1]), added(go[1], sums[0])
                came, sums = tied(came, sums)
            before = came
            if step < sends:
                sums = onward(go)
        else:
            (came,) = tied(came)
        if step < n:
            gate = taken(made(step)[1], step)
            if step > 0:
                gate = added(gate[0], came[1]), added(gate[1], came[0])
            onto = gate
            if step == n - 1 and sends > step:
                onto = gate
        if n <= step < sends:
            where = jnp.stack([as_int(at_end), *map(as_int, turn(step))])
            onto = gate = merge(where, made(step)[1], came, gated)
        elif step == sends:
            gate = (None, added(taken(made(step)[1], step)[1], came[0][:, :ch]))
        if step >= max(n, sends):
            onto = came[1][:, -ch:], came[0][:, -ch:]
            if gated is not None:
                onto = jnp.where(at_end, gated, onto[0]), onto[1]
        came = onward(onto)
        arrived[step] = came
        if block >= 0:
            if gated is not None:
                went[block - 1] = onto[0]
            gated = None
        if 0 <= block < blocks:
            gated, state, tail = scan_block(
                gate[1], go[1], tail, state, index[block], table, rate, taps
            )
            if pending is not None and block + 1 < blocks:
                state, outs[pending] = lax.optimization_barrier((state, outs[pending]))
                pending = None
            if (block + 1) * BLOCK % rows == 0:
                states.append(state.astype(bf16).T)
        if pending is not None and sends < step < last_step:
            came, (outs[pending], _) = tied(came, (outs[pending], state))
            pending = None
        done = step - (2 * n - 2)
        if done >= 0 and (done + 1) % per == 0 and (done + 1) // per in group_ends:
            needed = []
            for b in range(done + 1 - per * groups[len(outs)], done + 1):
                for _ in range(2):
                    needed.append(went[b])
                    needed.extend(arrived[b + n - 1 + k][1 - k % 2] for k in range(1, n))
            pending = len(outs)
            outs.append(
                output_block(as_int(here)[None], needed, n, gain, output_projection_weight, ch)
            )

    landed = [jnp.where(at_first, states[0], states[n - 1])]
    for k in range(1, n):
        leaving = jnp.where(at_first, states[k], states[n - 1 - k])
        landed.append(lax.ppermute(leaving, "seq", [(0, k), (n - 1, n - 1 - k)]))

    if chips == 2:
        keep = own(outs[0], core * size, size, 0)
        give = own(outs[0], (1 - core) * size, size, 0)
        back = lax.ppermute(give, "tensor", swap)
        both = added(keep, back)
        came = lax.ppermute(both, "tensor", [(2, 0), (3, 1)])
        total = both.astype(f32) + came.astype(f32)
        for t in range(2, shards):
            give = [(j, j ^ 1) for j in range(shards) if j % 2 != t % 2]
            back = lax.ppermute(outs[t - 1], "tensor", give)
            both = added(outs[t - 1], back)
            came = lax.ppermute(both, "tensor", [(t ^ 2, t)])
            total = jnp.where(shard == t, both.astype(f32) + came.astype(f32), total)
            if t == shards - 2:
                total = lax.optimization_barrier(total)
    else:
        halves = []
        for k in range(chips):
            keep = jnp.where(core == 0, outs[2 * k], outs[2 * k + 1])
            give = jnp.where(core == 0, outs[2 * k + 1], outs[2 * k])
            halves.append(added(keep, lax.ppermute(give, "tensor", swap)))
        both = halves[-1]
        halves = jnp.stack(halves)
        total = lax.dynamic_index_in_dim(halves, chip, 0, False).astype(f32)
        for k in range(1, chips):
            pairs = [(j, (j + 2 * k) % shards) for j in range(shards)]
            give = lax.dynamic_index_in_dim(halves, (chip + k) % chips, 0, False)
            total = total + lax.ppermute(give, "tensor", pairs).astype(f32)
    *landed, _ = lax.optimization_barrier((*landed, both))
    landed = jnp.stack(landed)
    finish = jnp.concatenate(
        [lax.dynamic_index_in_dim(landed, which, 0, False) for which in (here, n - 1 - here)], axis=0
    ).astype(f32).reshape(heads_here, HEAD_DIM, STATE)
    width = output_projection_weight.shape[1]
    scale = lax.rsqrt(total[:, width : width + 1] / (HEADS * HEAD_DIM) + 1e-05)
    mixed = (total[:, :width] * scale).astype(bf16)
    return (mixed, finish[None])


def solution(mesh):
    return jax.shard_map(
        per_device,
        mesh=mesh,
        in_specs=(
            P(("groups", "seq"), None),
            P(("groups", "seq")),
            P("seq", None, "tensor"),
            P("seq", None, None),
            P("seq", "tensor"),
            P("seq", None),
            P(None, None, "tensor"),
            P(None, "tensor"),
            P(),
            P("groups", "tensor"),
            P("groups", None, None),
            P("tensor"),
            P(None, "tensor"),
            P("tensor"),
            P(("groups", "tensor"), None, None),
            P("tensor"),
            P("tensor", "seq"),
        ),
        out_specs=(P(("groups", "tensor"), "seq"), P(("groups", "seq"), "tensor", None, None)),
        check_vma=False,
    )
```

```python
import functools
import jax
import jax.numpy as jnp
from jax import lax
from jax.experimental import pallas as pl
from jax.experimental.pallas import tpu as pltpu
from jax.sharding import PartitionSpec as P


HEADS = 128
HEAD_DIM = 64
STATE = 128
HEAD_SETS = 8
ADAPTER_COUNT = 16
ADAPTER_RANK = 16
CONV = 4
BLOCK = 128
LANES = 128


bf16 = jnp.bfloat16
f32 = jnp.float32


def silu(v):
    return v / (1.0 + jnp.exp(-v))


def project_kernel(where, *refs, rows, first, count):
    mine, other, down, weight, up, small, *refs = refs
    earlier, (mixed_out, gate_out, values) = refs[:-3], refs[-3:]
    half = mine.shape[2]
    begin = first * rows
    depth = 2 * half
    core = where[0]
    step = pl.program_id(0)
    tile = gate_out.shape[2]
    per_end = pl.num_programs(0) // 2
    ch = mixed_out.shape[2] - small.shape[2]

    def plane(end):
        return jnp.where(where[1] == 1, 1 - end, end)

    @pl.when(step == 0)
    def _():
        rank = down.shape[1]
        span = min(half, rows)
        owner = lax.broadcasted_iota(jnp.int32, (rank, span), 0) // ADAPTER_RANK
        near = pl.ds(pl.multiple_of(core * half, half), half)
        far = pl.ds(pl.multiple_of((1 - core) * half, half), half)
        masks = []
        if earlier:
            mixed_out[:, :begin, :] = earlier[0][...]
        for b in range(count):
            source = where[2 + first + b] if count > 1 else 0
            values[b * rows : (b + 1) * rows, near] = mine[source, :rows, :]
            values[b * rows : (b + 1) * rows, far] = other[source, :rows, :]
            for part in range(rows // span):
                index = mine[source, rows : rows + 16, :span].astype(f32)
                index = index[part : part + 1].astype(jnp.int32)
                masks.append((owner == index).astype(f32).T)
        mask = masks[0] if len(masks) == 1 else jnp.concatenate(masks, axis=0)
        full = jnp.dot(values[:, :depth], down[...], preferred_element_type=f32)
        values[:, depth:] = jnp.where(mask > 0.5, full, 0.0).astype(bf16)
        for end in range(2):
            mixed_out[plane(end), begin:, ch:] = jnp.dot(
                values[:, :depth], small[end], preferred_element_type=f32
            ).astype(bf16)

    end = step // per_end
    dst = pl.ds(pl.multiple_of((step - end * per_end) * tile, tile), tile)
    if earlier:
        gate_out[0, :begin, :] = earlier[1][0]

    def columns(part, pair):
        total = jnp.dot(
            values[part, :depth],
            weight[:, pair].reshape(depth, tile),
            preferred_element_type=f32,
        )
        return (
            total
            + jnp.dot(
                values[part, depth:],
                up[:, pair].reshape(values.shape[1] - depth, tile),
                preferred_element_type=f32,
            )
        ).astype(bf16)

    def some_rows(at, carry):
        part = pl.ds(pl.multiple_of(at * rows, rows), rows)
        onto = pl.ds(pl.multiple_of(begin + at * rows, rows), rows)
        gate_out[0, onto, :] = columns(part, 0)
        mixed_out[plane(end), onto, dst] = columns(part, 1)
        return carry

    lax.fori_loop(0, count, some_rows, 0)


def project(where, mine, other, down, weight, up, small, rows, ch, count, earlier=()):
    height, half = mine.shape[1:]
    first = earlier[0].shape[1] // rows if earlier else 0
    n = first + count
    tile = min(512, ch)
    per_end = ch // tile
    whole = lambda a: pl.BlockSpec(a.shape, lambda b, w: (0,) * a.ndim)
    picked = lambda a: (
        whole(a)
        if count > 1
        else pl.BlockSpec((1, height, half), lambda b, w: (w[2 + first], 0, 0))
    )
    striped = lambda a: pl.BlockSpec((*a.shape[:3], tile), lambda b, w: (0, 0, 0, b))
    gate_spot = lambda r: pl.BlockSpec(
        (1, r, tile),
        lambda b, w: (jnp.where(w[1] == 1, 1 - b // per_end, b // per_end), 0, b % per_end),
    )
    wide = ch + small.shape[2]
    full = 2 * half + down.shape[1]
    return pl.pallas_call(
        functools.partial(project_kernel, rows=rows, first=first, count=count),
        out_shape=(
            jax.ShapeDtypeStruct((2, n * rows, wide), bf16),
            jax.ShapeDtypeStruct((2, n * rows, ch), bf16),
        ),
        grid_spec=pltpu.PrefetchScalarGridSpec(
            num_scalar_prefetch=1,
            grid=(2 * per_end,),
            in_specs=[
                picked(mine), picked(other), whole(down), striped(weight), striped(up), whole(small),
                *((whole(earlier[0]), gate_spot(first * rows)) if earlier else ()),
            ],
            out_specs=[
                pl.BlockSpec((2, n * rows, wide), lambda b, w: (0, 0, 0)),
                gate_spot(n * rows),
            ],
            scratch_shapes=[pltpu.VMEM((count * rows, full), bf16)],
        ),
        cost_estimate=pl.CostEstimate(
            flops=4 * count * rows * full * (ch + wide),
            bytes_accessed=2 * weight.size + 4 * n * rows * (ch + wide),
            transcendentals=0,
        ),
        name="project",
    )(where, mine, other, down, weight, up, small, *earlier)


def merge_kernel(
    where, gate_a, gate_b, from_a, from_b, gated, go_a, go_b, came_a, came_b, sems, *, passing
):
    ch = gated.shape[1]
    copies = [
        pltpu.make_async_copy(source, target, sems.at[k])
        for k, (source, target) in enumerate(((from_a, came_a), (from_b, came_b)))
    ]
    for copy in copies:
        copy.start()
    for copy in copies:
        copy.wait()
    go_a[:, :ch] = (gate_a[0].astype(f32) + came_b[:, :ch].astype(f32)).astype(bf16)
    go_b[:, :ch] = (gate_b[0].astype(f32) + came_a[:, :ch].astype(f32)).astype(bf16)
    own = gated[...]
    if passing:
        own = jnp.where(where[0] == 1, own.astype(f32), came_b[:, ch:].astype(f32)).astype(bf16)
        go_b[:, ch:] = came_a[:, ch:]
    else:
        go_b[:, ch:] = own
    go_a[:, ch:] = own


def merge(where, gates, came, gated):
    ch = gated.shape[1]
    passing = came[0].shape[1] > ch
    whole = lambda a: pl.BlockSpec(a.shape, lambda b, w: (0,) * a.ndim)
    out = jax.ShapeDtypeStruct((BLOCK, 2 * ch), bf16)
    return pl.pallas_call(
        functools.partial(merge_kernel, passing=passing),
        out_shape=(out, out),
        grid_spec=pltpu.PrefetchScalarGridSpec(
            num_scalar_prefetch=1,
            grid=(1,),
            in_specs=[
                pl.BlockSpec((1, BLOCK, ch), lambda b, w: (0, w[1], 0)),
                pl.BlockSpec((1, BLOCK, ch), lambda b, w: (1, w[2], 0)),
                *(pl.BlockSpec(memory_space=pl.ANY) for _ in came), whole(gated),
            ],
            out_specs=[whole(out), whole(out)],
            scratch_shapes=[
                *(pltpu.VMEM(a.shape, bf16) for a in came),
                pltpu.SemaphoreType.DMA((2,)),
            ],
        ),
        cost_estimate=pl.CostEstimate(
            flops=4 * BLOCK * ch, bytes_accessed=22 * BLOCK * ch, transcendentals=0
        ),
        name="merge",
    )(where, gates, gates, *came, gated)


def scan_kernel(
    gates, sums, tail, state, index, table, rate, taps,
    gated_out, state_out, tail_out, rows, cum_rows, step_rows,
):
    ch = state.shape[1]
    wide = ch + 2 * STATE
    rows[0:8, :] = tail[...]
    rows[8 : 8 + BLOCK, :] = sums[:, :wide].astype(f32)
    tail_out[...] = rows[BLOCK : BLOCK + 8, :]

    def conv(at):
        total = jnp.zeros((BLOCK, LANES), f32)
        for k in range(CONV):
            begin = 8 - (CONV - 1) + k
            total = total + taps[k : k + 1, at] * rows[begin : begin + BLOCK, at]
        return silu(total).astype(bf16)

    input_vec = conv(pl.ds(ch, STATE))
    output_vec = conv(pl.ds(ch + STATE, STATE))
    row = lax.broadcasted_iota(jnp.int32, (BLOCK, BLOCK), 0)
    col = lax.broadcasted_iota(jnp.int32, (BLOCK, BLOCK), 1)
    causal = row >= col
    chosen = (row == index[...].astype(jnp.int32)).astype(f32).T
    shift = jnp.dot(
        chosen, table[...], precision=lax.Precision.HIGHEST, preferred_element_type=f32
    )
    raw = sums[:, wide:].astype(f32) + shift
    step = jnp.maximum(raw, 0.0) + jnp.log1p(jnp.exp(-jnp.abs(raw)))
    cum = jnp.dot(
        causal.astype(f32),
        -rate[...] * step,
        precision=lax.Precision.HIGHEST,
        preferred_element_type=f32,
    )
    cum_rows[...] = cum.T
    step_rows[...] = step.T
    scores = lax.dot_general(
        output_vec, input_vec, (((1,), (1,)), ((), ())), preferred_element_type=f32
    )
    scores = jnp.where(causal, scores, 0.0)
    first_half = col < HEAD_DIM
    input_t = input_vec.T

    def two_heads(pair, carry):
        lanes = pl.ds(pl.multiple_of(pair * LANES, LANES), LANES)
        x = conv(lanes)
        held = state[:, lanes]
        high = held.astype(bf16)
        low = (held - high.astype(f32)).astype(bf16)
        inter = jnp.dot(output_vec, high, preferred_element_type=f32) + jnp.dot(
            output_vec, low, preferred_element_type=f32
        )
        turned = LANES - 2 * pair
        cum_here = pltpu.roll(cum, turned, 1)
        step_here = pltpu.roll(step, turned, 1)
        cums, steps, outs = [], [], []
        for h in range(2):
            row_of = pl.ds(2 * pair + h, 1)
            cum_i = jnp.broadcast_to(cum_here[:, h : h + 1], (BLOCK, BLOCK))
            weight = jnp.exp(jnp.minimum(cum_i - cum_rows[row_of, :], 0.0))
            mixing = (scores * weight * step_rows[row_of, :]).astype(bf16)
            outs.append(jnp.dot(mixing, x, preferred_element_type=f32))
            cums.append(cum_i)
            steps.append(jnp.broadcast_to(step_here[:, h : h + 1], (BLOCK, BLOCK)))
        cum_i = jnp.where(first_half, cums[0], cums[1])
        total = cum_i[BLOCK - 1 :, :]
        out = jnp.where(first_half, outs[0], outs[1]) + jnp.exp(cum_i) * inter
        gated_out[:, lanes] = (out * silu(gates[:, lanes].astype(f32))).astype(bf16)
        factor = jnp.where(first_half, steps[0], steps[1]) * jnp.exp(total - cum_i)
        scaled = (x.astype(f32) * factor).astype(bf16)
        state_out[:, lanes] = jnp.exp(total) * held + jnp.dot(
            input_t, scaled, preferred_element_type=f32
        )
        return carry

    lax.fori_loop(0, ch // LANES, two_heads, 0, unroll=2)


def scan_block(gates, sums, tail, state, index, table, rate, taps):
    ch = state.shape[1]
    wide = ch + 2 * STATE
    whole = lambda a: pl.BlockSpec(a.shape, lambda b: (0,) * a.ndim)
    others = (sums, tail, state, index, table, rate, taps)
    outs = (
        jax.ShapeDtypeStruct((BLOCK, ch), bf16),
        jax.ShapeDtypeStruct((STATE, ch), f32),
        jax.ShapeDtypeStruct((8, wide), f32),
    )
    return pl.pallas_call(
        scan_kernel,
        out_shape=outs,
        grid=(1,),
        in_specs=[pl.BlockSpec((BLOCK, ch), lambda b: (0, 0)), *map(whole, others)],
        out_specs=[whole(o) for o in outs],
        scratch_shapes=[
            pltpu.VMEM((BLOCK + 8, wide), f32),
            pltpu.VMEM((LANES, BLOCK), f32),
            pltpu.VMEM((LANES, BLOCK), f32),
        ],
        cost_estimate=pl.CostEstimate(
            flops=8 * BLOCK * BLOCK * ch,
            bytes_accessed=16 * BLOCK * ch,
            transcendentals=2 * BLOCK * BLOCK * ch // HEAD_DIM,
        ),
        name="scan_block",
    )(gates, *others)


def output_kernel(where, *refs, n, count):
    blocks = refs[: 2 * n * count]
    gain, weight_source, out, held, weight, sems, weight_sems = refs[2 * n * count :]
    ch = held.shape[1] // 2
    width = weight.shape[1]
    here = where[0]

    def fetch(act):
        for block in range(count):
            for side in range(2):
                place = here if side == 0 else n - 1 - here
                for k in range(n):
                    source = blocks[(block * 2 + side) * n + k]
                    start = source.shape[1] - ch

                    @pl.when(place == k)
                    def _():
                        act(
                            pltpu.make_async_copy(
                                source.at[:, start:],
                                held.at[pl.ds(block * BLOCK, BLOCK), pl.ds(side * ch, ch)],
                                sems.at[block, side],
                            )
                        )

    fetch(lambda copy: copy.start())
    tile = min(256, width)
    tiles = width // tile
    for k in range(tiles):
        columns = pl.ds(k * tile, tile)
        pltpu.make_async_copy(
            weight_source.at[:, columns], weight.at[:, columns], weight_sems.at[k]
        ).start()
    fetch(lambda copy: copy.wait())
    values = held[...].astype(f32)
    squares = jnp.sum(values * values, axis=1, keepdims=True)
    held[...] = (values * gain[...]).astype(bf16)

    def some_columns(at, carry):
        part = pl.ds(pl.multiple_of(at * tile, tile), tile)
        pltpu.make_async_copy(
            weight_source.at[:, part], weight.at[:, part], weight_sems.at[at]
        ).wait()
        out[:, part] = jnp.dot(
            held[...], weight[:, part], preferred_element_type=f32
        ).astype(bf16)
        return carry

    lax.fori_loop(0, tiles, some_columns, 0)
    out[:, width:] = jnp.broadcast_to(squares, (count * BLOCK, LANES)).astype(bf16)


def output_block(where, blocks, n, gain, weight, ch):
    count = len(blocks) // (2 * n)
    width = weight.shape[1]
    whole = lambda a: pl.BlockSpec(a.shape, lambda b, w: (0, 0))
    return pl.pallas_call(
        functools.partial(output_kernel, n=n, count=count),
        out_shape=jax.ShapeDtypeStruct((count * BLOCK, width + LANES), bf16),
        grid_spec=pltpu.PrefetchScalarGridSpec(
            num_scalar_prefetch=1,
            grid=(1,),
            in_specs=[
                *(pl.BlockSpec(memory_space=pl.ANY) for _ in blocks),
                whole(gain),
                pl.BlockSpec(memory_space=pl.ANY),
            ],
            out_specs=pl.BlockSpec((count * BLOCK, width + LANES), lambda b, w: (0, 0)),
            scratch_shapes=[
                pltpu.VMEM((count * BLOCK, 2 * ch), bf16),
                pltpu.VMEM(weight.shape, bf16),
                pltpu.SemaphoreType.DMA((count, 2)),
                pltpu.SemaphoreType.DMA((max(1, width // 256),)),
            ],
        ),
        cost_estimate=pl.CostEstimate(
            flops=4 * count * BLOCK * ch * width, bytes_accessed=4 * ch * width + 8 * count * BLOCK * ch, transcendentals=0
        ),
        name="output_block",
    )(where, *blocks, gain, weight)


def per_device(
    activations,
    token_adapter_index,
    gate_scanned_weight,
    state_vector_weight,
    time_step_weight,
    adapter_down_maps,
    adapter_up_maps,
    scanned_channel_taps,
    state_vector_taps,
    earlier_scanned_channels,
    earlier_state_vectors,
    head_step_bias,
    adapter_step_shift,
    head_decay_rate,
    starting_head_state,
    gated_norm_gain,
    output_projection_weight,
):
    n = lax.axis_size("seq")
    here = lax.axis_index("seq")
    shards = lax.axis_size("tensor")
    shard = lax.axis_index("tensor")
    core = shard % 2
    rows = activations.shape[0]
    tokens = rows * n
    depth = gate_scanned_weight.shape[0]
    heads_here = time_step_weight.shape[1]
    heads = heads_here // 2
    ch = heads * HEAD_DIM
    per_set = HEADS // HEAD_SETS
    size = tokens // shards
    assert per_set % heads == 0 and n % 2 == 0 and shards % 2 == 0 and size % BLOCK == 0
    blocks = tokens // BLOCK
    pairs_a = [(j, j ^ 1) for j in range(n)]
    pairs_b = [(j, ((j - 1) ^ 1) + 1) for j in range(1, n - 1)]
    swap = [(j, j ^ 1) for j in range(shards)]
    at_first = here == 0
    at_end = at_first | (here == n - 1)
    odd = here % 2
    as_int = lambda v: v.astype(jnp.int32)

    def own(array, start, count, axis):
        return lax.dynamic_slice_in_dim(array, start, count, axis)

    half = depth // 2
    index_rows = 16 * -(-rows // (16 * half))
    index_pad = jnp.pad(
        token_adapter_index.astype(bf16), (0, index_rows * half - rows)
    ).reshape(index_rows, half)

    def piece(dest):
        part = lax.dynamic_slice(activations, (0, dest * depth + core * half), (rows, half))
        return jnp.concatenate([part, index_pad], axis=0)

    pieces = [piece(here)]
    for k in range(1, n):
        pairs = [(j, (j + k) % n) for j in range(n)]
        pieces.append(lax.ppermute(piece((here + k) % n), "seq", pairs))

    def by_pair(array):
        split = array.reshape(array.shape[0] // 16, 16, 2, array.shape[2])
        return jnp.swapaxes(split, 1, 2)

    weight = by_pair(gate_scanned_weight)
    up = by_pair(adapter_up_maps)

    def small_of(end):
        first = (shard * heads_here + end * heads) // per_set * STATE
        io = own(state_vector_weight, first, STATE, 2).reshape(depth, 2 * STATE)
        steps = time_step_weight[:, end * heads : (end + 1) * heads]
        return jnp.concatenate([io, jnp.pad(steps, ((0, 0), (0, LANES - heads)))], axis=1)

    small = jnp.stack([small_of(0), small_of(1)])
    mine, weight, up, small = lax.optimization_barrier((jnp.stack(pieces), weight, up, small))
    other = lax.ppermute(mine, "tensor", swap)
    index = mine[:, rows:].reshape(n, -1)[:, :rows]
    index = jnp.concatenate(
        [lax.dynamic_index_in_dim(index, (here - b) % n, 0, False) for b in range(n)]
    ).astype(f32).reshape(blocks, 1, BLOCK)

    order = [as_int(core), as_int(1 - odd)] + [as_int((here - b) % n) for b in range(n)]
    order = jnp.stack(order)
    projected = ()
    versions = []
    for count in (1, n - 1):
        projected = project(
            order, mine, other, adapter_down_maps, weight, up, small, rows, ch, count, projected
        )
        versions.append(projected)

    end = jnp.where(at_first, 0, 1)
    first_head = end * heads
    first_ch = end * ch
    first_io = (shard * heads_here + first_head) // per_set * STATE
    taps = jnp.concatenate(
        [
            own(scanned_channel_taps, first_ch, ch, 1),
            own(state_vector_taps, first_io, STATE, 2).reshape(CONV, 2 * STATE),
        ],
        axis=1,
    )
    tail = jnp.concatenate(
        [
            own(earlier_scanned_channels, first_ch, ch, 1),
            own(earlier_state_vectors, first_io, STATE, 2).reshape(CONV - 1, 2 * STATE),
        ],
        axis=1,
    ).astype(f32)
    tail = jnp.pad(tail, ((8 - (CONV - 1), 0), (0, 0)))
    table = own(adapter_step_shift + head_step_bias, first_head, heads, 1)
    table = jnp.pad(table, ((0, LANES - ADAPTER_COUNT), (0, LANES - heads)))
    rate = jnp.pad(own(head_decay_rate, first_head, heads, 0), (0, LANES - heads))[None]
    state = own(starting_head_state, first_head, heads, 0).reshape(ch, STATE).T
    gain = gated_norm_gain[None]

    def made(step):
        return versions[min(step * BLOCK // rows, len(versions) - 1)]

    def turn(step):
        limit = made(step)[0].shape[1] // BLOCK
        to_last = jnp.clip(step - here, 0, limit - 1)
        to_first = jnp.clip(step - (n - 1 - here), 0, limit - 1)
        return jnp.where(odd == 0, to_last, to_first), jnp.where(odd == 0, to_first, to_last)

    def taken(array, step):
        shape = (1, BLOCK, array.shape[2])
        return tuple(
            lax.dynamic_slice(array, (side, at * BLOCK, 0), shape)[0]
            for side, at in enumerate(turn(step))
        )

    def added(a, b):
        return (a.astype(f32) + b.astype(f32)).astype(bf16)

    def onward(pair):
        from_a = lax.ppermute(pair[0], "seq", pairs_a)
        from_b = lax.ppermute(pair[1], "seq", pairs_b)
        return from_a, from_b

    def tied(*pairs):
        flat = lax.optimization_barrier(tuple(a for pair in pairs for a in pair))
        return [tuple(flat[k : k + 2]) for k in range(0, len(flat), 2)]

    sends = blocks + n - 2
    last_step = blocks + 2 * n - 3
    per = size // BLOCK
    chips = shards // 2
    chip = shard // 2
    groups = [2, 1, 1] if chips == 2 else [1] * shards
    group_ends = [sum(groups[: k + 1]) for k in range(len(groups))]
    sums = came = before = gated = None
    went, arrived, states, outs = {}, {}, [], []
    pending = None
    for step in range(last_step + 1):
        block = step - (n - 1)
        if step <= sends:
            go = taken(made(step)[0], step)
            if step > 1:
                sums, before = tied(sums, before)
            if step > 0:
                go = added(go[0], sums[1]), added(go[1], sums[0])
                came, sums = tied(came, sums)
            before = came
            if step < sends:
                sums = onward(go)
        else:
            (came,) = tied(came)
        if step < n:
            gate = taken(made(step)[1], step)
            if step > 0:
                gate = added(gate[0], came[1]), added(gate[1], came[0])
            onto = gate
            if step == n - 1 and sends > step:
                onto = gate
        if n <= step < sends:
            where = jnp.stack([as_int(at_end), *map(as_int, turn(step))])
            onto = gate = merge(where, made(step)[1], came, gated)
        elif step == sends:
            gate = (None, added(taken(made(step)[1], step)[1], came[0][:, :ch]))
        if step >= max(n, sends):
            onto = came[1][:, -ch:], came[0][:, -ch:]
            if gated is not None:
                onto = jnp.where(at_end, gated, onto[0]), onto[1]
        came = onward(onto)
        arrived[step] = came
        if block >= 0:
            if gated is not None:
                went[block - 1] = onto[0]
            gated = None
        if 0 <= block < blocks:
            gated, state, tail = scan_block(
                gate[1], go[1], tail, state, index[block], table, rate, taps
            )
            if pending is not None and block + 1 < blocks:
                state, outs[pending] = lax.optimization_barrier((state, outs[pending]))
                pending = None
            if (block + 1) * BLOCK % rows == 0:
                states.append(state.astype(bf16).T)
        if pending is not None and sends < step < last_step:
            came, (outs[pending], _) = tied(came, (outs[pending], state))
            pending = None
        done = step - (2 * n - 2)
        if done >= 0 and (done + 1) % per == 0 and (done + 1) // per in group_ends:
            needed = []
            for b in range(done + 1 - per * groups[len(outs)], done + 1):
                for _ in range(2):
                    needed.append(went[b])
                    needed.extend(arrived[b + n - 1 + k][1 - k % 2] for k in range(1, n))
            pending = len(outs)
            outs.append(
                output_block(as_int(here)[None], needed, n, gain, output_projection_weight, ch)
            )

    landed = [jnp.where(at_first, states[0], states[n - 1])]
    for k in range(1, n):
        leaving = jnp.where(at_first, states[k], states[n - 1 - k])
        landed.append(lax.ppermute(leaving, "seq", [(0, k), (n - 1, n - 1 - k)]))

    if chips == 2:
        first, *rest = outs
        keep = own(first, core * size, size, 0), jnp.where(core == 0, *rest)
        give = own(first, (1 - core) * size, size, 0), jnp.where(core == 0, *rest[::-1])
        back = lax.ppermute(jnp.concatenate(give, axis=0), "tensor", swap)
        both = added(jnp.concatenate(keep, axis=0), back)
        total = own(both, chip * size, size, 0).astype(f32)
        give = own(both, (1 - chip) * size, size, 0)
        came = lax.ppermute(give, "tensor", [(j, j ^ 2) for j in range(shards)])
        total = total + came.astype(f32)
    else:
        halves = []
        for k in range(chips):
            keep = jnp.where(core == 0, outs[2 * k], outs[2 * k + 1])
            give = jnp.where(core == 0, outs[2 * k + 1], outs[2 * k])
            halves.append(added(keep, lax.ppermute(give, "tensor", swap)))
        both = halves[-1]
        halves = jnp.stack(halves)
        total = lax.dynamic_index_in_dim(halves, chip, 0, False).astype(f32)
        for k in range(1, chips):
            pairs = [(j, (j + 2 * k) % shards) for j in range(shards)]
            give = lax.dynamic_index_in_dim(halves, (chip + k) % chips, 0, False)
            total = total + lax.ppermute(give, "tensor", pairs).astype(f32)
    *landed, _ = lax.optimization_barrier((*landed, both))
    landed = jnp.stack(landed)
    finish = jnp.concatenate(
        [lax.dynamic_index_in_dim(landed, which, 0, False) for which in (here, n - 1 - here)], axis=0
    ).astype(f32).reshape(heads_here, HEAD_DIM, STATE)
    width = output_projection_weight.shape[1]
    scale = lax.rsqrt(total[:, width : width + 1] / (HEADS * HEAD_DIM) + 1e-05)
    mixed = (total[:, :width] * scale).astype(bf16)
    return (mixed, finish[None])


def solution(mesh):
    return jax.shard_map(
        per_device,
        mesh=mesh,
        in_specs=(
            P(("groups", "seq"), None),
            P(("groups", "seq")),
            P("seq", None, "tensor"),
            P("seq", None, None),
            P("seq", "tensor"),
            P("seq", None),
            P(None, None, "tensor"),
            P(None, "tensor"),
            P(),
            P("groups", "tensor"),
            P("groups", None, None),
            P("tensor"),
            P(None, "tensor"),
            P("tensor"),
            P(("groups", "tensor"), None, None),
            P("tensor"),
            P("tensor", "seq"),
        ),
        out_specs=(P(("groups", "tensor"), "seq"), P(("groups", "seq"), "tensor", None, None)),
        check_vma=False,
    )
```

```python
import functools
import jax
import jax.numpy as jnp
from jax import lax
from jax.experimental import pallas as pl
from jax.experimental.pallas import tpu as pltpu
from jax.sharding import PartitionSpec as P


HEADS = 128
HEAD_DIM = 64
STATE = 128
HEAD_SETS = 8
ADAPTER_COUNT = 16
ADAPTER_RANK = 16
CONV = 4
BLOCK = 128
LANES = 128


bf16 = jnp.bfloat16
f32 = jnp.float32


def silu(v):
    return v / (1.0 + jnp.exp(-v))


def project_kernel(where, *refs, rows, first, count):
    mine, other, down, weight, up, small, *refs = refs
    earlier, (mixed_out, gate_out, values) = refs[:-3], refs[-3:]
    half = mine.shape[2]
    begin = first * rows
    depth = 2 * half
    core = where[0]
    step = pl.program_id(0)
    tile = gate_out.shape[2]
    per_end = pl.num_programs(0) // 2
    ch = mixed_out.shape[2] - small.shape[2]

    def plane(end):
        return jnp.where(where[1] == 1, 1 - end, end)

    @pl.when(step == 0)
    def _():
        rank = down.shape[1]
        span = min(half, rows)
        owner = lax.broadcasted_iota(jnp.int32, (rank, span), 0) // ADAPTER_RANK
        near = pl.ds(pl.multiple_of(core * half, half), half)
        far = pl.ds(pl.multiple_of((1 - core) * half, half), half)
        masks = []
        if earlier:
            mixed_out[:, :begin, :] = earlier[0][...]
        for b in range(count):
            source = where[2 + first + b] if count > 1 else 0
            values[b * rows : (b + 1) * rows, near] = mine[source, :rows, :]
            values[b * rows : (b + 1) * rows, far] = other[source, :rows, :]
            for part in range(rows // span):
                index = mine[source, rows : rows + 16, :span].astype(f32)
                index = index[part : part + 1].astype(jnp.int32)
                masks.append((owner == index).astype(f32).T)
        mask = masks[0] if len(masks) == 1 else jnp.concatenate(masks, axis=0)
        full = jnp.dot(values[:, :depth], down[...], preferred_element_type=f32)
        values[:, depth:] = jnp.where(mask > 0.5, full, 0.0).astype(bf16)
        for end in range(2):
            mixed_out[plane(end), begin:, ch:] = jnp.dot(
                values[:, :depth], small[end], preferred_element_type=f32
            ).astype(bf16)

    end = step // per_end
    dst = pl.ds(pl.multiple_of((step - end * per_end) * tile, tile), tile)
    if earlier:
        gate_out[0, :begin, :] = earlier[1][0]

    def columns(part, pair):
        total = jnp.dot(
            values[part, :depth],
            weight[:, pair].reshape(depth, tile),
            preferred_element_type=f32,
        )
        return (
            total
            + jnp.dot(
                values[part, depth:],
                up[:, pair].reshape(values.shape[1] - depth, tile),
                preferred_element_type=f32,
            )
        ).astype(bf16)

    def some_rows(at, carry):
        part = pl.ds(pl.multiple_of(at * rows, rows), rows)
        onto = pl.ds(pl.multiple_of(begin + at * rows, rows), rows)
        gate_out[0, onto, :] = columns(part, 0)
        mixed_out[plane(end), onto, dst] = columns(part, 1)
        return carry

    lax.fori_loop(0, count, some_rows, 0)


def project(where, mine, other, down, weight, up, small, rows, ch, count, earlier=()):
    height, half = mine.shape[1:]
    first = earlier[0].shape[1] // rows if earlier else 0
    n = first + count
    tile = min(512, ch)
    per_end = ch // tile
    whole = lambda a: pl.BlockSpec(a.shape, lambda b, w: (0,) * a.ndim)
    picked = lambda a: (
        whole(a)
        if count > 1
        else pl.BlockSpec((1, height, half), lambda b, w: (w[2 + first], 0, 0))
    )
    striped = lambda a: pl.BlockSpec((*a.shape[:3], tile), lambda b, w: (0, 0, 0, b))
    gate_spot = lambda r: pl.BlockSpec(
        (1, r, tile),
        lambda b, w: (jnp.where(w[1] == 1, 1 - b // per_end, b // per_end), 0, b % per_end),
    )
    wide = ch + small.shape[2]
    full = 2 * half + down.shape[1]
    return pl.pallas_call(
        functools.partial(project_kernel, rows=rows, first=first, count=count),
        out_shape=(
            jax.ShapeDtypeStruct((2, n * rows, wide), bf16),
            jax.ShapeDtypeStruct((2, n * rows, ch), bf16),
        ),
        grid_spec=pltpu.PrefetchScalarGridSpec(
            num_scalar_prefetch=1,
            grid=(2 * per_end,),
            in_specs=[
                picked(mine), picked(other), whole(down), striped(weight), striped(up), whole(small),
                *((whole(earlier[0]), gate_spot(first * rows)) if earlier else ()),
            ],
            out_specs=[
                pl.BlockSpec((2, n * rows, wide), lambda b, w: (0, 0, 0)),
                gate_spot(n * rows),
            ],
            scratch_shapes=[pltpu.VMEM((count * rows, full), bf16)],
        ),
        cost_estimate=pl.CostEstimate(
            flops=4 * count * rows * full * (ch + wide),
            bytes_accessed=2 * weight.size + 4 * n * rows * (ch + wide),
            transcendentals=0,
        ),
        name="project",
    )(where, mine, other, down, weight, up, small, *earlier)


def merge_kernel(where, gate_a, gate_b, came_a, came_b, gated, go_a, go_b, *, passing):
    ch = gated.shape[1]
    go_a[:, :ch] = (gate_a[0].astype(f32) + came_b[:, :ch].astype(f32)).astype(bf16)
    go_b[:, :ch] = (gate_b[0].astype(f32) + came_a[:, :ch].astype(f32)).astype(bf16)
    own = gated[...]
    if passing:
        own = jnp.where(where[0] == 1, own.astype(f32), came_b[:, ch:].astype(f32)).astype(bf16)
        go_b[:, ch:] = came_a[:, ch:]
    else:
        go_b[:, ch:] = own
    go_a[:, ch:] = own


def merge(where, gates, came, gated):
    ch = gated.shape[1]
    passing = came[0].shape[1] > ch
    whole = lambda a: pl.BlockSpec(a.shape, lambda b, w: (0,) * a.ndim)
    out = jax.ShapeDtypeStruct((BLOCK, 2 * ch), bf16)
    return pl.pallas_call(
        functools.partial(merge_kernel, passing=passing),
        out_shape=(out, out),
        grid_spec=pltpu.PrefetchScalarGridSpec(
            num_scalar_prefetch=1,
            grid=(1,),
            in_specs=[
                pl.BlockSpec((1, BLOCK, ch), lambda b, w: (0, w[1], 0)),
                pl.BlockSpec((1, BLOCK, ch), lambda b, w: (1, w[2], 0)),
                whole(came[0]), whole(came[1]), whole(gated),
            ],
            out_specs=[whole(out), whole(out)],
        ),
        cost_estimate=pl.CostEstimate(
            flops=4 * BLOCK * ch, bytes_accessed=22 * BLOCK * ch, transcendentals=0
        ),
        name="merge",
    )(where, gates, gates, *came, gated)


def scan_kernel(
    gates, sums, tail, state, index, table, rate, taps,
    gated_out, state_out, tail_out, rows, cum_rows, step_rows,
):
    ch = state.shape[1]
    wide = ch + 2 * STATE
    rows[0:8, :] = tail[...]
    rows[8 : 8 + BLOCK, :] = sums[:, :wide].astype(f32)
    tail_out[...] = rows[BLOCK : BLOCK + 8, :]

    def conv(at):
        total = jnp.zeros((BLOCK, LANES), f32)
        for k in range(CONV):
            begin = 8 - (CONV - 1) + k
            total = total + taps[k : k + 1, at] * rows[begin : begin + BLOCK, at]
        return silu(total).astype(bf16)

    input_vec = conv(pl.ds(ch, STATE))
    output_vec = conv(pl.ds(ch + STATE, STATE))
    row = lax.broadcasted_iota(jnp.int32, (BLOCK, BLOCK), 0)
    col = lax.broadcasted_iota(jnp.int32, (BLOCK, BLOCK), 1)
    causal = row >= col
    chosen = (row == index[...].astype(jnp.int32)).astype(f32).T
    shift = jnp.dot(
        chosen, table[...], precision=lax.Precision.HIGHEST, preferred_element_type=f32
    )
    raw = sums[:, wide:].astype(f32) + shift
    step = jnp.maximum(raw, 0.0) + jnp.log1p(jnp.exp(-jnp.abs(raw)))
    cum = jnp.dot(
        causal.astype(f32),
        -rate[...] * step,
        precision=lax.Precision.HIGHEST,
        preferred_element_type=f32,
    )
    cum_rows[...] = cum.T
    step_rows[...] = step.T
    scores = lax.dot_general(
        output_vec, input_vec, (((1,), (1,)), ((), ())), preferred_element_type=f32
    )
    scores = jnp.where(causal, scores, 0.0)
    first_half = col < HEAD_DIM
    input_t = input_vec.T

    def two_heads(pair, carry):
        lanes = pl.ds(pl.multiple_of(pair * LANES, LANES), LANES)
        x = conv(lanes)
        held = state[:, lanes]
        high = held.astype(bf16)
        low = (held - high.astype(f32)).astype(bf16)
        inter = jnp.dot(output_vec, high, preferred_element_type=f32) + jnp.dot(
            output_vec, low, preferred_element_type=f32
        )
        turned = LANES - 2 * pair
        cum_here = pltpu.roll(cum, turned, 1)
        step_here = pltpu.roll(step, turned, 1)
        cums, steps, outs = [], [], []
        for h in range(2):
            row_of = pl.ds(2 * pair + h, 1)
            cum_i = jnp.broadcast_to(cum_here[:, h : h + 1], (BLOCK, BLOCK))
            weight = jnp.exp(jnp.minimum(cum_i - cum_rows[row_of, :], 0.0))
            mixing = (scores * weight * step_rows[row_of, :]).astype(bf16)
            outs.append(jnp.dot(mixing, x, preferred_element_type=f32))
            cums.append(cum_i)
            steps.append(jnp.broadcast_to(step_here[:, h : h + 1], (BLOCK, BLOCK)))
        cum_i = jnp.where(first_half, cums[0], cums[1])
        total = cum_i[BLOCK - 1 :, :]
        out = jnp.where(first_half, outs[0], outs[1]) + jnp.exp(cum_i) * inter
        gated_out[:, lanes] = (out * silu(gates[:, lanes].astype(f32))).astype(bf16)
        factor = jnp.where(first_half, steps[0], steps[1]) * jnp.exp(total - cum_i)
        scaled = (x.astype(f32) * factor).astype(bf16)
        state_out[:, lanes] = jnp.exp(total) * held + jnp.dot(
            input_t, scaled, preferred_element_type=f32
        )
        return carry

    lax.fori_loop(0, ch // LANES, two_heads, 0, unroll=2)


def scan_block(gates, sums, tail, state, index, table, rate, taps):
    ch = state.shape[1]
    wide = ch + 2 * STATE
    whole = lambda a: pl.BlockSpec(a.shape, lambda b: (0,) * a.ndim)
    others = (sums, tail, state, index, table, rate, taps)
    outs = (
        jax.ShapeDtypeStruct((BLOCK, ch), bf16),
        jax.ShapeDtypeStruct((STATE, ch), f32),
        jax.ShapeDtypeStruct((8, wide), f32),
    )
    return pl.pallas_call(
        scan_kernel,
        out_shape=outs,
        grid=(1,),
        in_specs=[pl.BlockSpec((BLOCK, ch), lambda b: (0, 0)), *map(whole, others)],
        out_specs=[whole(o) for o in outs],
        scratch_shapes=[
            pltpu.VMEM((BLOCK + 8, wide), f32),
            pltpu.VMEM((LANES, BLOCK), f32),
            pltpu.VMEM((LANES, BLOCK), f32),
        ],
        cost_estimate=pl.CostEstimate(
            flops=8 * BLOCK * BLOCK * ch,
            bytes_accessed=16 * BLOCK * ch,
            transcendentals=2 * BLOCK * BLOCK * ch // HEAD_DIM,
        ),
        name="scan_block",
    )(gates, *others)


def output_kernel(where, *refs, n, count):
    blocks = refs[: 2 * n * count]
    gain, weight_source, out, held, weight, sems, weight_sems = refs[2 * n * count :]
    ch = held.shape[1] // 2
    width = weight.shape[1]
    here = where[0]

    def fetch(act):
        for block in range(count):
            for side in range(2):
                place = here if side == 0 else n - 1 - here
                for k in range(n):
                    source = blocks[(block * 2 + side) * n + k]
                    start = source.shape[1] - ch

                    @pl.when(place == k)
                    def _():
                        act(
                            pltpu.make_async_copy(
                                source.at[:, start:],
                                held.at[pl.ds(block * BLOCK, BLOCK), pl.ds(side * ch, ch)],
                                sems.at[block, side],
                            )
                        )

    fetch(lambda copy: copy.start())
    tile = min(256, width)
    tiles = width // tile
    for k in range(tiles):
        columns = pl.ds(k * tile, tile)
        pltpu.make_async_copy(
            weight_source.at[:, columns], weight.at[:, columns], weight_sems.at[k]
        ).start()
    fetch(lambda copy: copy.wait())
    values = held[...].astype(f32)
    squares = jnp.sum(values * values, axis=1, keepdims=True)
    held[...] = (values * gain[...]).astype(bf16)

    def some_columns(at, carry):
        part = pl.ds(pl.multiple_of(at * tile, tile), tile)
        pltpu.make_async_copy(
            weight_source.at[:, part], weight.at[:, part], weight_sems.at[at]
        ).wait()
        out[:, part] = jnp.dot(
            held[...], weight[:, part], preferred_element_type=f32
        ).astype(bf16)
        return carry

    lax.fori_loop(0, tiles, some_columns, 0)
    out[:, width:] = jnp.broadcast_to(squares, (count * BLOCK, LANES)).astype(bf16)


def output_block(where, blocks, n, gain, weight, ch):
    count = len(blocks) // (2 * n)
    width = weight.shape[1]
    whole = lambda a: pl.BlockSpec(a.shape, lambda b, w: (0, 0))
    return pl.pallas_call(
        functools.partial(output_kernel, n=n, count=count),
        out_shape=jax.ShapeDtypeStruct((count * BLOCK, width + LANES), bf16),
        grid_spec=pltpu.PrefetchScalarGridSpec(
            num_scalar_prefetch=1,
            grid=(1,),
            in_specs=[
                *(pl.BlockSpec(memory_space=pl.ANY) for _ in blocks),
                whole(gain),
                pl.BlockSpec(memory_space=pl.ANY),
            ],
            out_specs=pl.BlockSpec((count * BLOCK, width + LANES), lambda b, w: (0, 0)),
            scratch_shapes=[
                pltpu.VMEM((count * BLOCK, 2 * ch), bf16),
                pltpu.VMEM(weight.shape, bf16),
                pltpu.SemaphoreType.DMA((count, 2)),
                pltpu.SemaphoreType.DMA((max(1, width // 256),)),
            ],
        ),
        cost_estimate=pl.CostEstimate(
            flops=4 * count * BLOCK * ch * width, bytes_accessed=4 * ch * width + 8 * count * BLOCK * ch, transcendentals=0
        ),
        name="output_block",
    )(where, *blocks, gain, weight)


def per_device(
    activations,
    token_adapter_index,
    gate_scanned_weight,
    state_vector_weight,
    time_step_weight,
    adapter_down_maps,
    adapter_up_maps,
    scanned_channel_taps,
    state_vector_taps,
    earlier_scanned_channels,
    earlier_state_vectors,
    head_step_bias,
    adapter_step_shift,
    head_decay_rate,
    starting_head_state,
    gated_norm_gain,
    output_projection_weight,
):
    n = lax.axis_size("seq")
    here = lax.axis_index("seq")
    shards = lax.axis_size("tensor")
    shard = lax.axis_index("tensor")
    core = shard % 2
    rows = activations.shape[0]
    tokens = rows * n
    depth = gate_scanned_weight.shape[0]
    heads_here = time_step_weight.shape[1]
    heads = heads_here // 2
    ch = heads * HEAD_DIM
    per_set = HEADS // HEAD_SETS
    size = tokens // shards
    assert per_set % heads == 0 and n % 2 == 0 and shards % 2 == 0 and size % BLOCK == 0
    blocks = tokens // BLOCK
    pairs_a = [(j, j ^ 1) for j in range(n)]
    pairs_b = [(j, ((j - 1) ^ 1) + 1) for j in range(1, n - 1)]
    swap = [(j, j ^ 1) for j in range(shards)]
    at_first = here == 0
    at_end = at_first | (here == n - 1)
    odd = here % 2
    as_int = lambda v: v.astype(jnp.int32)

    def own(array, start, count, axis):
        return lax.dynamic_slice_in_dim(array, start, count, axis)

    half = depth // 2
    index_rows = 16 * -(-rows // (16 * half))
    index_pad = jnp.pad(
        token_adapter_index.astype(bf16), (0, index_rows * half - rows)
    ).reshape(index_rows, half)

    def piece(dest):
        part = lax.dynamic_slice(activations, (0, dest * depth + core * half), (rows, half))
        return jnp.concatenate([part, index_pad], axis=0)

    pieces = [piece(here)]
    for k in range(1, n):
        pairs = [(j, (j + k) % n) for j in range(n)]
        pieces.append(lax.ppermute(piece((here + k) % n), "seq", pairs))

    def by_pair(array):
        split = array.reshape(array.shape[0] // 16, 16, 2, array.shape[2])
        return jnp.swapaxes(split, 1, 2)

    weight = by_pair(gate_scanned_weight)
    up = by_pair(adapter_up_maps)

    def small_of(end):
        first = (shard * heads_here + end * heads) // per_set * STATE
        io = own(state_vector_weight, first, STATE, 2).reshape(depth, 2 * STATE)
        steps = time_step_weight[:, end * heads : (end + 1) * heads]
        return jnp.concatenate([io, jnp.pad(steps, ((0, 0), (0, LANES - heads)))], axis=1)

    small = jnp.stack([small_of(0), small_of(1)])
    mine, weight, up, small = lax.optimization_barrier((jnp.stack(pieces), weight, up, small))
    other = lax.ppermute(mine, "tensor", swap)
    index = mine[:, rows:].reshape(n, -1)[:, :rows]
    index = jnp.concatenate(
        [lax.dynamic_index_in_dim(index, (here - b) % n, 0, False) for b in range(n)]
    ).astype(f32).reshape(blocks, 1, BLOCK)

    order = [as_int(core), as_int(1 - odd)] + [as_int((here - b) % n) for b in range(n)]
    order = jnp.stack(order)
    projected = ()
    versions = []
    for count in (n,):
        projected = project(
            order, mine, other, adapter_down_maps, weight, up, small, rows, ch, count, projected
        )
        versions.append(projected)

    end = jnp.where(at_first, 0, 1)
    first_head = end * heads
    first_ch = end * ch
    first_io = (shard * heads_here + first_head) // per_set * STATE
    taps = jnp.concatenate(
        [
            own(scanned_channel_taps, first_ch, ch, 1),
            own(state_vector_taps, first_io, STATE, 2).reshape(CONV, 2 * STATE),
        ],
        axis=1,
    )
    tail = jnp.concatenate(
        [
            own(earlier_scanned_channels, first_ch, ch, 1),
            own(earlier_state_vectors, first_io, STATE, 2).reshape(CONV - 1, 2 * STATE),
        ],
        axis=1,
    ).astype(f32)
    tail = jnp.pad(tail, ((8 - (CONV - 1), 0), (0, 0)))
    table = own(adapter_step_shift + head_step_bias, first_head, heads, 1)
    table = jnp.pad(table, ((0, LANES - ADAPTER_COUNT), (0, LANES - heads)))
    rate = jnp.pad(own(head_decay_rate, first_head, heads, 0), (0, LANES - heads))[None]
    state = own(starting_head_state, first_head, heads, 0).reshape(ch, STATE).T
    gain = gated_norm_gain[None]

    def made(step):
        return versions[min(step * BLOCK // rows, len(versions) - 1)]

    def turn(step):
        limit = made(step)[0].shape[1] // BLOCK
        to_last = jnp.clip(step - here, 0, limit - 1)
        to_first = jnp.clip(step - (n - 1 - here), 0, limit - 1)
        return jnp.where(odd == 0, to_last, to_first), jnp.where(odd == 0, to_first, to_last)

    def taken(array, step):
        shape = (1, BLOCK, array.shape[2])
        return tuple(
            lax.dynamic_slice(array, (side, at * BLOCK, 0), shape)[0]
            for side, at in enumerate(turn(step))
        )

    def added(a, b):
        return (a.astype(f32) + b.astype(f32)).astype(bf16)

    def onward(pair):
        from_a = lax.ppermute(pair[0], "seq", pairs_a)
        from_b = lax.ppermute(pair[1], "seq", pairs_b)
        return from_a, from_b

    def tied(*pairs):
        flat = lax.optimization_barrier(tuple(a for pair in pairs for a in pair))
        return [tuple(flat[k : k + 2]) for k in range(0, len(flat), 2)]

    sends = blocks + n - 2
    last_step = blocks + 2 * n - 3
    per = size // BLOCK
    chips = shards // 2
    chip = shard // 2
    groups = [2, 1, 1] if chips == 2 else [1] * shards
    group_ends = [sum(groups[: k + 1]) for k in range(len(groups))]
    sums = came = before = gated = None
    went, arrived, states, outs = {}, {}, [], []
    pending = None
    for step in range(last_step + 1):
        block = step - (n - 1)
        if step <= sends:
            go = taken(made(step)[0], step)
            if step > 1:
                sums, before = tied(sums, before)
            if step > 0:
                go = added(go[0], sums[1]), added(go[1], sums[0])
                came, sums = tied(came, sums)
            before = came
            if step < sends:
                sums = onward(go)
        else:
            (came,) = tied(came)
        if step < n:
            gate = taken(made(step)[1], step)
            if step > 0:
                gate = added(gate[0], came[1]), added(gate[1], came[0])
            onto = gate
            if step == n - 1 and sends > step:
                onto = gate
        if n <= step < sends:
            where = jnp.stack([as_int(at_end), *map(as_int, turn(step))])
            onto = gate = merge(where, made(step)[1], came, gated)
        elif step == sends:
            gate = (None, added(taken(made(step)[1], step)[1], came[0][:, :ch]))
        if step >= max(n, sends):
            onto = came[1][:, -ch:], came[0][:, -ch:]
            if gated is not None:
                onto = jnp.where(at_end, gated, onto[0]), onto[1]
        came = onward(onto)
        arrived[step] = came
        if block >= 0:
            if gated is not None:
                went[block - 1] = onto[0]
            gated = None
        if 0 <= block < blocks:
            gated, state, tail = scan_block(
                gate[1], go[1], tail, state, index[block], table, rate, taps
            )
            if pending is not None and block + 1 < blocks:
                state, outs[pending] = lax.optimization_barrier((state, outs[pending]))
                pending = None
            if (block + 1) * BLOCK % rows == 0:
                states.append(state.astype(bf16).T)
        if pending is not None and sends < step < last_step:
            came, (outs[pending], _) = tied(came, (outs[pending], state))
            pending = None
        done = step - (2 * n - 2)
        if done >= 0 and (done + 1) % per == 0 and (done + 1) // per in group_ends:
            needed = []
            for b in range(done + 1 - per * groups[len(outs)], done + 1):
                for _ in range(2):
                    needed.append(went[b])
                    needed.extend(arrived[b + n - 1 + k][1 - k % 2] for k in range(1, n))
            pending = len(outs)
            outs.append(
                output_block(as_int(here)[None], needed, n, gain, output_projection_weight, ch)
            )

    landed = [jnp.where(at_first, states[0], states[n - 1])]
    for k in range(1, n):
        leaving = jnp.where(at_first, states[k], states[n - 1 - k])
        landed.append(lax.ppermute(leaving, "seq", [(0, k), (n - 1, n - 1 - k)]))

    if chips == 2:
        first, *rest = outs
        keep = own(first, core * size, size, 0)
        give = own(first, (1 - core) * size, size, 0)
        back = lax.ppermute(give, "tensor", swap)
        both_first = added(keep, back)
        give = jnp.where(core == 0, *rest[::-1])
        back = lax.ppermute(give, "tensor", swap)
        both_last = added(jnp.where(core == 0, *rest), back)
        total = jnp.where(chip == 0, both_first, both_last).astype(f32)
        both = give = jnp.where(chip == 0, both_last, both_first)
        came = lax.ppermute(give, "tensor", [(j, j ^ 2) for j in range(shards)])
        total = total + came.astype(f32)
    else:
        halves = []
        for k in range(chips):
            keep = jnp.where(core == 0, outs[2 * k], outs[2 * k + 1])
            give = jnp.where(core == 0, outs[2 * k + 1], outs[2 * k])
            halves.append(added(keep, lax.ppermute(give, "tensor", swap)))
        both = halves[-1]
        halves = jnp.stack(halves)
        total = lax.dynamic_index_in_dim(halves, chip, 0, False).astype(f32)
        for k in range(1, chips):
            pairs = [(j, (j + 2 * k) % shards) for j in range(shards)]
            give = lax.dynamic_index_in_dim(halves, (chip + k) % chips, 0, False)
            total = total + lax.ppermute(give, "tensor", pairs).astype(f32)
    *landed, _ = lax.optimization_barrier((*landed, both))
    landed = jnp.stack(landed)
    finish = jnp.concatenate(
        [lax.dynamic_index_in_dim(landed, which, 0, False) for which in (here, n - 1 - here)], axis=0
    ).astype(f32).reshape(heads_here, HEAD_DIM, STATE)
    width = output_projection_weight.shape[1]
    scale = lax.rsqrt(total[:, width : width + 1] / (HEADS * HEAD_DIM) + 1e-05)
    mixed = (total[:, :width] * scale).astype(bf16)
    return (mixed, finish[None])


def solution(mesh):
    return jax.shard_map(
        per_device,
        mesh=mesh,
        in_specs=(
            P(("groups", "seq"), None),
            P(("groups", "seq")),
            P("seq", None, "tensor"),
            P("seq", None, None),
            P("seq", "tensor"),
            P("seq", None),
            P(None, None, "tensor"),
            P(None, "tensor"),
            P(),
            P("groups", "tensor"),
            P("groups", None, None),
            P("tensor"),
            P(None, "tensor"),
            P("tensor"),
            P(("groups", "tensor"), None, None),
            P("tensor"),
            P("tensor", "seq"),
        ),
        out_specs=(P(("groups", "tensor"), "seq"), P(("groups", "seq"), "tensor", None, None)),
        check_vma=False,
    )
```

```python
import functools
import jax
import jax.numpy as jnp
from jax import lax
from jax.experimental import pallas as pl
from jax.experimental.pallas import tpu as pltpu
from jax.sharding import PartitionSpec as P


HEADS = 128
HEAD_DIM = 64
STATE = 128
HEAD_SETS = 8
ADAPTER_COUNT = 16
ADAPTER_RANK = 16
CONV = 4
BLOCK = 128
LANES = 128


bf16 = jnp.bfloat16
f32 = jnp.float32


def silu(v):
    return v / (1.0 + jnp.exp(-v))


def project_kernel(where, *refs, rows, first, count):
    mine, other, down, weight, up, small, *refs = refs
    earlier, (mixed_out, gate_out, values) = refs[:-3], refs[-3:]
    half = mine.shape[2]
    begin = first * rows
    depth = 2 * half
    core = where[0]
    step = pl.program_id(0)
    tile = gate_out.shape[2]
    per_end = pl.num_programs(0) // 2
    ch = mixed_out.shape[2] - small.shape[2]

    def plane(end):
        return jnp.where(where[1] == 1, 1 - end, end)

    @pl.when(step == 0)
    def _():
        rank = down.shape[1]
        span = min(half, rows)
        owner = lax.broadcasted_iota(jnp.int32, (rank, span), 0) // ADAPTER_RANK
        near = pl.ds(pl.multiple_of(core * half, half), half)
        far = pl.ds(pl.multiple_of((1 - core) * half, half), half)
        masks = []
        if earlier:
            mixed_out[:, :begin, :] = earlier[0][...]
        for b in range(count):
            source = where[2 + first + b] if count > 1 else 0
            values[b * rows : (b + 1) * rows, near] = mine[source, :rows, :]
            values[b * rows : (b + 1) * rows, far] = other[source, :rows, :]
            for part in range(rows // span):
                index = mine[source, rows : rows + 16, :span].astype(f32)
                index = index[part : part + 1].astype(jnp.int32)
                masks.append((owner == index).astype(f32).T)
        mask = masks[0] if len(masks) == 1 else jnp.concatenate(masks, axis=0)
        full = jnp.dot(values[:, :depth], down[...], preferred_element_type=f32)
        values[:, depth:] = jnp.where(mask > 0.5, full, 0.0).astype(bf16)
        for end in range(2):
            mixed_out[plane(end), begin:, ch:] = jnp.dot(
                values[:, :depth], small[end], preferred_element_type=f32
            ).astype(bf16)

    end = step // per_end
    dst = pl.ds(pl.multiple_of((step - end * per_end) * tile, tile), tile)
    if earlier:
        gate_out[0, :begin, :] = earlier[1][0]

    def columns(part, pair):
        total = jnp.dot(
            values[part, :depth],
            weight[:, pair].reshape(depth, tile),
            preferred_element_type=f32,
        )
        return (
            total
            + jnp.dot(
                values[part, depth:],
                up[:, pair].reshape(values.shape[1] - depth, tile),
                preferred_element_type=f32,
            )
        ).astype(bf16)

    def some_rows(at, carry):
        part = pl.ds(pl.multiple_of(at * rows, rows), rows)
        onto = pl.ds(pl.multiple_of(begin + at * rows, rows), rows)
        gate_out[0, onto, :] = columns(part, 0)
        mixed_out[plane(end), onto, dst] = columns(part, 1)
        return carry

    lax.fori_loop(0, count, some_rows, 0)


def project(where, mine, other, down, weight, up, small, rows, ch, count, earlier=()):
    height, half = mine.shape[1:]
    first = earlier[0].shape[1] // rows if earlier else 0
    n = first + count
    tile = min(512, ch)
    per_end = ch // tile
    whole = lambda a: pl.BlockSpec(a.shape, lambda b, w: (0,) * a.ndim)
    picked = lambda a: (
        whole(a)
        if count > 1
        else pl.BlockSpec((1, height, half), lambda b, w: (w[2 + first], 0, 0))
    )
    striped = lambda a: pl.BlockSpec((*a.shape[:3], tile), lambda b, w: (0, 0, 0, b))
    gate_spot = lambda r: pl.BlockSpec(
        (1, r, tile),
        lambda b, w: (jnp.where(w[1] == 1, 1 - b // per_end, b // per_end), 0, b % per_end),
    )
    wide = ch + small.shape[2]
    full = 2 * half + down.shape[1]
    return pl.pallas_call(
        functools.partial(project_kernel, rows=rows, first=first, count=count),
        out_shape=(
            jax.ShapeDtypeStruct((2, n * rows, wide), bf16),
            jax.ShapeDtypeStruct((2, n * rows, ch), bf16),
        ),
        grid_spec=pltpu.PrefetchScalarGridSpec(
            num_scalar_prefetch=1,
            grid=(2 * per_end,),
            in_specs=[
                picked(mine), picked(other), whole(down), striped(weight), striped(up), whole(small),
                *((whole(earlier[0]), gate_spot(first * rows)) if earlier else ()),
            ],
            out_specs=[
                pl.BlockSpec((2, n * rows, wide), lambda b, w: (0, 0, 0)),
                gate_spot(n * rows),
            ],
            scratch_shapes=[pltpu.VMEM((count * rows, full), bf16)],
        ),
        cost_estimate=pl.CostEstimate(
            flops=4 * count * rows * full * (ch + wide),
            bytes_accessed=2 * weight.size + 4 * n * rows * (ch + wide),
            transcendentals=0,
        ),
        name="project",
    )(where, mine, other, down, weight, up, small, *earlier)


def merge_kernel(where, gate_a, gate_b, came_a, came_b, gated, go_a, go_b, *, passing):
    ch = gated.shape[1]
    go_a[:, :ch] = (gate_a[0].astype(f32) + came_b[:, :ch].astype(f32)).astype(bf16)
    go_b[:, :ch] = (gate_b[0].astype(f32) + came_a[:, :ch].astype(f32)).astype(bf16)
    own = gated[...]
    if passing:
        own = jnp.where(where[0] == 1, own.astype(f32), came_b[:, ch:].astype(f32)).astype(bf16)
        go_b[:, ch:] = came_a[:, ch:]
    else:
        go_b[:, ch:] = own
    go_a[:, ch:] = own


def merge(where, gates, came, gated):
    ch = gated.shape[1]
    passing = came[0].shape[1] > ch
    whole = lambda a: pl.BlockSpec(a.shape, lambda b, w: (0,) * a.ndim)
    out = jax.ShapeDtypeStruct((BLOCK, 2 * ch), bf16)
    return pl.pallas_call(
        functools.partial(merge_kernel, passing=passing),
        out_shape=(out, out),
        grid_spec=pltpu.PrefetchScalarGridSpec(
            num_scalar_prefetch=1,
            grid=(1,),
            in_specs=[
                pl.BlockSpec((1, BLOCK, ch), lambda b, w: (0, w[1], 0)),
                pl.BlockSpec((1, BLOCK, ch), lambda b, w: (1, w[2], 0)),
                whole(came[0]), whole(came[1]), whole(gated),
            ],
            out_specs=[whole(out), whole(out)],
        ),
        cost_estimate=pl.CostEstimate(
            flops=4 * BLOCK * ch, bytes_accessed=22 * BLOCK * ch, transcendentals=0
        ),
        name="merge",
    )(where, gates, gates, *came, gated)


def scan_kernel(
    gates, sums, tail, state, index, table, rate, taps,
    gated_out, state_out, tail_out, rows, cum_rows, step_rows,
):
    ch = state.shape[1]
    wide = ch + 2 * STATE
    rows[0:8, :] = tail[...]
    rows[8 : 8 + BLOCK, :] = sums[:, :wide].astype(f32)
    tail_out[...] = rows[BLOCK : BLOCK + 8, :]

    def conv(at):
        total = jnp.zeros((BLOCK, LANES), f32)
        for k in range(CONV):
            begin = 8 - (CONV - 1) + k
            total = total + taps[k : k + 1, at] * rows[begin : begin + BLOCK, at]
        return silu(total).astype(bf16)

    input_vec = conv(pl.ds(ch, STATE))
    output_vec = conv(pl.ds(ch + STATE, STATE))
    row = lax.broadcasted_iota(jnp.int32, (BLOCK, BLOCK), 0)
    col = lax.broadcasted_iota(jnp.int32, (BLOCK, BLOCK), 1)
    causal = row >= col
    chosen = (row == index[...].astype(jnp.int32)).astype(f32).T
    shift = jnp.dot(
        chosen, table[...], precision=lax.Precision.HIGHEST, preferred_element_type=f32
    )
    raw = sums[:, wide:].astype(f32) + shift
    step = jnp.maximum(raw, 0.0) + jnp.log1p(jnp.exp(-jnp.abs(raw)))
    cum = jnp.dot(
        causal.astype(f32),
        -rate[...] * step,
        precision=lax.Precision.HIGHEST,
        preferred_element_type=f32,
    )
    cum_rows[...] = cum.T
    step_rows[...] = step.T
    scores = lax.dot_general(
        output_vec, input_vec, (((1,), (1,)), ((), ())), preferred_element_type=f32
    )
    scores = jnp.where(causal, scores, 0.0)
    first_half = col < HEAD_DIM
    input_t = input_vec.T

    def two_heads(pair, carry):
        lanes = pl.ds(pl.multiple_of(pair * LANES, LANES), LANES)
        x = conv(lanes)
        held = state[:, lanes]
        high = held.astype(bf16)
        low = (held - high.astype(f32)).astype(bf16)
        inter = jnp.dot(output_vec, high, preferred_element_type=f32) + jnp.dot(
            output_vec, low, preferred_element_type=f32
        )
        turned = LANES - 2 * pair
        cum_here = pltpu.roll(cum, turned, 1)
        step_here = pltpu.roll(step, turned, 1)
        cums, steps, outs = [], [], []
        for h in range(2):
            row_of = pl.ds(2 * pair + h, 1)
            cum_i = jnp.broadcast_to(cum_here[:, h : h + 1], (BLOCK, BLOCK))
            weight = jnp.exp(jnp.minimum(cum_i - cum_rows[row_of, :], 0.0))
            mixing = (scores * weight * step_rows[row_of, :]).astype(bf16)
            outs.append(jnp.dot(mixing, x, preferred_element_type=f32))
            cums.append(cum_i)
            steps.append(jnp.broadcast_to(step_here[:, h : h + 1], (BLOCK, BLOCK)))
        cum_i = jnp.where(first_half, cums[0], cums[1])
        total = cum_i[BLOCK - 1 :, :]
        out = jnp.where(first_half, outs[0], outs[1]) + jnp.exp(cum_i) * inter
        gated_out[:, lanes] = (out * silu(gates[:, lanes].astype(f32))).astype(bf16)
        factor = jnp.where(first_half, steps[0], steps[1]) * jnp.exp(total - cum_i)
        scaled = (x.astype(f32) * factor).astype(bf16)
        state_out[:, lanes] = jnp.exp(total) * held + jnp.dot(
            input_t, scaled, preferred_element_type=f32
        )
        return carry

    lax.fori_loop(0, ch // LANES, two_heads, 0, unroll=2)


def scan_block(gates, sums, tail, state, index, table, rate, taps):
    ch = state.shape[1]
    wide = ch + 2 * STATE
    whole = lambda a: pl.BlockSpec(a.shape, lambda b: (0,) * a.ndim)
    others = (sums, tail, state, index, table, rate, taps)
    outs = (
        jax.ShapeDtypeStruct((BLOCK, ch), bf16),
        jax.ShapeDtypeStruct((STATE, ch), f32),
        jax.ShapeDtypeStruct((8, wide), f32),
    )
    return pl.pallas_call(
        scan_kernel,
        out_shape=outs,
        grid=(1,),
        in_specs=[pl.BlockSpec((BLOCK, ch), lambda b: (0, 0)), *map(whole, others)],
        out_specs=[whole(o) for o in outs],
        scratch_shapes=[
            pltpu.VMEM((BLOCK + 8, wide), f32),
            pltpu.VMEM((LANES, BLOCK), f32),
            pltpu.VMEM((LANES, BLOCK), f32),
        ],
        cost_estimate=pl.CostEstimate(
            flops=8 * BLOCK * BLOCK * ch,
            bytes_accessed=16 * BLOCK * ch,
            transcendentals=2 * BLOCK * BLOCK * ch // HEAD_DIM,
        ),
        name="scan_block",
    )(gates, *others)


def output_kernel(where, *refs, n, count, paired):
    blocks = refs[: 2 * n * count]
    gain, weight_source, *refs = refs[2 * n * count :]
    prior, (out, *handed), (held, weight, sems, weight_sems) = (
        (refs[0], refs[1:3], refs[3:]) if paired else (None, refs[:1], refs[1:])
    )
    ch = held.shape[1] // 2
    width = weight.shape[1]
    here = where[0]

    def fetch(act):
        for block in range(count):
            for side in range(2):
                place = here if side == 0 else n - 1 - here
                for k in range(n):
                    source = blocks[(block * 2 + side) * n + k]
                    start = source.shape[1] - ch

                    @pl.when(place == k)
                    def _():
                        act(
                            pltpu.make_async_copy(
                                source.at[:, start:],
                                held.at[pl.ds(block * BLOCK, BLOCK), pl.ds(side * ch, ch)],
                                sems.at[block, side],
                            )
                        )

    fetch(lambda copy: copy.start())
    tile = min(256, width)
    tiles = width // tile
    for k in range(tiles):
        columns = pl.ds(k * tile, tile)
        pltpu.make_async_copy(
            weight_source.at[:, columns], weight.at[:, columns], weight_sems.at[k]
        ).start()
    fetch(lambda copy: copy.wait())

    def put(columns, result):
        if paired:
            mine = where[1] == 0
            before = prior[:, columns].astype(f32)
            out[:, columns] = jnp.where(mine, before, result).astype(bf16)
            handed[0][:, columns] = jnp.where(mine, result, before).astype(bf16)
        else:
            out[:, columns] = result.astype(bf16)

    sums = []
    for block in range(count):
        part = slice(block * BLOCK, (block + 1) * BLOCK)

        def some_channels(at, total):
            lanes = pl.ds(pl.multiple_of(at * LANES, LANES), LANES)
            values = held[part, lanes].astype(f32)
            held[part, lanes] = (values * gain[:, lanes]).astype(bf16)
            return total + values * values

        total = lax.fori_loop(
            0, 2 * ch // LANES, some_channels, jnp.zeros((BLOCK, LANES), f32), unroll=2
        )
        sums.append(jnp.sum(total, axis=1, keepdims=True))
    squares = jnp.concatenate(sums, axis=0)

    def some_columns(at, carry):
        part = pl.ds(pl.multiple_of(at * tile, tile), tile)
        pltpu.make_async_copy(
            weight_source.at[:, part], weight.at[:, part], weight_sems.at[at]
        ).wait()
        put(part, jnp.dot(held[...], weight[:, part], preferred_element_type=f32))
        return carry

    lax.fori_loop(0, tiles, some_columns, 0)
    put(slice(width, width + LANES), jnp.broadcast_to(squares, (count * BLOCK, LANES)))


def output_block(where, blocks, n, gain, weight, ch, prior=None):
    count = len(blocks) // (2 * n)
    width = weight.shape[1]
    whole = lambda a: pl.BlockSpec(a.shape, lambda b, w: (0, 0))
    result = jax.ShapeDtypeStruct((count * BLOCK, width + LANES), bf16)
    extra = () if prior is None else (prior,)
    return pl.pallas_call(
        functools.partial(output_kernel, n=n, count=count, paired=prior is not None),
        out_shape=result if prior is None else (result, result),
        grid_spec=pltpu.PrefetchScalarGridSpec(
            num_scalar_prefetch=1,
            grid=(1,),
            in_specs=[
                *(pl.BlockSpec(memory_space=pl.ANY) for _ in blocks),
                whole(gain),
                pl.BlockSpec(memory_space=pl.ANY),
                *map(whole, extra),
            ],
            out_specs=whole(result) if prior is None else [whole(result)] * 2,
            scratch_shapes=[
                pltpu.VMEM((count * BLOCK, 2 * ch), bf16),
                pltpu.VMEM(weight.shape, bf16),
                pltpu.SemaphoreType.DMA((count, 2)),
                pltpu.SemaphoreType.DMA((max(1, width // 256),)),
            ],
        ),
        cost_estimate=pl.CostEstimate(
            flops=4 * count * BLOCK * ch * width, bytes_accessed=4 * ch * width + 8 * count * BLOCK * ch, transcendentals=0
        ),
        name="output_block",
    )(where, *blocks, gain, weight, *extra)


def per_device(
    activations,
    token_adapter_index,
    gate_scanned_weight,
    state_vector_weight,
    time_step_weight,
    adapter_down_maps,
    adapter_up_maps,
    scanned_channel_taps,
    state_vector_taps,
    earlier_scanned_channels,
    earlier_state_vectors,
    head_step_bias,
    adapter_step_shift,
    head_decay_rate,
    starting_head_state,
    gated_norm_gain,
    output_projection_weight,
):
    n = lax.axis_size("seq")
    here = lax.axis_index("seq")
    shards = lax.axis_size("tensor")
    shard = lax.axis_index("tensor")
    core = shard % 2
    rows = activations.shape[0]
    tokens = rows * n
    depth = gate_scanned_weight.shape[0]
    heads_here = time_step_weight.shape[1]
    heads = heads_here // 2
    ch = heads * HEAD_DIM
    per_set = HEADS // HEAD_SETS
    size = tokens // shards
    assert per_set % heads == 0 and n % 2 == 0 and shards % 2 == 0 and size % BLOCK == 0
    blocks = tokens // BLOCK
    pairs_a = [(j, j ^ 1) for j in range(n)]
    pairs_b = [(j, ((j - 1) ^ 1) + 1) for j in range(1, n - 1)]
    swap = [(j, j ^ 1) for j in range(shards)]
    at_first = here == 0
    at_end = at_first | (here == n - 1)
    odd = here % 2
    as_int = lambda v: v.astype(jnp.int32)

    def own(array, start, count, axis):
        return lax.dynamic_slice_in_dim(array, start, count, axis)

    half = depth // 2
    index_rows = 16 * -(-rows // (16 * half))
    index_pad = jnp.pad(
        token_adapter_index.astype(bf16), (0, index_rows * half - rows)
    ).reshape(index_rows, half)

    def piece(dest):
        part = lax.dynamic_slice(activations, (0, dest * depth + core * half), (rows, half))
        return jnp.concatenate([part, index_pad], axis=0)

    pieces = [piece(here)]
    for k in range(1, n):
        pairs = [(j, (j + k) % n) for j in range(n)]
        pieces.append(lax.ppermute(piece((here + k) % n), "seq", pairs))

    def by_pair(array):
        split = array.reshape(array.shape[0] // 16, 16, 2, array.shape[2])
        return jnp.swapaxes(split, 1, 2)

    weight = by_pair(gate_scanned_weight)
    up = by_pair(adapter_up_maps)

    def small_of(end):
        first = (shard * heads_here + end * heads) // per_set * STATE
        io = own(state_vector_weight, first, STATE, 2).reshape(depth, 2 * STATE)
        steps = time_step_weight[:, end * heads : (end + 1) * heads]
        return jnp.concatenate([io, jnp.pad(steps, ((0, 0), (0, LANES - heads)))], axis=1)

    small = jnp.stack([small_of(0), small_of(1)])
    mine, weight, up, small = lax.optimization_barrier((jnp.stack(pieces), weight, up, small))
    other = lax.ppermute(mine, "tensor", swap)
    index = mine[:, rows:].reshape(n, -1)[:, :rows]
    index = jnp.concatenate(
        [lax.dynamic_index_in_dim(index, (here - b) % n, 0, False) for b in range(n)]
    ).astype(f32).reshape(blocks, 1, BLOCK)

    order = [as_int(core), as_int(1 - odd)] + [as_int((here - b) % n) for b in range(n)]
    order = jnp.stack(order)
    projected = ()
    versions = []
    for count in (n,):
        projected = project(
            order, mine, other, adapter_down_maps, weight, up, small, rows, ch, count, projected
        )
        versions.append(projected)

    end = jnp.where(at_first, 0, 1)
    first_head = end * heads
    first_ch = end * ch
    first_io = (shard * heads_here + first_head) // per_set * STATE
    taps = jnp.concatenate(
        [
            own(scanned_channel_taps, first_ch, ch, 1),
            own(state_vector_taps, first_io, STATE, 2).reshape(CONV, 2 * STATE),
        ],
        axis=1,
    )
    tail = jnp.concatenate(
        [
            own(earlier_scanned_channels, first_ch, ch, 1),
            own(earlier_state_vectors, first_io, STATE, 2).reshape(CONV - 1, 2 * STATE),
        ],
        axis=1,
    ).astype(f32)
    tail = jnp.pad(tail, ((8 - (CONV - 1), 0), (0, 0)))
    table = own(adapter_step_shift + head_step_bias, first_head, heads, 1)
    table = jnp.pad(table, ((0, LANES - ADAPTER_COUNT), (0, LANES - heads)))
    rate = jnp.pad(own(head_decay_rate, first_head, heads, 0), (0, LANES - heads))[None]
    state = own(starting_head_state, first_head, heads, 0).reshape(ch, STATE).T
    gain = gated_norm_gain[None]

    def made(step):
        return versions[min(step * BLOCK // rows, len(versions) - 1)]

    def turn(step):
        limit = made(step)[0].shape[1] // BLOCK
        to_last = jnp.clip(step - here, 0, limit - 1)
        to_first = jnp.clip(step - (n - 1 - here), 0, limit - 1)
        return jnp.where(odd == 0, to_last, to_first), jnp.where(odd == 0, to_first, to_last)

    def taken(array, step):
        shape = (1, BLOCK, array.shape[2])
        return tuple(
            lax.dynamic_slice(array, (side, at * BLOCK, 0), shape)[0]
            for side, at in enumerate(turn(step))
        )

    def added(a, b):
        return (a.astype(f32) + b.astype(f32)).astype(bf16)

    def onward(pair):
        from_a = lax.ppermute(pair[0], "seq", pairs_a)
        from_b = lax.ppermute(pair[1], "seq", pairs_b)
        return from_a, from_b

    def tied(*pairs):
        flat = lax.optimization_barrier(tuple(a for pair in pairs for a in pair))
        return [tuple(flat[k : k + 2]) for k in range(0, len(flat), 2)]

    sends = blocks + n - 2
    last_step = blocks + 2 * n - 3
    per = size // BLOCK
    chips = shards // 2
    chip = shard // 2
    spot = jnp.stack([as_int(here), as_int(core)])
    groups = [2, 1, 1] if chips == 2 else [1] * shards
    group_ends = [sum(groups[: k + 1]) for k in range(len(groups))]
    sums = came = before = gated = None
    went, arrived, states, outs = {}, {}, [], []
    pending = None
    for step in range(last_step + 1):
        block = step - (n - 1)
        if step <= sends:
            go = taken(made(step)[0], step)
            if step > 1:
                sums, before = tied(sums, before)
            if step > 0:
                go = added(go[0], sums[1]), added(go[1], sums[0])
                came, sums = tied(came, sums)
            before = came
            if step < sends:
                sums = onward(go)
        else:
            (came,) = tied(came)
        if step < n:
            gate = taken(made(step)[1], step)
            if step > 0:
                gate = added(gate[0], came[1]), added(gate[1], came[0])
            onto = gate
            if step == n - 1 and sends > step:
                onto = gate
        if n <= step < sends:
            where = jnp.stack([as_int(at_end), *map(as_int, turn(step))])
            onto = gate = merge(where, made(step)[1], came, gated)
        elif step == sends:
            gate = (None, added(taken(made(step)[1], step)[1], came[0][:, :ch]))
        if step >= max(n, sends):
            onto = came[1][:, -ch:], came[0][:, -ch:]
            if gated is not None:
                onto = jnp.where(at_end, gated, onto[0]), onto[1]
        came = onward(onto)
        arrived[step] = came
        if block >= 0:
            if gated is not None:
                went[block - 1] = onto[0]
            gated = None
        if 0 <= block < blocks:
            gated, state, tail = scan_block(
                gate[1], go[1], tail, state, index[block], table, rate, taps
            )
            if pending is not None and block + 1 < blocks:
                state, outs[pending] = lax.optimization_barrier((state, outs[pending]))
                pending = None
            if (block + 1) * BLOCK % rows == 0:
                states.append(state.astype(bf16).T)
        if pending is not None and sends < step < last_step:
            came, (outs[pending], _) = tied(came, (outs[pending], state))
            pending = None
        done = step - (2 * n - 2)
        if done >= 0 and (done + 1) % per == 0 and (done + 1) // per in group_ends:
            needed = []
            for b in range(done + 1 - per * groups[len(outs)], done + 1):
                for _ in range(2):
                    needed.append(went[b])
                    needed.extend(arrived[b + n - 1 + k][1 - k % 2] for k in range(1, n))
            pending = len(outs)
            prior = outs[-1] if chips == 2 and pending == len(groups) - 1 else None
            outs.append(
                output_block(
                    spot, needed, n, gain, output_projection_weight, ch, prior
                )
            )

    landed = [jnp.where(at_first, states[0], states[n - 1])]
    for k in range(1, n):
        leaving = jnp.where(at_first, states[k], states[n - 1 - k])
        landed.append(lax.ppermute(leaving, "seq", [(0, k), (n - 1, n - 1 - k)]))

    if chips == 2:
        first, _, (keep_last, give_last) = outs
        keep = own(first, core * size, size, 0)
        give = own(first, (1 - core) * size, size, 0)
        back = lax.ppermute(give, "tensor", swap)
        both_first = added(keep, back)
        back = lax.ppermute(give_last, "tensor", swap)
        both_last = added(keep_last, back)
        total = jnp.where(chip == 0, both_first, both_last).astype(f32)
        both = give = jnp.where(chip == 0, both_last, both_first)
        came = lax.ppermute(give, "tensor", [(j, j ^ 2) for j in range(shards)])
        total = total + came.astype(f32)
    else:
        halves = []
        for k in range(chips):
            keep = jnp.where(core == 0, outs[2 * k], outs[2 * k + 1])
            give = jnp.where(core == 0, outs[2 * k + 1], outs[2 * k])
            halves.append(added(keep, lax.ppermute(give, "tensor", swap)))
        both = halves[-1]
        halves = jnp.stack(halves)
        total = lax.dynamic_index_in_dim(halves, chip, 0, False).astype(f32)
        for k in range(1, chips):
            pairs = [(j, (j + 2 * k) % shards) for j in range(shards)]
            give = lax.dynamic_index_in_dim(halves, (chip + k) % chips, 0, False)
            total = total + lax.ppermute(give, "tensor", pairs).astype(f32)
    *landed, _ = lax.optimization_barrier((*landed, both))
    landed = jnp.stack(landed)
    finish = jnp.concatenate(
        [lax.dynamic_index_in_dim(landed, which, 0, False) for which in (here, n - 1 - here)], axis=0
    ).astype(f32).reshape(heads_here, HEAD_DIM, STATE)
    width = output_projection_weight.shape[1]
    scale = lax.rsqrt(total[:, width : width + 1] / (HEADS * HEAD_DIM) + 1e-05)
    mixed = (total[:, :width] * scale).astype(bf16)
    return (mixed, finish[None])


def solution(mesh):
    return jax.shard_map(
        per_device,
        mesh=mesh,
        in_specs=(
            P(("groups", "seq"), None),
            P(("groups", "seq")),
            P("seq", None, "tensor"),
            P("seq", None, None),
            P("seq", "tensor"),
            P("seq", None),
            P(None, None, "tensor"),
            P(None, "tensor"),
            P(),
            P("groups", "tensor"),
            P("groups", None, None),
            P("tensor"),
            P(None, "tensor"),
            P("tensor"),
            P(("groups", "tensor"), None, None),
            P("tensor"),
            P("tensor", "seq"),
        ),
        out_specs=(P(("groups", "tensor"), "seq"), P(("groups", "seq"), "tensor", None, None)),
        check_vma=False,
    )
```

```python
import functools
import jax
import jax.numpy as jnp
from jax import lax
from jax.experimental import pallas as pl
from jax.experimental.pallas import tpu as pltpu
from jax.sharding import PartitionSpec as P


HEADS = 128
HEAD_DIM = 64
STATE = 128
HEAD_SETS = 8
ADAPTER_COUNT = 16
ADAPTER_RANK = 16
CONV = 4
BLOCK = 128
LANES = 128


bf16 = jnp.bfloat16
f32 = jnp.float32


def silu(v):
    return v / (1.0 + jnp.exp(-v))


def project_kernel(where, *refs, rows, first, count):
    mine, other, down, weight, up, small, *refs = refs
    earlier, (mixed_out, gate_out, values) = refs[:-3], refs[-3:]
    half = mine.shape[2]
    begin = first * rows
    depth = 2 * half
    core = where[0]
    step = pl.program_id(0)
    tile = gate_out.shape[2]
    per_end = pl.num_programs(0) // 2
    ch = mixed_out.shape[2] - small.shape[2]

    def plane(end):
        return jnp.where(where[1] == 1, 1 - end, end)

    @pl.when(step == 0)
    def _():
        rank = down.shape[1]
        span = min(half, rows)
        owner = lax.broadcasted_iota(jnp.int32, (rank, span), 0) // ADAPTER_RANK
        near = pl.ds(pl.multiple_of(core * half, half), half)
        far = pl.ds(pl.multiple_of((1 - core) * half, half), half)
        masks = []
        if earlier:
            mixed_out[:, :begin, :] = earlier[0][...]
        for b in range(count):
            source = where[2 + first + b] if count > 1 else 0
            values[b * rows : (b + 1) * rows, near] = mine[source, :rows, :]
            values[b * rows : (b + 1) * rows, far] = other[source, :rows, :]
            for part in range(rows // span):
                index = mine[source, rows : rows + 16, :span].astype(f32)
                index = index[part : part + 1].astype(jnp.int32)
                masks.append((owner == index).astype(f32).T)
        mask = masks[0] if len(masks) == 1 else jnp.concatenate(masks, axis=0)
        full = jnp.dot(values[:, :depth], down[...], preferred_element_type=f32)
        values[:, depth:] = jnp.where(mask > 0.5, full, 0.0).astype(bf16)
        for end in range(2):
            mixed_out[plane(end), begin:, ch:] = jnp.dot(
                values[:, :depth], small[end], preferred_element_type=f32
            ).astype(bf16)

    end = step // per_end
    dst = pl.ds(pl.multiple_of((step - end * per_end) * tile, tile), tile)
    if earlier:
        gate_out[0, :begin, :] = earlier[1][0]

    def columns(part, pair):
        total = jnp.dot(
            values[part, :depth],
            weight[:, pair].reshape(depth, tile),
            preferred_element_type=f32,
        )
        return (
            total
            + jnp.dot(
                values[part, depth:],
                up[:, pair].reshape(values.shape[1] - depth, tile),
                preferred_element_type=f32,
            )
        ).astype(bf16)

    def some_rows(at, carry):
        part = pl.ds(pl.multiple_of(at * rows, rows), rows)
        onto = pl.ds(pl.multiple_of(begin + at * rows, rows), rows)
        gate_out[0, onto, :] = columns(part, 0)
        mixed_out[plane(end), onto, dst] = columns(part, 1)
        return carry

    lax.fori_loop(0, count, some_rows, 0)


def project(where, mine, other, down, weight, up, small, rows, ch, count, earlier=()):
    height, half = mine.shape[1:]
    first = earlier[0].shape[1] // rows if earlier else 0
    n = first + count
    tile = min(512, ch)
    per_end = ch // tile
    whole = lambda a: pl.BlockSpec(a.shape, lambda b, w: (0,) * a.ndim)
    picked = lambda a: (
        whole(a)
        if count > 1
        else pl.BlockSpec((1, height, half), lambda b, w: (w[2 + first], 0, 0))
    )
    striped = lambda a: pl.BlockSpec((*a.shape[:3], tile), lambda b, w: (0, 0, 0, b))
    gate_spot = lambda r: pl.BlockSpec(
        (1, r, tile),
        lambda b, w: (jnp.where(w[1] == 1, 1 - b // per_end, b // per_end), 0, b % per_end),
    )
    wide = ch + small.shape[2]
    full = 2 * half + down.shape[1]
    return pl.pallas_call(
        functools.partial(project_kernel, rows=rows, first=first, count=count),
        out_shape=(
            jax.ShapeDtypeStruct((2, n * rows, wide), bf16),
            jax.ShapeDtypeStruct((2, n * rows, ch), bf16),
        ),
        grid_spec=pltpu.PrefetchScalarGridSpec(
            num_scalar_prefetch=1,
            grid=(2 * per_end,),
            in_specs=[
                picked(mine), picked(other), whole(down), striped(weight), striped(up), whole(small),
                *((whole(earlier[0]), gate_spot(first * rows)) if earlier else ()),
            ],
            out_specs=[
                pl.BlockSpec((2, n * rows, wide), lambda b, w: (0, 0, 0)),
                gate_spot(n * rows),
            ],
            scratch_shapes=[pltpu.VMEM((count * rows, full), bf16)],
        ),
        cost_estimate=pl.CostEstimate(
            flops=4 * count * rows * full * (ch + wide),
            bytes_accessed=2 * weight.size + 4 * n * rows * (ch + wide),
            transcendentals=0,
        ),
        name="project",
    )(where, mine, other, down, weight, up, small, *earlier)


def merge_kernel(where, gate_a, gate_b, came_a, came_b, gated, go_a, go_b, *, passing):
    ch = gated.shape[1]
    go_a[:, :ch] = (gate_a[0].astype(f32) + came_b[:, :ch].astype(f32)).astype(bf16)
    go_b[:, :ch] = (gate_b[0].astype(f32) + came_a[:, :ch].astype(f32)).astype(bf16)
    own = gated[...]
    if passing:
        own = jnp.where(where[0] == 1, own.astype(f32), came_b[:, ch:].astype(f32)).astype(bf16)
        go_b[:, ch:] = came_a[:, ch:]
    else:
        go_b[:, ch:] = own
    go_a[:, ch:] = own


def merge(where, gates, came, gated):
    ch = gated.shape[1]
    passing = came[0].shape[1] > ch
    whole = lambda a: pl.BlockSpec(a.shape, lambda b, w: (0,) * a.ndim)
    out = jax.ShapeDtypeStruct((BLOCK, 2 * ch), bf16)
    return pl.pallas_call(
        functools.partial(merge_kernel, passing=passing),
        out_shape=(out, out),
        grid_spec=pltpu.PrefetchScalarGridSpec(
            num_scalar_prefetch=1,
            grid=(1,),
            in_specs=[
                pl.BlockSpec((1, BLOCK, ch), lambda b, w: (0, w[1], 0)),
                pl.BlockSpec((1, BLOCK, ch), lambda b, w: (1, w[2], 0)),
                whole(came[0]), whole(came[1]), whole(gated),
            ],
            out_specs=[whole(out), whole(out)],
        ),
        cost_estimate=pl.CostEstimate(
            flops=4 * BLOCK * ch, bytes_accessed=22 * BLOCK * ch, transcendentals=0
        ),
        name="merge",
    )(where, gates, gates, *came, gated)


def scan_kernel(
    gates, sums, tail, state, index, table, rate, taps,
    gated_out, state_out, tail_out, rows, cum_rows, step_rows,
):
    ch = state.shape[1]
    wide = ch + 2 * STATE
    rows[0:8, :] = tail[...]
    rows[8 : 8 + BLOCK, :] = sums[:, :wide].astype(f32)
    tail_out[...] = rows[BLOCK : BLOCK + 8, :]

    def conv(at):
        total = jnp.zeros((BLOCK, LANES), f32)
        for k in range(CONV):
            begin = 8 - (CONV - 1) + k
            total = total + taps[k : k + 1, at] * rows[begin : begin + BLOCK, at]
        return silu(total).astype(bf16)

    input_vec = conv(pl.ds(ch, STATE))
    output_vec = conv(pl.ds(ch + STATE, STATE))
    row = lax.broadcasted_iota(jnp.int32, (BLOCK, BLOCK), 0)
    col = lax.broadcasted_iota(jnp.int32, (BLOCK, BLOCK), 1)
    causal = row >= col
    chosen = (row == index[...].astype(jnp.int32)).astype(f32).T
    shift = jnp.dot(
        chosen, table[...], precision=lax.Precision.HIGHEST, preferred_element_type=f32
    )
    raw = sums[:, wide:].astype(f32) + shift
    step = jnp.maximum(raw, 0.0) + jnp.log1p(jnp.exp(-jnp.abs(raw)))
    cum = jnp.dot(
        causal.astype(f32),
        -rate[...] * step,
        precision=lax.Precision.HIGHEST,
        preferred_element_type=f32,
    )
    cum_rows[...] = cum.T
    step_rows[...] = step.T
    scores = lax.dot_general(
        output_vec, input_vec, (((1,), (1,)), ((), ())), preferred_element_type=f32
    )
    scores = jnp.where(causal, scores, 0.0)
    first_half = col < HEAD_DIM
    input_t = input_vec.T

    def two_heads(pair, carry):
        lanes = pl.ds(pl.multiple_of(pair * LANES, LANES), LANES)
        x = conv(lanes)
        held = state[:, lanes]
        high = held.astype(bf16)
        low = (held - high.astype(f32)).astype(bf16)
        inter = jnp.dot(output_vec, high, preferred_element_type=f32) + jnp.dot(
            output_vec, low, preferred_element_type=f32
        )
        turned = LANES - 2 * pair
        cum_here = pltpu.roll(cum, turned, 1)
        step_here = pltpu.roll(step, turned, 1)
        cums, steps, outs = [], [], []
        for h in range(2):
            row_of = pl.ds(2 * pair + h, 1)
            cum_i = jnp.broadcast_to(cum_here[:, h : h + 1], (BLOCK, BLOCK))
            weight = jnp.exp(jnp.minimum(cum_i - cum_rows[row_of, :], 0.0))
            mixing = (scores * weight * step_rows[row_of, :]).astype(bf16)
            outs.append(jnp.dot(mixing, x, preferred_element_type=f32))
            cums.append(cum_i)
            steps.append(jnp.broadcast_to(step_here[:, h : h + 1], (BLOCK, BLOCK)))
        cum_i = jnp.where(first_half, cums[0], cums[1])
        total = cum_i[BLOCK - 1 :, :]
        out = jnp.where(first_half, outs[0], outs[1]) + jnp.exp(cum_i) * inter
        gated_out[:, lanes] = (out * silu(gates[:, lanes].astype(f32))).astype(bf16)
        factor = jnp.where(first_half, steps[0], steps[1]) * jnp.exp(total - cum_i)
        scaled = (x.astype(f32) * factor).astype(bf16)
        state_out[:, lanes] = jnp.exp(total) * held + jnp.dot(
            input_t, scaled, preferred_element_type=f32
        )
        return carry

    lax.fori_loop(0, ch // LANES, two_heads, 0, unroll=2)


def scan_block(gates, sums, tail, state, index, table, rate, taps):
    ch = state.shape[1]
    wide = ch + 2 * STATE
    whole = lambda a: pl.BlockSpec(a.shape, lambda b: (0,) * a.ndim)
    others = (sums, tail, state, index, table, rate, taps)
    outs = (
        jax.ShapeDtypeStruct((BLOCK, ch), bf16),
        jax.ShapeDtypeStruct((STATE, ch), f32),
        jax.ShapeDtypeStruct((8, wide), f32),
    )
    return pl.pallas_call(
        scan_kernel,
        out_shape=outs,
        grid=(1,),
        in_specs=[pl.BlockSpec((BLOCK, ch), lambda b: (0, 0)), *map(whole, others)],
        out_specs=[whole(o) for o in outs],
        scratch_shapes=[
            pltpu.VMEM((BLOCK + 8, wide), f32),
            pltpu.VMEM((LANES, BLOCK), f32),
            pltpu.VMEM((LANES, BLOCK), f32),
        ],
        cost_estimate=pl.CostEstimate(
            flops=8 * BLOCK * BLOCK * ch,
            bytes_accessed=16 * BLOCK * ch,
            transcendentals=2 * BLOCK * BLOCK * ch // HEAD_DIM,
        ),
        name="scan_block",
    )(gates, *others)


def output_kernel(where, *refs, n, count, paired):
    blocks = refs[: 2 * n * count]
    gain, weight_source, *refs = refs[2 * n * count :]
    prior, (out, *handed), (held, weight, sems, weight_sems) = (
        (refs[0], refs[1:3], refs[3:]) if paired else (None, refs[:1], refs[1:])
    )
    ch = held.shape[1] // 2
    width = weight.shape[1]
    here = where[0]

    def fetch(act):
        for block in range(count):
            for side in range(2):
                place = here if side == 0 else n - 1 - here
                for k in range(n):
                    source = blocks[(block * 2 + side) * n + k]
                    start = source.shape[1] - ch

                    @pl.when(place == k)
                    def _():
                        act(
                            pltpu.make_async_copy(
                                source.at[:, start:],
                                held.at[pl.ds(block * BLOCK, BLOCK), pl.ds(side * ch, ch)],
                                sems.at[block, side],
                            )
                        )

    fetch(lambda copy: copy.start())
    tile = min(256, width)
    tiles = width // tile
    for k in range(tiles):
        columns = pl.ds(k * tile, tile)
        pltpu.make_async_copy(
            weight_source.at[:, columns], weight.at[:, columns], weight_sems.at[k]
        ).start()
    fetch(lambda copy: copy.wait())

    def put(part, columns, result):
        if paired:
            mine = where[1] == 0
            before = prior[part, columns].astype(f32)
            out[part, columns] = jnp.where(mine, before, result).astype(bf16)
            handed[0][part, columns] = jnp.where(mine, result, before).astype(bf16)
        else:
            out[part, columns] = result.astype(bf16)

    def some_rows(at, carry):
        part = pl.ds(pl.multiple_of(at * BLOCK, BLOCK), BLOCK)
        values = held[part, :].astype(f32)
        squares = jnp.sum(values * values, axis=1, keepdims=True)
        held[part, :] = (values * gain[...]).astype(bf16)
        put(part, slice(width, width + LANES), jnp.broadcast_to(squares, (BLOCK, LANES)))
        return carry

    lax.fori_loop(0, count, some_rows, 0)

    def some_columns(at, carry):
        part = pl.ds(pl.multiple_of(at * tile, tile), tile)
        pltpu.make_async_copy(
            weight_source.at[:, part], weight.at[:, part], weight_sems.at[at]
        ).wait()
        put(slice(None), part, jnp.dot(held[...], weight[:, part], preferred_element_type=f32))
        return carry

    lax.fori_loop(0, tiles, some_columns, 0)


def output_block(where, blocks, n, gain, weight, ch, prior=None):
    count = len(blocks) // (2 * n)
    width = weight.shape[1]
    whole = lambda a: pl.BlockSpec(a.shape, lambda b, w: (0, 0))
    result = jax.ShapeDtypeStruct((count * BLOCK, width + LANES), bf16)
    extra = () if prior is None else (prior,)
    return pl.pallas_call(
        functools.partial(output_kernel, n=n, count=count, paired=prior is not None),
        out_shape=result if prior is None else (result, result),
        grid_spec=pltpu.PrefetchScalarGridSpec(
            num_scalar_prefetch=1,
            grid=(1,),
            in_specs=[
                *(pl.BlockSpec(memory_space=pl.ANY) for _ in blocks),
                whole(gain),
                pl.BlockSpec(memory_space=pl.ANY),
                *map(whole, extra),
            ],
            out_specs=whole(result) if prior is None else [whole(result)] * 2,
            scratch_shapes=[
                pltpu.VMEM((count * BLOCK, 2 * ch), bf16),
                pltpu.VMEM(weight.shape, bf16),
                pltpu.SemaphoreType.DMA((count, 2)),
                pltpu.SemaphoreType.DMA((max(1, width // 256),)),
            ],
        ),
        cost_estimate=pl.CostEstimate(
            flops=4 * count * BLOCK * ch * width, bytes_accessed=4 * ch * width + 8 * count * BLOCK * ch, transcendentals=0
        ),
        name="output_block",
    )(where, *blocks, gain, weight, *extra)


def per_device(
    activations,
    token_adapter_index,
    gate_scanned_weight,
    state_vector_weight,
    time_step_weight,
    adapter_down_maps,
    adapter_up_maps,
    scanned_channel_taps,
    state_vector_taps,
    earlier_scanned_channels,
    earlier_state_vectors,
    head_step_bias,
    adapter_step_shift,
    head_decay_rate,
    starting_head_state,
    gated_norm_gain,
    output_projection_weight,
):
    n = lax.axis_size("seq")
    here = lax.axis_index("seq")
    shards = lax.axis_size("tensor")
    shard = lax.axis_index("tensor")
    core = shard % 2
    rows = activations.shape[0]
    tokens = rows * n
    depth = gate_scanned_weight.shape[0]
    heads_here = time_step_weight.shape[1]
    heads = heads_here // 2
    ch = heads * HEAD_DIM
    per_set = HEADS // HEAD_SETS
    size = tokens // shards
    assert per_set % heads == 0 and n % 2 == 0 and shards % 2 == 0 and size % BLOCK == 0
    blocks = tokens // BLOCK
    pairs_a = [(j, j ^ 1) for j in range(n)]
    pairs_b = [(j, ((j - 1) ^ 1) + 1) for j in range(1, n - 1)]
    swap = [(j, j ^ 1) for j in range(shards)]
    at_first = here == 0
    at_end = at_first | (here == n - 1)
    odd = here % 2
    as_int = lambda v: v.astype(jnp.int32)

    def own(array, start, count, axis):
        return lax.dynamic_slice_in_dim(array, start, count, axis)

    half = depth // 2
    index_rows = 16 * -(-rows // (16 * half))
    index_pad = jnp.pad(
        token_adapter_index.astype(bf16), (0, index_rows * half - rows)
    ).reshape(index_rows, half)

    def piece(dest):
        part = lax.dynamic_slice(activations, (0, dest * depth + core * half), (rows, half))
        return jnp.concatenate([part, index_pad], axis=0)

    pieces = [piece(here)]
    for k in range(1, n):
        pairs = [(j, (j + k) % n) for j in range(n)]
        pieces.append(lax.ppermute(piece((here + k) % n), "seq", pairs))

    def by_pair(array):
        split = array.reshape(array.shape[0] // 16, 16, 2, array.shape[2])
        return jnp.swapaxes(split, 1, 2)

    weight = by_pair(gate_scanned_weight)
    up = by_pair(adapter_up_maps)

    def small_of(end):
        first = (shard * heads_here + end * heads) // per_set * STATE
        io = own(state_vector_weight, first, STATE, 2).reshape(depth, 2 * STATE)
        steps = time_step_weight[:, end * heads : (end + 1) * heads]
        return jnp.concatenate([io, jnp.pad(steps, ((0, 0), (0, LANES - heads)))], axis=1)

    small = jnp.stack([small_of(0), small_of(1)])
    mine, weight, up, small = lax.optimization_barrier((jnp.stack(pieces), weight, up, small))
    other = lax.ppermute(mine, "tensor", swap)
    index = mine[:, rows:].reshape(n, -1)[:, :rows]
    index = jnp.concatenate(
        [lax.dynamic_index_in_dim(index, (here - b) % n, 0, False) for b in range(n)]
    ).astype(f32).reshape(blocks, 1, BLOCK)

    order = [as_int(core), as_int(1 - odd)] + [as_int((here - b) % n) for b in range(n)]
    order = jnp.stack(order)
    projected = ()
    versions = []
    for count in (n,):
        projected = project(
            order, mine, other, adapter_down_maps, weight, up, small, rows, ch, count, projected
        )
        versions.append(projected)

    end = jnp.where(at_first, 0, 1)
    first_head = end * heads
    first_ch = end * ch
    first_io = (shard * heads_here + first_head) // per_set * STATE
    taps = jnp.concatenate(
        [
            own(scanned_channel_taps, first_ch, ch, 1),
            own(state_vector_taps, first_io, STATE, 2).reshape(CONV, 2 * STATE),
        ],
        axis=1,
    )
    tail = jnp.concatenate(
        [
            own(earlier_scanned_channels, first_ch, ch, 1),
            own(earlier_state_vectors, first_io, STATE, 2).reshape(CONV - 1, 2 * STATE),
        ],
        axis=1,
    ).astype(f32)
    tail = jnp.pad(tail, ((8 - (CONV - 1), 0), (0, 0)))
    table = own(adapter_step_shift + head_step_bias, first_head, heads, 1)
    table = jnp.pad(table, ((0, LANES - ADAPTER_COUNT), (0, LANES - heads)))
    rate = jnp.pad(own(head_decay_rate, first_head, heads, 0), (0, LANES - heads))[None]
    state = own(starting_head_state, first_head, heads, 0).reshape(ch, STATE).T
    gain = gated_norm_gain[None]

    def made(step):
        return versions[min(step * BLOCK // rows, len(versions) - 1)]

    def turn(step):
        limit = made(step)[0].shape[1] // BLOCK
        to_last = jnp.clip(step - here, 0, limit - 1)
        to_first = jnp.clip(step - (n - 1 - here), 0, limit - 1)
        return jnp.where(odd == 0, to_last, to_first), jnp.where(odd == 0, to_first, to_last)

    def taken(array, step):
        shape = (1, BLOCK, array.shape[2])
        return tuple(
            lax.dynamic_slice(array, (side, at * BLOCK, 0), shape)[0]
            for side, at in enumerate(turn(step))
        )

    def added(a, b):
        return (a.astype(f32) + b.astype(f32)).astype(bf16)

    def onward(pair):
        from_a = lax.ppermute(pair[0], "seq", pairs_a)
        from_b = lax.ppermute(pair[1], "seq", pairs_b)
        return from_a, from_b

    def tied(*pairs):
        flat = lax.optimization_barrier(tuple(a for pair in pairs for a in pair))
        return [tuple(flat[k : k + 2]) for k in range(0, len(flat), 2)]

    sends = blocks + n - 2
    last_step = blocks + 2 * n - 3
    per = size // BLOCK
    chips = shards // 2
    chip = shard // 2
    spot = jnp.stack([as_int(here), as_int(core)])
    groups = [2, 1, 1] if chips == 2 else [1] * shards
    group_ends = [sum(groups[: k + 1]) for k in range(len(groups))]
    sums = came = before = gated = None
    went, arrived, states, outs = {}, {}, [], []
    pending = None
    for step in range(last_step + 1):
        block = step - (n - 1)
        if step <= sends:
            go = taken(made(step)[0], step)
            if step > 1:
                sums, before = tied(sums, before)
            if step > 0:
                go = added(go[0], sums[1]), added(go[1], sums[0])
                came, sums = tied(came, sums)
            before = came
            if step < sends:
                sums = onward(go)
        else:
            (came,) = tied(came)
        if step < n:
            gate = taken(made(step)[1], step)
            if step > 0:
                gate = added(gate[0], came[1]), added(gate[1], came[0])
            onto = gate
            if step == n - 1 and sends > step:
                onto = gate
        if n <= step < sends:
            where = jnp.stack([as_int(at_end), *map(as_int, turn(step))])
            onto = gate = merge(where, made(step)[1], came, gated)
        elif step == sends:
            gate = (None, added(taken(made(step)[1], step)[1], came[0][:, :ch]))
        if step >= max(n, sends):
            onto = came[1][:, -ch:], came[0][:, -ch:]
            if gated is not None:
                onto = jnp.where(at_end, gated, onto[0]), onto[1]
        came = onward(onto)
        arrived[step] = came
        if block >= 0:
            if gated is not None:
                went[block - 1] = onto[0]
            gated = None
        if 0 <= block < blocks:
            gated, state, tail = scan_block(
                gate[1], go[1], tail, state, index[block], table, rate, taps
            )
            if pending is not None and block + 1 < blocks:
                state, outs[pending] = lax.optimization_barrier((state, outs[pending]))
                pending = None
            if (block + 1) * BLOCK % rows == 0:
                states.append(state.astype(bf16).T)
        if pending is not None and sends < step < last_step:
            came, (outs[pending], _) = tied(came, (outs[pending], state))
            pending = None
        done = step - (2 * n - 2)
        if done >= 0 and (done + 1) % per == 0 and (done + 1) // per in group_ends:
            needed = []
            for b in range(done + 1 - per * groups[len(outs)], done + 1):
                for _ in range(2):
                    needed.append(went[b])
                    needed.extend(arrived[b + n - 1 + k][1 - k % 2] for k in range(1, n))
            pending = len(outs)
            prior = outs[-1] if chips == 2 and pending == len(groups) - 1 else None
            outs.append(
                output_block(
                    spot, needed, n, gain, output_projection_weight, ch, prior
                )
            )

    landed = [jnp.where(at_first, states[0], states[n - 1])]
    for k in range(1, n):
        leaving = jnp.where(at_first, states[k], states[n - 1 - k])
        landed.append(lax.ppermute(leaving, "seq", [(0, k), (n - 1, n - 1 - k)]))

    if chips == 2:
        first, _, (keep_last, give_last) = outs
        keep = own(first, core * size, size, 0)
        give = own(first, (1 - core) * size, size, 0)
        back = lax.ppermute(give, "tensor", swap)
        both_first = added(keep, back)
        back = lax.ppermute(give_last, "tensor", swap)
        both_last = added(keep_last, back)
        total = jnp.where(chip == 0, both_first, both_last).astype(f32)
        both = give = jnp.where(chip == 0, both_last, both_first)
        came = lax.ppermute(give, "tensor", [(j, j ^ 2) for j in range(shards)])
        total = total + came.astype(f32)
    else:
        halves = []
        for k in range(chips):
            keep = jnp.where(core == 0, outs[2 * k], outs[2 * k + 1])
            give = jnp.where(core == 0, outs[2 * k + 1], outs[2 * k])
            halves.append(added(keep, lax.ppermute(give, "tensor", swap)))
        both = halves[-1]
        halves = jnp.stack(halves)
        total = lax.dynamic_index_in_dim(halves, chip, 0, False).astype(f32)
        for k in range(1, chips):
            pairs = [(j, (j + 2 * k) % shards) for j in range(shards)]
            give = lax.dynamic_index_in_dim(halves, (chip + k) % chips, 0, False)
            total = total + lax.ppermute(give, "tensor", pairs).astype(f32)
    *landed, _ = lax.optimization_barrier((*landed, both))
    landed = jnp.stack(landed)
    finish = jnp.concatenate(
        [lax.dynamic_index_in_dim(landed, which, 0, False) for which in (here, n - 1 - here)], axis=0
    ).astype(f32).reshape(heads_here, HEAD_DIM, STATE)
    width = output_projection_weight.shape[1]
    scale = lax.rsqrt(total[:, width : width + 1] / (HEADS * HEAD_DIM) + 1e-05)
    mixed = (total[:, :width] * scale).astype(bf16)
    return (mixed, finish[None])


def solution(mesh):
    return jax.shard_map(
        per_device,
        mesh=mesh,
        in_specs=(
            P(("groups", "seq"), None),
            P(("groups", "seq")),
            P("seq", None, "tensor"),
            P("seq", None, None),
            P("seq", "tensor"),
            P("seq", None),
            P(None, None, "tensor"),
            P(None, "tensor"),
            P(),
            P("groups", "tensor"),
            P("groups", None, None),
            P("tensor"),
            P(None, "tensor"),
            P("tensor"),
            P(("groups", "tensor"), None, None),
            P("tensor"),
            P("tensor", "seq"),
        ),
        out_specs=(P(("groups", "tensor"), "seq"), P(("groups", "seq"), "tensor", None, None)),
        check_vma=False,
    )
```
